32 devices in a mesh: gx: 4 (over y, core), gy: 8 (over z, x).
Axes of the slice: x: 2, y: 2, z: 4, core: 2. Of those that a mesh axis runs over, the one named last changes fastest.
Arguments:
- depth: float32 [16, 64, 1024], P(None, 'gx', 'gy'), may hold values from 0.5 to 2
- momentum: float32 [3, 16, 64, 1024], P(None, None, 'gx', 'gy'), may hold values from -2.5 to 2.5
- tracer: float32 [16, 64, 1024], P(None, 'gx', 'gy'), may hold values from -6 to 6
- cell_wet: int32 [64, 1024], P('gx', 'gy'), may hold values 0 or 1
- tile_wet: int32 [1, 8], replicated, may hold values 0 or 1
Outputs:
- new_depth: float32 [16, 64, 1024], P(None, 'gx', 'gy')
- new_momentum: float32 [3, 16, 64, 1024], P(None, None, 'gx', 'gy')
- new_tracer: float32 [16, 64, 1024], P(None, 'gx', 'gy')
The draws below stay inside these ranges and needn't reach their ends.
All inputs are finite; a program needn't handle non-finite values. No bound on the sum of `cell_wet` on one device may be relied on, other than what follows from the above.
Results may differ from the reference program's by a relative error of at most 0.0003.
Values sent between devices are 32-bit elements; how exact they have to be, the bound alone decides.
A program may use at most 64 MiB of HBM per device.

```python
import jax
import jax.numpy as jnp
from jax import lax

L = 16
ITERS = 3
TILE = 128
NX = 64
NY = 1024
NXT = 1
NYT = 8


def touch_ends(drawn, own_key, smallest, largest):
    longest = drawn.shape.index(max(drawn.shape))
    spots = []
    for shift in (0, 1):
        where = [jax.random.randint(jax.random.fold_in(own_key, axis), (), 0, length) for axis, length in enumerate(drawn.shape)]
        where[longest] = (where[longest] + shift) % drawn.shape[longest]
        spots.append(tuple(where))
    return drawn.at[spots[0]].set(smallest).at[spots[1]].set(largest)


def block_scale(rng, dims, cuts, low, high):
    gain, own = 1.0, jax.random.fold_in(rng, 6)
    for position, parts in cuts:
        steps = jnp.exp(jax.random.uniform(jax.random.fold_in(own, position), (parts,), jnp.float32, low / len(cuts), high / len(cuts)))
        gain = gain * jnp.repeat(steps, dims[position] // parts).reshape([-1 if axis == position else 1 for axis in range(len(dims))])
    return gain


def normal_values(key, extent, width, limit, shards=(), dtype=jnp.bfloat16):
    drawn = jax.random.normal(key, extent, jnp.float32) * width
    if len(shards) > 0:
        drawn = block_scale(key, extent, shards, -0.22, 0.18) * drawn
    return jnp.clip(drawn, min=-limit, max=limit).astype(dtype)


def setup_inputs(seed: int = 0) -> dict:
    seeds = jax.random.split(jax.random.key(seed), 6)
    depth = jnp.clip(0.5 + 1.5 * jax.random.uniform(seeds[0], (L, NX, NY), jnp.float32) ** block_scale(seeds[0], (L, NX, NY), ((1, 4), (2, 8)), -0.2, 0.2), 0.5, 2.0)
    momentum = normal_values(seeds[1], (3, L, NX, NY), 0.3, 2.5, ((2, 4), (3, 8)), jnp.float32)
    tracer = normal_values(seeds[2], (L, NX, NY), 1.0, 6.0, ((1, 4), (2, 8)), jnp.float32)
    cell_wet = touch_ends((jax.random.randint(seeds[3], (NX, NY), 0, 10) < 9).astype(jnp.int32), jax.random.fold_in(seeds[3], 1), 0, 1)
    tile_wet = touch_ends((jax.random.randint(seeds[4], (NXT, NYT), 0, 4) < 3).astype(jnp.int32), jax.random.fold_in(seeds[4], 1), 0, 1)
    return dict(depth=depth, momentum=momentum, tracer=tracer, cell_wet=cell_wet, tile_wet=tile_wet)


gravity = 9.81
time_step = 0.025

def minmod(first_slope, second_slope):
    return 0.5 * (jnp.sign(first_slope) + jnp.sign(second_slope)) * jnp.minimum(jnp.abs(first_slope), jnp.abs(second_slope))

def riemann_flux(left_state, right_state, normal):
    unit_shape = (5,) + (1,) * (left_state.ndim - 1)
    normal_unit = (jnp.arange(5) == normal).astype(jnp.float32).reshape(unit_shape)
    depth_left = left_state[0]
    depth_right = right_state[0]
    speed_left = left_state[normal] / depth_left
    speed_right = right_state[normal] / depth_right
    wave_left = jnp.sqrt(gravity * depth_left)
    wave_right = jnp.sqrt(gravity * depth_right)
    flux_left = left_state * speed_left + normal_unit * (0.5 * gravity * depth_left * depth_left)
    flux_right = right_state * speed_right + normal_unit * (0.5 * gravity * depth_right * depth_right)
    lower_speed = jnp.minimum(jnp.minimum(speed_left - wave_left, speed_right - wave_right), 0.0)
    upper_speed = jnp.maximum(jnp.maximum(speed_left + wave_left, speed_right + wave_right), 0.0)
    return (upper_speed * flux_left - lower_speed * flux_right + lower_speed * upper_speed * (right_state - left_state)) / (upper_speed - lower_speed)

def face_flux(fields, wetness, direction, normal):
    face_count = fields.shape[direction] - 3

    def window(values, offset):
        return lax.slice_in_dim(values, offset, offset + face_count, axis=values.ndim + direction)
    behind = window(fields, 0)
    centre = window(fields, 1)
    onward = window(fields, 2)
    beyond = window(fields, 3)
    left_state = centre + 0.5 * minmod(centre - behind, onward - centre)
    right_state = onward - 0.5 * minmod(onward - centre, beyond - onward)
    return riemann_flux(left_state, right_state, normal) * (window(wetness, 1) * window(wetness, 2))

def section_rate(fields, wetness):
    layer_depth = fields[0] * wetness + (1.0 - wetness)
    usable = jnp.concatenate([layer_depth[None], fields[1:]], 0)
    east_flux = face_flux(usable[..., 2:-2], wetness[:, 2:-2], -2, 1)
    north_flux = face_flux(usable[..., 2:-2, :], wetness[2:-2, :], -1, 2)
    return -time_step * (east_flux[..., 1:, :] - east_flux[..., :-1, :] + (north_flux[..., 1:] - north_flux[..., :-1]))

def advance(fields, wetness_wide):

    def widen(values):
        return jnp.pad(values, ((0, 0), (2, 2), (2, 2)))
    section_one = fields + section_rate(widen(fields), wetness_wide)
    section_two = 0.75 * fields + 0.25 * (section_one + section_rate(widen(section_one), wetness_wide))
    return fields / 3.0 + 2.0 / 3.0 * (section_two + section_rate(widen(section_two), wetness_wide))

def coefficients(columns, vertical_momentum, wetness_cycle):
    depth_wide = columns[0]
    inside = wetness_cycle[1:-1, 1:-1]
    layer_depth = depth_wide[:, 1:-1, 1:-1]
    east_west = 0.5 * (depth_wide[:, :-1, 1:-1] + depth_wide[:, 1:, 1:-1]) * (wetness_cycle[:-1, 1:-1] * wetness_cycle[1:, 1:-1])
    north_south = 0.5 * (depth_wide[:, 1:-1, :-1] + depth_wide[:, 1:-1, 1:]) * (wetness_cycle[1:-1, :-1] * wetness_cycle[1:-1, 1:])
    between = 2.0 * inside / (layer_depth[:-1] + layer_depth[1:])
    surface = 2.0 * inside / layer_depth[-1:]
    nothing = jnp.zeros_like(surface)
    downward = jnp.concatenate([nothing, between], 0)
    upward = jnp.concatenate([between, surface], 0)
    diagonal = 0.5 * layer_depth + east_west[:, :-1] + east_west[:, 1:] + north_south[:, :, :-1] + north_south[:, :, 1:] + downward + upward
    lower_momentum = jnp.concatenate([jnp.zeros_like(vertical_momentum[:1]), vertical_momentum[:-1]], 0)
    divergence = 0.5 * (columns[1][:, 2:, 1:-1] - columns[1][:, :-2, 1:-1]) + 0.5 * (columns[2][:, 1:-1, 2:] - columns[2][:, 1:-1, :-2]) + (vertical_momentum - lower_momentum)
    forcing = -divergence * inside
    return (east_west, north_south, downward, upward, diagonal, forcing)

def apply_operator(pressure_wide, system):
    east_west, north_south, downward, upward, diagonal, forcing = system
    centre = pressure_wide[:, 1:-1, 1:-1]
    nothing = jnp.zeros_like(centre[:1])
    neighbour = east_west[:, :-1] * pressure_wide[:, :-2, 1:-1] + east_west[:, 1:] * pressure_wide[:, 2:, 1:-1]
    neighbour = neighbour + north_south[:, :, :-1] * pressure_wide[:, 1:-1, :-2] + north_south[:, :, 1:] * pressure_wide[:, 1:-1, 2:]
    vertical = downward * jnp.concatenate([nothing, centre[:-1]], 0) + upward * jnp.concatenate([centre[1:], nothing], 0)
    return diagonal * centre - neighbour - vertical

def correct(pressure_wide, system, momentum):
    east_west, north_south, downward, upward, diagonal, forcing = system
    centre = pressure_wide[:, 1:-1, 1:-1]
    nothing = jnp.zeros_like(centre[:1])
    push_east = 0.5 * (east_west[:, 1:] * (pressure_wide[:, 2:, 1:-1] - centre) + east_west[:, :-1] * (centre - pressure_wide[:, :-2, 1:-1]))
    push_north = 0.5 * (north_south[:, :, 1:] * (pressure_wide[:, 1:-1, 2:] - centre) + north_south[:, :, :-1] * (centre - pressure_wide[:, 1:-1, :-2]))
    push_upward = upward * (jnp.concatenate([centre[1:], nothing], 0) - centre)
    return momentum - jnp.stack([push_east, push_north, push_upward])

def reference(depth, momentum, tracer, cell_wet, tile_wet):
    tiles = jnp.repeat(jnp.repeat(tile_wet, TILE, axis=0), TILE, axis=1)[:NX, :NY]
    wetness = (cell_wet * tiles).astype(jnp.float32)
    wetness_wide = jnp.pad(wetness, 2)
    fields = jnp.concatenate([depth[None], momentum, tracer[None]], 0)
    layered = lax.map(lambda layer_fields: advance(layer_fields, wetness_wide), jnp.moveaxis(fields, 1, 0))
    result = jnp.moveaxis(layered, 0, 1)
    columns = jnp.pad(result[:3], ((0, 0), (0, 0), (1, 1), (1, 1)))
    system = coefficients(columns, result[3], wetness_wide[1:-1, 1:-1])
    diagonal = system[4]
    forcing = system[5]
    pressure = jnp.zeros_like(forcing)
    residual = forcing
    scaled = residual / diagonal
    direction = scaled
    energy = jnp.sum(residual * scaled)
    for sweep in range(ITERS):
        applied = apply_operator(jnp.pad(direction, ((0, 0), (1, 1), (1, 1))), system)
        step_size = energy / jnp.sum(direction * applied)
        pressure = pressure + step_size * direction
        residual = residual - step_size * applied
        if sweep + 1 < ITERS:
            scaled = residual / diagonal
            fresh = jnp.sum(residual * scaled)
            direction = scaled + fresh / energy * direction
            energy = fresh
    pressure_wide = jnp.pad(pressure, ((0, 0), (1, 1), (1, 1)))
    new_momentum = correct(pressure_wide, system, result[1:4])
    return (result[0], new_momentum, result[4])
```

```python
import functools

import jax
import jax.numpy as jnp
from jax import lax
from jax.experimental import pallas as pl
from jax.experimental.pallas import tpu as pltpu
from jax.sharding import PartitionSpec as P

ITERS = 3
TILE = 128
REACH = 2 * 3 + 1 + ITERS
SEG = 11

gravity = 9.81
time_step = 0.025
MESH = pl.DeviceIdType.MESH


def minmod(a, b):
    return jnp.maximum(jnp.minimum(a, b), 0.0) + jnp.minimum(jnp.maximum(a, b), 0.0)


def hll(left, right, weight, normal):
    hl, hr = left[0], right[0]
    rl, rr = lax.rsqrt(hl), lax.rsqrt(hr)
    ul, ur = left[normal] * (rl * rl), right[normal] * (rr * rr)
    al, ar = gravity**0.5 * (hl * rl), gravity**0.5 * (hr * rr)
    lower = jnp.minimum(jnp.minimum(ul - al, ur - ar), 0.0)
    upper = jnp.maximum(jnp.maximum(ul + al, ur + ar), 0.0)
    scale = weight / (upper - lower)
    low, high = lower * scale, upper * scale
    take_left = high * (ul - lower)
    take_right = low * (upper - ur)
    flux = [take_left * l + take_right * r for l, r in zip(left, right)]
    flux[normal] = flux[normal] + (0.5 * gravity) * (high * hl * hl - low * hr * hr)
    return flux


def lane_next(x):
    return pltpu.roll(x, x.shape[-1] - 1, 1)


def lane_prev(x):
    return pltpu.roll(x, 1, 1)


def kernel(
    nx, ny, rows, cols, layers,
    tile_hbm, depth_hbm, mom_hbm, tracer_hbm, wet_hbm,
    depth_out, mom_out, tracer_out,
    staged, wet_ref, tile_ref, load_sem, pushes,
    fa, fb, fc, wet, pack_l, pack_r, halo_l, halo_r,
    ce, cn, up, inv, z0, z1, z2, part, gather_x, gather_y,
    send_row, recv_row, send_wet, recv_wet, send_col, recv_col,
    send_cor, recv_cor, send_gx, recv_gx, send_gy, recv_gy,
):
    R = REACH
    high_rows = rows + 2 * R
    width = 2 * cols
    half = layers // 2
    gx, gy = lax.axis_index("gx"), lax.axis_index("gy")

    loads = [
        pltpu.make_async_copy(wet_hbm, wet_ref, load_sem.at[0]),
        pltpu.make_async_copy(depth_hbm, staged.at[0], load_sem.at[1]),
        pltpu.make_async_copy(mom_hbm, staged.at[pl.ds(1, 3)], load_sem.at[2]),
        pltpu.make_async_copy(tracer_hbm, staged.at[4], load_sem.at[3]),
        pltpu.make_async_copy(tile_hbm, tile_ref, load_sem.at[4]),
    ]
    for load in loads:
        load.start()

    wet[...] = jnp.zeros_like(wet)
    halo_l[...] = jnp.zeros_like(halo_l)
    halo_r[...] = jnp.zeros_like(halo_r)

    barrier = pltpu.get_barrier_semaphore()
    has = {-1: gx > 0, 1: gx < nx - 1}
    side = {-1: gy > 0, 1: gy < ny - 1}
    for o in range(1, nx):
        pl.semaphore_signal(barrier, inc=1, device_id=(lax.rem(gx + o, nx), gy), device_id_type=MESH)
    for o in range(1, ny):
        pl.semaphore_signal(barrier, inc=1, device_id=(gx, lax.rem(gy + o, ny)), device_id_type=MESH)
    for dx in (-1, 1):
        for dy in (-1, 1):
            @pl.when(jnp.logical_and(has[dx], side[dy]))
            def _(dx=dx, dy=dy):
                pl.semaphore_signal(barrier, inc=1, device_id=(gx + dx, gy + dy), device_id_type=MESH)

    for dx, start in ((-1, 0), (1, R + rows)):
        @pl.when(jnp.logical_not(has[dx]))
        def _(start=start):
            fa[:, start : start + R, :, :cols] = jnp.zeros((5, R, layers, cols), jnp.float32)

    for load in loads:
        load.wait()
    tile = tile_ref[(gx * rows) // TILE, (gy * cols) // TILE].astype(jnp.float32)
    for r in range(rows):
        wet[R + r, :, :cols] = wet_ref[r : r + 1, :].astype(jnp.float32) * tile

    def load_row(r, carry):
        at = pl.ds(r, layers, stride=rows)
        for f in range(5):
            fa[f, R + r, :, :cols] = staged[f, at, :]
        return carry

    lax.fori_loop(0, rows, load_row, 0, unroll=4)

    as_int = lambda flag: flag.astype(jnp.int32)
    corners = (as_int(has[-1]) + as_int(has[1])) * (as_int(side[-1]) + as_int(side[1]))
    pl.semaphore_wait(barrier, nx - 1 + ny - 1 + corners)

    copies = []
    mine = {-1: R, 1: rows}
    theirs = {-1: R + rows, 1: 0}
    pack = {-1: pack_l, 1: pack_r}
    halo = {-1: halo_r, 1: halo_l}
    for i, dx in enumerate((-1, 1)):
        for src, send, recv in ((fa, send_row, recv_row), (wet, send_wet, recv_wet)):
            if src is fa:
                a = fa.at[:, pl.ds(mine[dx], R), :, pl.ds(0, cols)]
                b = fa.at[:, pl.ds(theirs[dx], R), :, pl.ds(0, cols)]
            else:
                a = wet.at[pl.ds(mine[dx], R), :, pl.ds(0, cols)]
                b = wet.at[pl.ds(theirs[dx], R), :, pl.ds(0, cols)]
            send_to = pltpu.make_async_remote_copy(
                src_ref=a, dst_ref=b, send_sem=send.at[i], recv_sem=recv.at[i],
                device_id=(gx + dx, gy), device_id_type=MESH)
            come = pltpu.make_async_remote_copy(
                src_ref=a, dst_ref=b, send_sem=send.at[i], recv_sem=recv.at[1 - i],
                device_id=(gx + dx, gy), device_id_type=MESH)
            copies.append((has[dx], send_to, come))
    for j, dy in enumerate((-1, 1)):
        args = dict(src_ref=pack[dy], dst_ref=halo[dy].at[pl.ds(R, rows)], send_sem=send_col.at[j],
                    device_id=(gx, gy + dy), device_id_type=MESH)
        copies.append((side[dy],
                       pltpu.make_async_remote_copy(recv_sem=recv_col.at[j], **args),
                       pltpu.make_async_remote_copy(recv_sem=recv_col.at[1 - j], **args)))
        for i, dx in enumerate((-1, 1)):
            args = dict(src_ref=pack[dy].at[pl.ds(mine[dx] - R, R)],
                        dst_ref=halo[dy].at[pl.ds(theirs[dx], R)],
                        send_sem=send_cor.at[i, j],
                        device_id=(gx + dx, gy + dy), device_id_type=MESH)
            copies.append((jnp.logical_and(has[dx], side[dy]),
                           pltpu.make_async_remote_copy(recv_sem=recv_cor.at[i, j], **args),
                           pltpu.make_async_remote_copy(recv_sem=recv_cor.at[1 - i, 1 - j], **args)))
    def begin(group):
        for cond, go, come in group:
            @pl.when(cond)
            def _(go=go):
                go.start()

    def finish(group):
        for cond, go, come in group:
            @pl.when(cond)
            def _(go=go, come=come):
                go.wait_send()
                come.wait_recv()

    tall_copies, edge_copies, corner_copies = copies[:4], [copies[4], copies[7]], copies[5:7] + copies[8:]
    begin(tall_copies)

    lane = lax.broadcasted_iota(jnp.int32, (half, cols), 1)

    def pack_row(r, carry):
        left = jnp.zeros((half, cols), jnp.float32)
        right = left
        for s in range(11):
            if s < 10:
                x = fa[s % 5, R + r, (s // 5) * half : (s // 5 + 1) * half, :cols]
            else:
                x = jnp.broadcast_to(wet[R + r, :, :cols], (half, cols))
            mask = jnp.logical_and(lane >= SEG * s, lane < SEG * s + R)
            left = jnp.where(mask, pltpu.roll(x, SEG * s, 1) if s else x, left)
            right = jnp.where(mask, pltpu.roll(x, (SEG * s + R) % cols, 1), right)
        pack_l[r] = left
        pack_r[r] = right
        return carry

    lax.fori_loop(0, rows, pack_row, 0, unroll=4)

    begin(edge_copies)
    begin(corner_copies)
    finish(edge_copies)

    def unpack_row(r, carry):
        fr, fl = halo_r[r], halo_l[r]
        for s in range(11):
            a = pltpu.roll(fr, cols - SEG * s, 1) if s else fr
            b = pltpu.roll(fl, cols - R - SEG * s if SEG * s + R < cols else 2 * cols - R - SEG * s, 1)
            x = jnp.where(lane < R, a, jnp.where(lane >= cols - R, b, 0.0))
            if s < 10:
                fa[s % 5, r, (s // 5) * half : (s // 5 + 1) * half, cols:] = x
            else:
                wet[r, :, cols:] = x[:1]
        return carry

    lax.fori_loop(R, R + rows, unpack_row, 0, unroll=4)

    def transport(src, dst, lo, hi, keep, unroll=6):
        for part_of in range(2):
            cut = slice(part_of * half, (part_of + 1) * half)

            def usable(r):
                w = wet[r]
                u = [src[f, r, cut, :] for f in range(5)]
                u[0] = u[0] * w + (1.0 - w)
                return u

            def sides(u, before, after):
                s = [0.5 * minmod(b, a) for b, a in zip(before, after)]
                return [x - y for x, y in zip(u, s)], [x + y for x, y in zip(u, s)]

            def row_face(i, left):
                here, mid, far = usable(i), usable(i + 1), usable(i + 2)
                right, following = sides(
                    mid, [m - h for m, h in zip(mid, here)], [f - m for f, m in zip(far, mid)])
                return hll(left, right, wet[i] * wet[i + 1], 1), following

            def step(i, carry):
                flux_low, left = carry
                flux_high, following = row_face(i, left)
                u = usable(i)
                d = [lane_next(x) - x for x in u]
                right, left_c = sides(u, [lane_prev(x) for x in d], d)
                w = wet[i]
                across = hll(left_c, [lane_next(x) for x in right], w * lane_next(jnp.broadcast_to(w, (half, width))), 2)
                for f in range(5):
                    rate = -time_step * (flux_high[f] - flux_low[f] + (across[f] - lane_prev(across[f])))
                    old = src[f, i, cut, :]
                    if keep is None:
                        new = old + rate
                    elif keep == 0.75:
                        new = 0.75 * fa[f, i, cut, :] + 0.25 * (old + rate)
                    else:
                        new = fa[f, i, cut, :] * (1.0 / 3.0) + (2.0 / 3.0) * (old + rate)
                    dst[f, i, cut, :] = new
                return flux_high, following

            a, b, c = usable(lo - 2), usable(lo - 1), usable(lo)
            _, left = sides(b, [y - x for x, y in zip(a, b)], [y - x for x, y in zip(b, c)])
            flux, left = row_face(lo - 1, left)
            lax.fori_loop(lo, hi, step, (flux, left), unroll=unroll)

    transport(fa, fb, R + 2, R + rows - 2, None)
    finish(tall_copies)
    finish(corner_copies)
    lax.fori_loop(0, R, unpack_row, 0, unroll=5)
    lax.fori_loop(R + rows, high_rows, unpack_row, 0, unroll=5)
    transport(fa, fb, 2, R + 2, None, 5)
    transport(fa, fb, R + rows - 2, high_rows - 2, None, 5)
    transport(fb, fc, 4, high_rows - 4, 0.75)
    transport(fc, fb, 6, high_rows - 6, 1.0 / 3.0)

    layer_id = lax.broadcasted_iota(jnp.int32, (layers, width), 0)
    top = layer_id == layers - 1

    def above(x):
        return pltpu.roll(x, layers - 1, 0)

    def below(x):
        return pltpu.roll(x, 1, 0)

    def prepare(r, low):
        h, w = fb[0, r], wet[r]
        high = 0.5 * (h + fb[0, r + 1]) * (w * wet[r + 1])
        across = 0.5 * (h + lane_next(h)) * (w * lane_next(jnp.broadcast_to(w, (layers, width))))
        total = jnp.where(top, h, h + above(h))
        upward = jnp.where(jnp.broadcast_to(w, total.shape) > 0.0, 2.0 / total, 0.0)
        inner = jnp.where(top, 0.0, upward)
        diagonal = 0.5 * h + low + high + lane_prev(across) + across + below(inner) + upward
        v = fb[3, r]
        y = fb[2, r]
        div = (
            0.5 * (fb[1, r + 1] - fb[1, r - 1])
            + 0.5 * (lane_next(y) - lane_prev(y))
            + (v - jnp.where(layer_id == 0, 0.0, below(v)))
        )
        force = -div * w
        inverse = jnp.where(diagonal == 0.0, 0.0, 1.0 / diagonal)
        ce[r] = high
        cn[r] = across
        up[r] = upward
        inv[r] = inverse
        z = force * inverse
        z0[r] = z
        return high, force, z

    def fold(x):
        return x[:half, :cols] + x[half:, :cols]

    first = REACH - ITERS
    ce[first - 1] = 0.5 * (fb[0, first - 1] + fb[0, first]) * (wet[first - 1] * wet[first])

    def prep_outer(r, low):
        return prepare(r, low)[0]

    def prep_inner(r, carry):
        low, acc = carry
        high, force, z = prepare(r, low)
        return high, acc + fold(force * z)

    zero = jnp.zeros((half, cols), jnp.float32)
    low = lax.fori_loop(first, R, prep_outer, ce[first - 1], unroll=True)
    low, m0 = lax.fori_loop(R, R + rows, prep_inner, (low, zero), unroll=4)
    lax.fori_loop(R + rows, R + rows + ITERS, prep_outer, low, unroll=True)

    def spread(z, r):
        x = z[r]
        c = cn[r]
        u = jnp.where(top, 0.0, up[r])
        return (
            ce[r - 1] * z[r - 1] + ce[r] * z[r + 1]
            + c * lane_next(x) + lane_prev(c * x)
            + u * above(x) + below(u * x)
        )

    def advance(z, target, reach):
        def outer(r, carry):
            target[r] = spread(z, r) * inv[r]
            return carry

        def inner(r, carry):
            odd, even = carry
            n = spread(z, r)
            y = n * inv[r]
            target[r] = y
            return odd + fold(z[r] * n), even + fold(y * n)

        lax.fori_loop(R - reach, R, outer, 0, unroll=True)
        sums = lax.fori_loop(R, R + rows, inner, (zero, zero), unroll=4)
        lax.fori_loop(R + rows, R + rows + reach, outer, 0, unroll=True)
        return sums

    m1, m2 = advance(z0, z1, 2)
    m3, m4 = advance(z1, z2, 1)
    m5 = lax.fori_loop(R, R + rows, lambda r, acc: acc + fold(z2[r] * spread(z2, r)), zero, unroll=4)

    part[0] = jnp.zeros((8, cols), jnp.float32)
    for k, m in enumerate((m0, m1, m2, m3, m4, m5)):
        part[0, k : k + 1, :] = jnp.sum(m, axis=0, keepdims=True)

    def push_of(k, z):
        def row(r, carry):
            q, c = z[r], cn[r]
            east = 0.5 * (ce[r] * (z[r + 1] - q) + ce[r - 1] * (q - z[r - 1]))
            slope = c * (lane_next(q) - q)
            north = 0.5 * (slope + lane_prev(slope))
            upward = up[r] * (jnp.where(top, 0.0, above(q)) - q)
            for n, push in enumerate((east, north, upward)):
                pushes[k, n, r - R] = push[:, :cols]
            return carry

        lax.fori_loop(R, R + rows, row, 0, unroll=4)

    def everyone(count, slot, gather, send, recv, place):
        moves = [
            pltpu.make_async_remote_copy(
                src_ref=part.at[slot], dst_ref=gather.at[o - 1], send_sem=send.at[o - 1],
                recv_sem=recv.at[o - 1], device_id=place(o), device_id_type=MESH)
            for o in range(1, count)
        ]
        for move in moves:
            move.start()
        return moves

    def plain_out(r, carry):
        at = pl.ds(r - R, layers, stride=rows)
        depth_out[at, :] = fb[0, r, :, :cols]
        tracer_out[at, :] = fb[4, r, :, :cols]
        return carry

    moves = everyone(nx, 0, gather_x, send_gx, recv_gx, lambda o: (lax.rem(gx + o, nx), gy))
    push_of(0, z0)
    push_of(1, z1)
    for move in moves:
        move.wait()
    total = part[0]
    for o in range(nx - 1):
        total = total + gather_x[o]
    part[1] = total
    moves = everyone(ny, 1, gather_y, send_gy, recv_gy, lambda o: (gx, lax.rem(gy + o, ny)))
    push_of(2, z2)
    lax.fori_loop(R, R + rows, plain_out, 0, unroll=4)
    for move in moves:
        move.wait()
    for o in range(ny - 1):
        total = total + gather_y[o]
    sums = jnp.broadcast_to(jnp.sum(total, axis=1, keepdims=True), (8, cols))
    m = [sums[k : k + 1, :] for k in range(6)]

    def dots(a, b, table):
        out = None
        for i in range(3):
            for j in range(3):
                if a[i] is not None and b[j] is not None:
                    t = a[i] * b[j] * table[i + j]
                    out = t if out is None else out + t
        return out

    shifted = [m[k] - m[k + 1] for k in range(5)]

    def plus(a, b, f):
        out = []
        for x, y in zip(a, b):
            out.append(x if y is None else (f * y if x is None else x + f * y))
        return out

    def image(d):
        moved = [None, d[0], d[1]]
        return [x if y is None else (None if x is None and y is None else (-y if x is None else x - y)) for x, y in zip(d, moved)]

    one = jnp.ones_like(m[0])
    direction = [one, None, None]
    residual = [one, None, None]
    pressure = [None, None, None]
    energy = m[0]
    for sweep in range(ITERS):
        bottom = dots(direction, direction, shifted)
        size = energy / bottom
        pressure = plus(pressure, direction, size)
        if sweep + 1 < ITERS:
            residual = plus(residual, image(direction), -size)
            fresh = dots(residual, residual, m)
            direction = plus(residual, direction, fresh / energy)
            energy = fresh

    def correct(r, carry):
        at = pl.ds(r - R, layers, stride=rows)
        for n in range(3):
            push = pressure[0] * pushes[0, n, r - R]
            push = push + pressure[1] * pushes[1, n, r - R] + pressure[2] * pushes[2, n, r - R]
            mom_out[n, at, :] = fb[1 + n, r, :, :cols] - push
        return carry

    lax.fori_loop(R, R + rows, correct, 0, unroll=4)


def body(nx, ny, depth, momentum, tracer, cell_wet, tile_wet):
    layers, rows, cols = depth.shape
    assert TILE % rows == 0 and TILE % cols == 0 and cols == 128 and rows >= REACH
    f32 = jnp.float32
    tall = rows + 2 * REACH
    wide = 2 * cols
    half = layers // 2
    dma = pltpu.SemaphoreType.DMA
    vmem = pl.BlockSpec(memory_space=pltpu.VMEM)
    flat = jax.ShapeDtypeStruct((layers * rows, cols), f32)
    field = pltpu.VMEM((5, tall, layers, wide), f32)
    layer = pltpu.VMEM((tall, layers, wide), f32)
    packed = pltpu.VMEM((rows, half, cols), f32)
    halo = pltpu.VMEM((tall, half, cols), f32)
    pairs = [dma((2,))] * 6 + [dma((2, 2))] * 2 + [dma((nx - 1,))] * 2 + [dma((ny - 1,))] * 2
    new_depth, new_momentum, new_tracer = pl.pallas_call(
        functools.partial(kernel, nx, ny, rows, cols, layers),
        out_shape=(pltpu.VMEM((layers * rows, cols), f32), pltpu.VMEM((3, layers * rows, cols), f32), pltpu.VMEM((layers * rows, cols), f32)),
        in_specs=[pl.BlockSpec(memory_space=pltpu.HBM)] * 5,
        out_specs=(vmem, vmem, vmem),
        scratch_shapes=[
            pltpu.VMEM((5, layers * rows, cols), f32),
            pltpu.VMEM((rows, cols), jnp.int32),
            pltpu.SMEM(tile_wet.shape, jnp.int32),
            dma((5,)),
            pltpu.VMEM((3, 3, rows, layers, cols), f32),
            field, field, field,
            pltpu.VMEM((tall, 1, wide), f32),
            packed, packed, halo, halo,
            layer, layer, layer, layer, layer, layer, layer,
            pltpu.VMEM((2, 8, cols), f32),
            pltpu.VMEM((nx - 1, 8, cols), f32),
            pltpu.VMEM((ny - 1, 8, cols), f32),
            *pairs,
        ],
        compiler_params=pltpu.CompilerParams(
            collective_id=0, has_side_effects=True, vmem_limit_bytes=56 * 1024 * 1024
        ),
    )(
        tile_wet,
        depth.reshape(layers * rows, cols),
        momentum.reshape(3, layers * rows, cols),
        tracer.reshape(layers * rows, cols),
        cell_wet,
    )
    new_depth, new_momentum, new_tracer = pl.pallas_call(
        hand_on,
        out_shape=(flat, jax.ShapeDtypeStruct((3, layers * rows, cols), f32), flat),
        in_specs=[pl.BlockSpec(memory_space=pl.ANY)] * 3,
        out_specs=(pl.BlockSpec(memory_space=pl.ANY),) * 3,
        scratch_shapes=[dma((3,))],
        compiler_params=pltpu.CompilerParams(vmem_limit_bytes=8 * 1024 * 1024),
    )(new_depth, new_momentum, new_tracer)
    return (
        new_depth.reshape(depth.shape),
        new_momentum.reshape(momentum.shape),
        new_tracer.reshape(tracer.shape),
    )


def hand_on(a, b, c, x, y, z, sem):
    moves = [pltpu.make_async_copy(s, d, sem.at[k]) for k, (s, d) in enumerate(((a, x), (b, y), (c, z)))]
    for m in moves:
        m.start()
    for m in moves:
        m.wait()


def solution(mesh):
    placed = (
        P(None, "gx", "gy"),
        P(None, None, "gx", "gy"),
        P(None, "gx", "gy"),
        P("gx", "gy"),
        P(),
    )
    return jax.shard_map(
        functools.partial(body, mesh.shape["gx"], mesh.shape["gy"]),
        mesh=mesh,
        in_specs=placed,
        out_specs=(P(None, "gx", "gy"), P(None, None, "gx", "gy"), P(None, "gx", "gy")),
        check_vma=False,
    )
```

```python
import functools

import jax
import jax.numpy as jnp
from jax import lax
from jax.experimental import pallas as pl
from jax.experimental.pallas import tpu as pltpu
from jax.sharding import PartitionSpec as P

ITERS = 3
TILE = 128
REACH = 2
DEEP = 1 + ITERS
SEG = 2 * DEEP
FIELDS = 5

gravity = 9.81
time_step = 0.025
root = gravity**0.5
MESH = pl.DeviceIdType.MESH


def minmod(a, b):
    return jnp.maximum(jnp.minimum(a, jnp.maximum(b, 0.0)), jnp.minimum(b, 0.0))


def hll(left, right, weight, normal):
    hl, hr = left[0], right[0]
    rl, rr = lax.rsqrt(hl), lax.rsqrt(hr)
    ul, ur = left[normal] * (rl * rl), right[normal] * (rr * rr)
    al, ar = hl * rl, hr * rr
    lower = jnp.minimum(jnp.minimum(ul - al, ur - ar), 0.0)
    upper = jnp.maximum(jnp.maximum(ul + al, ur + ar), 0.0)
    scale = weight / (upper - lower)
    low, high = lower * scale, upper * scale
    take_left = high * (ul - lower)
    take_right = low * (upper - ur)
    flux = [take_left * l + take_right * r for l, r in zip(left, right)]
    flux[normal] = flux[normal] + 0.5 * (high * hl * hl - low * hr * hr)
    return flux


def lane_next(x):
    return pltpu.roll(x, x.shape[-1] - 1, 1)


def lane_prev(x):
    return pltpu.roll(x, 1, 1)


def halves(u):
    return [0.5 * x for x in u]


def minus(a, b):
    return [x - y for x, y in zip(a, b)]


def sides(u, before, after):
    s = [minmod(b, a) for b, a in zip(before, after)]
    return minus(u, s), [x + y for x, y in zip(u, s)]


def across_flux(u, v, weight):
    d = [lane_next(x) - x for x in v]
    right, left = sides(u, [lane_prev(x) for x in d], d)
    return hll(left, [lane_next(x) for x in right], weight, 2)


def kernel(
    nx, ny, rows, cols, layers,
    tile_hbm, depth_hbm, mom_hbm, tracer_hbm, wet_hbm,
    depth_out, mom_out, tracer_out,
    staged, wet_ref, tile_ref, load_sem, pushes,
    fa, fb, fc, res, wet, wet_rows, wet_cols, wet_edge, packed, from_l, from_r, from_c, wet_c, change,
    ce, cn, up, inv, z0, z1, z2, part, gather_x, gather_y,
    send_row, recv_row, send_wet, recv_wet, send_col, recv_col,
    send_wc, recv_wc, send_cor, recv_cor, send_gx, recv_gx, send_gy, recv_gy,
):
    R = DEEP
    H = REACH
    width = 2 * cols
    half = layers // 2
    flows = 2 * FIELDS
    gx, gy = lax.axis_index("gx"), lax.axis_index("gy")

    loads = [
        pltpu.make_async_copy(wet_hbm, wet_ref, load_sem.at[0]),
        pltpu.make_async_copy(tile_hbm, tile_ref, load_sem.at[4]),
        pltpu.make_async_copy(depth_hbm, staged.at[0], load_sem.at[1]),
        pltpu.make_async_copy(mom_hbm, staged.at[pl.ds(1, 3)], load_sem.at[2]),
        pltpu.make_async_copy(tracer_hbm, staged.at[4], load_sem.at[3]),
    ]
    for load in loads:
        load.start()

    barrier = pltpu.get_barrier_semaphore()
    has = {-1: gx > 0, 1: gx < nx - 1}
    side = {-1: gy > 0, 1: gy < ny - 1}
    for o in range(1, nx):
        pl.semaphore_signal(barrier, inc=1, device_id=(lax.rem(gx + o, nx), gy), device_id_type=MESH)
    for o in range(1, ny):
        pl.semaphore_signal(barrier, inc=1, device_id=(gx, lax.rem(gy + o, ny)), device_id_type=MESH)
    for dx in (-1, 1):
        for dy in (-1, 1):
            @pl.when(jnp.logical_and(has[dx], side[dy]))
            def _(dx=dx, dy=dy):
                pl.semaphore_signal(barrier, inc=1, device_id=(gx + dx, gy + dy), device_id_type=MESH)

    f32 = jnp.float32
    for dx in (-1, 1):
        @pl.when(jnp.logical_not(has[dx]))
        def _(dx=dx):
            at = slice(0, H) if dx < 0 else slice(H + rows, rows + 2 * H)
            for x in (fa, fb, fc):
                x[0, at] = jnp.ones((H, layers, cols), f32)
                x[1:, at] = jnp.zeros((FIELDS - 1, H, layers, cols), f32)
            at = slice(0, R) if dx < 0 else slice(R + rows, rows + 2 * R)
            res[0, at, :, :cols] = jnp.ones((R, layers, cols), f32)
            res[1:4, at, :, :cols] = jnp.zeros((3, R, layers, cols), f32)
            wet[at, :, :cols] = jnp.zeros((R, 1, cols), f32)
    for dy, landing in ((-1, from_l), (1, from_r)):
        @pl.when(jnp.logical_not(side[dy]))
        def _(landing=landing):
            landing[:, :2] = jnp.ones((4, 2, half, cols), f32)
            landing[:, 2:] = jnp.zeros((4, flows - 1, half, cols), f32)
    for i, dx in enumerate((-1, 1)):
        for j, dy in enumerate((-1, 1)):
            @pl.when(jnp.logical_not(jnp.logical_and(has[dx], side[dy])))
            def _(i=i, j=j):
                from_c[i, j, :2] = jnp.ones((2, half, cols), f32)
                from_c[i, j, 2:] = jnp.zeros((6, half, cols), f32)
                wet_c[i, j] = jnp.zeros((half, cols), f32)

    as_int = lambda flag: flag.astype(jnp.int32)
    corners = (as_int(has[-1]) + as_int(has[1])) * (as_int(side[-1]) + as_int(side[1]))

    def exchange(cond, src, dst, send, recv, back, device):
        args = dict(src_ref=src, dst_ref=dst, send_sem=send, device_id=device, device_id_type=MESH)
        return (cond, pltpu.make_async_remote_copy(recv_sem=recv, **args),
                pltpu.make_async_remote_copy(recv_sem=back, **args))

    started = []

    def begin(group):
        for cond, go, come in group:
            @pl.when(cond)
            def _(go=go):
                go.start()
        started.extend(group)

    def arrive(group):
        for cond, go, come in group:
            @pl.when(cond)
            def _(come=come):
                come.wait_recv()

    def row_copies(k, x, deep, part_of):
        group = []
        for i, dx in enumerate((-1, 1)):
            mine = deep if dx < 0 else rows
            theirs = deep + rows if dx < 0 else 0
            group.append(exchange(
                has[dx], part_of(x, mine), part_of(x, theirs),
                send_row.at[k, i], recv_row.at[k, i], recv_row.at[k, 1 - i], (gx + dx, gy)))
        return group

    def stage_rows(x, at):
        return x.at[:, pl.ds(at, H)]

    def result_rows(x, at):
        return x.at[pl.ds(0, 4), pl.ds(at, R), :, pl.ds(0, cols)]

    def column_copies(k, count):
        group = []
        for j, (dy, landing) in enumerate(((-1, from_r), (1, from_l))):
            group.append(exchange(
                side[dy], packed.at[k, pl.ds(0, count)], landing.at[k, pl.ds(0, count)],
                send_col.at[k, j], recv_col.at[k, j], recv_col.at[k, 1 - j], (gx, gy + dy)))
        return group

    def corner_copies(src, landing, send, recv):
        group = []
        for i, dx in enumerate((-1, 1)):
            for j, dy in enumerate((-1, 1)):
                group.append(exchange(
                    jnp.logical_and(has[dx], side[dy]), src, landing.at[1 - i, 1 - j],
                    send.at[i, j], recv.at[i, j], recv.at[1 - i, 1 - j], (gx + dx, gy + dy)))
        return group

    lane = lax.broadcasted_iota(jnp.int32, (half, cols), 1)
    seg = lane // SEG
    pos = lane % SEG
    own_right = pos < DEEP
    edge = jnp.logical_or(lane < H, lane >= cols - H)
    cuts = [slice(q * half, (q + 1) * half) for q in range(2)]

    def into(x, r, total):
        return jnp.where(seg == r, pltpu.roll(x, SEG * r + DEEP, 1), total)

    def out_of(x, r):
        return pltpu.roll(x, cols - DEEP - SEG * r, 1)

    for load in loads:
        load.wait()
    tile = tile_ref[(gx * rows) // TILE, (gy * cols) // TILE].astype(f32)
    for r in range(rows):
        wet[R + r, :, :cols] = wet_ref[r : r + 1, :].astype(f32) * tile

    def load_row(r, carry):
        at = pl.ds(r, layers, stride=rows)
        w = wet[R + r, :, :cols]
        carry = list(carry)
        for f in range(FIELDS):
            x = staged[f, at, :]
            if f == 0:
                x = x * w + (1.0 - w)
            elif f < 3:
                x = x * (1.0 / root)
            fa[f, H + r] = x
            for q in range(2):
                carry[2 * f + q] = into(x[cuts[q]], r, carry[2 * f + q])
        carry[flows] = into(jnp.broadcast_to(w, (half, cols)), r, carry[flows])
        return tuple(carry)

    blank = jnp.zeros((half, cols), f32)
    carry = (blank,) * (flows + 1)
    for lo, hi in ((0, H), (rows - H, rows)):
        carry = lax.fori_loop(lo, hi, load_row, carry, unroll=True)
    pl.semaphore_wait(barrier, nx - 1 + ny - 1 + corners)
    coming_rows = row_copies(0, fa, H, stage_rows)
    begin(coming_rows)
    wet_copies = []
    for i, dx in enumerate((-1, 1)):
        mine, theirs = (R, R + rows) if dx < 0 else (rows, 0)
        wet_copies.append(exchange(
            has[dx], wet.at[pl.ds(mine, R), :, pl.ds(0, cols)], wet.at[pl.ds(theirs, R), :, pl.ds(0, cols)],
            send_wet.at[i], recv_wet.at[i], recv_wet.at[1 - i], (gx + dx, gy)))
    begin(wet_copies)
    carry = lax.fori_loop(H, rows - H, load_row, carry, unroll=4)
    for n in range(flows + 1):
        packed[0, n] = carry[n]
    coming_cols = column_copies(0, flows + 1)
    begin(coming_cols)
    wet_corners = corner_copies(packed.at[0, flows], wet_c, send_wc, recv_wc)
    begin(wet_corners)

    inner = jnp.logical_and(lane >= 1, lane < cols - H)

    def column_weight(r, carry):
        w = jnp.broadcast_to(wet[R + r, :, :cols], (half, cols))
        wet_cols[r] = jnp.where(inner, (-time_step * root) * w * lane_next(w), 0.0)
        return carry

    def row_weight(r, carry):
        w = wet[R + r - 1, :, :cols] * wet[R + r, :, :cols]
        wet_rows[r] = jnp.broadcast_to((-time_step * root) * w, (half, cols))
        return carry

    lax.fori_loop(0, rows, column_weight, 0, unroll=4)
    lax.fori_loop(1, rows, row_weight, 0, unroll=5)

    def sweep(src, dst, deep, lo, hi, keep, unroll):
        for q in range(2):
            cut = cuts[q]

            def state(i):
                return [src[f, i + H, cut, :] for f in range(FIELDS)]

            def step(i, carry):
                flux_low, left, v0, v1, d = carry
                v2 = halves(state(i + 2))
                ahead = minus(v2, v1)
                right, following = sides(state(i + 1), d, ahead)
                flux_high = hll(left, right, wet_rows[i + 1], 1)
                u = state(i)
                across = across_flux(u, v0, wet_cols[i])
                for f in range(FIELDS):
                    rate = flux_high[f] - flux_low[f] + (across[f] - lane_prev(across[f]))
                    if keep is None:
                        new = u[f] + rate
                    elif keep == 0.75:
                        new = 0.75 * fa[f, i + H, cut, :] + 0.25 * (u[f] + rate)
                    else:
                        new = fa[f, i + H, cut, :] * (1.0 / 3.0) + (2.0 / 3.0) * (u[f] + rate)
                    dst[f, i + deep, cut, :cols] = new
                return flux_high, following, v1, v2, ahead

            a, b, c, e = [state(lo + o) for o in (-2, -1, 0, 1)]
            va, vb, vc, ve = [halves(x) for x in (a, b, c, e)]
            dab, dbc, dce = minus(vb, va), minus(vc, vb), minus(ve, vc)
            _, left = sides(b, dab, dbc)
            right, following = sides(c, dbc, dce)
            flux = hll(left, right, wet_rows[lo], 1)
            lax.fori_loop(lo, hi, step, (flux, following, vc, ve, dce), unroll=unroll)

    def edges(k, factor):
        for q in range(2):
            own = [packed[k, 2 * f + q] for f in range(FIELDS)]
            left = [jnp.where(own_right, from_l[k, 2 * f + q], own[f]) for f in range(FIELDS)]
            right = [jnp.where(own_right, own[f], from_r[k, 2 * f + q]) for f in range(FIELDS)]
            flux_l = across_flux(left, halves(left), wet_edge[0])
            flux_r = across_flux(right, halves(right), wet_edge[1])
            for f in range(FIELDS):
                a, b = flux_r[f] - lane_prev(flux_r[f]), flux_l[f] - lane_prev(flux_l[f])
                t = jnp.where(own_right, a, b)
                change[2 * f + q] = t if factor == 1.0 else factor * t

    def settle(dst, deep, last):
        def row(r, carry):
            carry = list(carry)
            for f in range(FIELDS):
                for q in range(2):
                    x = dst[f, r + deep, cuts[q], :cols]
                    x = x + jnp.where(edge, out_of(change[2 * f + q], r), 0.0)
                    if last and f in (1, 2):
                        x = x * root
                    dst[f, r + deep, cuts[q], :cols] = x
                    if not (last and f == 4):
                        carry[2 * f + q] = into(x, r, carry[2 * f + q])
            return tuple(carry)
        return row

    plan = ((fa, fb, H, None, 1.0), (fb, fc, H, 0.75, 0.25), (fc, res, R, 1.0 / 3.0, 2.0 / 3.0))
    for k, (src, dst, deep, keep, factor) in enumerate(plan):
        last = k == 2
        sweep(src, dst, deep, H, rows - H, keep, 6)
        if k == 0:
            arrive(wet_copies)
            for r in (0, rows):
                row_weight(r, 0)
        arrive(coming_rows)
        sweep(src, dst, deep, 0, H, keep, True)
        sweep(src, dst, deep, rows - H, rows, keep, True)
        arrive(coming_cols)
        if k == 0:
            own = packed[0, flows]
            for n, (w, first) in enumerate((
                    (jnp.where(own_right, from_l[0, flows], own), DEEP - 1),
                    (jnp.where(own_right, own, from_r[0, flows]), DEEP - 2))):
                used = jnp.logical_or(pos == first, pos == first + 1)
                wet_edge[n] = jnp.where(used, (-time_step * root) * w * lane_next(w), 0.0)
        edges(k, factor)
        row = settle(dst, deep, last)
        count = flows - 2 if last else flows
        carry = (blank,) * count
        for lo, hi in ((0, deep), (rows - deep, rows)):
            carry = lax.fori_loop(lo, hi, row, carry, unroll=True)
        coming_rows = row_copies(k + 1, dst, deep, result_rows if last else stage_rows)
        begin(coming_rows)
        carry = lax.fori_loop(deep, rows - deep, row, carry, unroll=4)
        for n in range(count):
            packed[k + 1, n] = carry[n]
        coming_cols = column_copies(k + 1, count)
        begin(coming_cols)
    coming_corners = corner_copies(packed.at[3, pl.ds(0, 8)], from_c, send_cor, recv_cor)
    begin(coming_corners)

    def unpack(left, right, wet_l, wet_r, base, shift):
        both = [jnp.where(own_right, left(n), right(n)) for n in range(8)]
        w = jnp.where(own_right, wet_l, wet_r)

        def row(r, carry):
            for f in range(4):
                for q in range(2):
                    res[f, r + base, cuts[q], cols:] = out_of(both[2 * f + q], r)
            wet[r + base, :, cols:] = out_of(w, r)[:1]
            return carry

        return row

    arrive(coming_cols)
    row = unpack(lambda n: from_l[3, n], lambda n: from_r[3, n], from_l[0, flows], from_r[0, flows], R, 0)
    lax.fori_loop(0, rows, row, 0, unroll=4)
    arrive(wet_corners)
    arrive(coming_corners)
    for i, (lo, base) in enumerate(((rows - R, R - rows), (0, R + rows))):
        row = unpack(lambda n: from_c[i, 0, n], lambda n: from_c[i, 1, n], wet_c[i, 0], wet_c[i, 1], base, 0)
        lax.fori_loop(lo, lo + R, row, 0, unroll=True)
    arrive(coming_rows)

    layer_id = lax.broadcasted_iota(jnp.int32, (layers, width), 0)
    top = layer_id == layers - 1

    def above(x):
        return pltpu.roll(x, layers - 1, 0)

    def below(x):
        return pltpu.roll(x, 1, 0)

    def prepare(r, low):
        h, w = res[0, r], wet[r]
        high = 0.5 * (h + res[0, r + 1]) * (w * wet[r + 1])
        across = 0.5 * (h + lane_next(h)) * (w * lane_next(jnp.broadcast_to(w, (layers, width))))
        total = jnp.where(top, h, h + above(h))
        upward = jnp.where(jnp.broadcast_to(w, total.shape) > 0.0, 2.0 / total, 0.0)
        inner = jnp.where(top, 0.0, upward)
        diagonal = 0.5 * h + low + high + lane_prev(across) + across + below(inner) + upward
        v = res[3, r]
        y = res[2, r]
        div = (
            0.5 * (res[1, r + 1] - res[1, r - 1])
            + 0.5 * (lane_next(y) - lane_prev(y))
            + (v - jnp.where(layer_id == 0, 0.0, below(v)))
        )
        force = -div * w
        inverse = jnp.where(diagonal == 0.0, 0.0, 1.0 / diagonal)
        ce[r] = high
        cn[r] = across
        up[r] = upward
        inv[r] = inverse
        z = force * inverse
        z0[r] = z
        return high, force, z

    def fold(x):
        return x[:half, :cols] + x[half:, :cols]

    first = R - ITERS
    ce[first - 1] = 0.5 * (res[0, first - 1] + res[0, first]) * (wet[first - 1] * wet[first])

    def prep_outer(r, low):
        return prepare(r, low)[0]

    def prep_inner(r, carry):
        low, acc = carry
        high, force, z = prepare(r, low)
        return high, acc + fold(force * z)

    zero = jnp.zeros((half, cols), jnp.float32)
    low = lax.fori_loop(first, R, prep_outer, ce[first - 1], unroll=True)
    low, m0 = lax.fori_loop(R, R + rows, prep_inner, (low, zero), unroll=4)
    lax.fori_loop(R + rows, R + rows + ITERS, prep_outer, low, unroll=True)

    def spread(z, r):
        x = z[r]
        c = cn[r]
        u = jnp.where(top, 0.0, up[r])
        return (
            ce[r - 1] * z[r - 1] + ce[r] * z[r + 1]
            + c * lane_next(x) + lane_prev(c * x)
            + u * above(x) + below(u * x)
        )

    def advance(z, target, reach):
        def outer(r, carry):
            target[r] = spread(z, r) * inv[r]
            return carry

        def inner(r, carry):
            odd, even = carry
            n = spread(z, r)
            y = n * inv[r]
            target[r] = y
            return odd + fold(z[r] * n), even + fold(y * n)

        lax.fori_loop(R - reach, R, outer, 0, unroll=True)
        sums = lax.fori_loop(R, R + rows, inner, (zero, zero), unroll=4)
        lax.fori_loop(R + rows, R + rows + reach, outer, 0, unroll=True)
        return sums

    m1, m2 = advance(z0, z1, 2)
    m3, m4 = advance(z1, z2, 1)
    m5 = lax.fori_loop(R, R + rows, lambda r, acc: acc + fold(z2[r] * spread(z2, r)), zero, unroll=4)

    part[0] = jnp.zeros((8, cols), jnp.float32)
    for k, m in enumerate((m0, m1, m2, m3, m4, m5)):
        part[0, k : k + 1, :] = jnp.sum(m, axis=0, keepdims=True)

    def push_of(k, z):
        def row(r, carry):
            q, c = z[r], cn[r]
            east = 0.5 * (ce[r] * (z[r + 1] - q) + ce[r - 1] * (q - z[r - 1]))
            slope = c * (lane_next(q) - q)
            north = 0.5 * (slope + lane_prev(slope))
            upward = up[r] * (jnp.where(top, 0.0, above(q)) - q)
            for n, push in enumerate((east, north, upward)):
                pushes[k, n, r - R] = push[:, :cols]
            return carry

        lax.fori_loop(R, R + rows, row, 0, unroll=4)

    def everyone(count, slot, gather, send, recv, place):
        moves = [
            pltpu.make_async_remote_copy(
                src_ref=part.at[slot], dst_ref=gather.at[o - 1], send_sem=send.at[o - 1],
                recv_sem=recv.at[o - 1], device_id=place(o), device_id_type=MESH)
            for o in range(1, count)
        ]
        for move in moves:
            move.start()
        return moves

    def plain_out(r, carry):
        at = pl.ds(r - R, layers, stride=rows)
        depth_out[at, :] = jnp.where(jnp.broadcast_to(wet[r, :, :cols], (layers, cols)) > 0.0, res[0, r, :, :cols], staged[0, at, :])
        tracer_out[at, :] = res[4, r, :, :cols]
        return carry

    moves = everyone(nx, 0, gather_x, send_gx, recv_gx, lambda o: (lax.rem(gx + o, nx), gy))
    push_of(0, z0)
    push_of(1, z1)
    for move in moves:
        move.wait()
    total = part[0]
    for o in range(nx - 1):
        total = total + gather_x[o]
    part[1] = total
    moves = everyone(ny, 1, gather_y, send_gy, recv_gy, lambda o: (gx, lax.rem(gy + o, ny)))
    push_of(2, z2)
    lax.fori_loop(R, R + rows, plain_out, 0, unroll=4)
    for move in moves:
        move.wait()
    for o in range(ny - 1):
        total = total + gather_y[o]
    sums = jnp.broadcast_to(jnp.sum(total, axis=1, keepdims=True), (8, cols))
    m = [sums[k : k + 1, :] for k in range(6)]

    def dots(a, b, table):
        out = None
        for i in range(3):
            for j in range(3):
                if a[i] is not None and b[j] is not None:
                    t = a[i] * b[j] * table[i + j]
                    out = t if out is None else out + t
        return out

    shifted = [m[k] - m[k + 1] for k in range(5)]

    def plus(a, b, f):
        out = []
        for x, y in zip(a, b):
            out.append(x if y is None else (f * y if x is None else x + f * y))
        return out

    def image(d):
        moved = [None, d[0], d[1]]
        return [x if y is None else (None if x is None and y is None else (-y if x is None else x - y)) for x, y in zip(d, moved)]

    one = jnp.ones_like(m[0])
    direction = [one, None, None]
    residual = [one, None, None]
    pressure = [None, None, None]
    energy = m[0]
    for sweep in range(ITERS):
        bottom = dots(direction, direction, shifted)
        size = energy / bottom
        pressure = plus(pressure, direction, size)
        if sweep + 1 < ITERS:
            residual = plus(residual, image(direction), -size)
            fresh = dots(residual, residual, m)
            direction = plus(residual, direction, fresh / energy)
            energy = fresh

    def correct(r, carry):
        at = pl.ds(r - R, layers, stride=rows)
        for n in range(3):
            push = pressure[0] * pushes[0, n, r - R]
            push = push + pressure[1] * pushes[1, n, r - R] + pressure[2] * pushes[2, n, r - R]
            mom_out[n, at, :] = res[1 + n, r, :, :cols] - push
        return carry

    lax.fori_loop(R, R + rows, correct, 0, unroll=4)
    for cond, go, come in started:
        @pl.when(cond)
        def _(go=go):
            go.wait_send()


def body(nx, ny, depth, momentum, tracer, cell_wet, tile_wet):
    layers, rows, cols = depth.shape
    assert TILE % rows == 0 and TILE % cols == 0 and cols == 128 and rows * SEG == cols and layers == 16
    f32 = jnp.float32
    tall = rows + 2 * DEEP
    wide = 2 * cols
    half = layers // 2
    dma = pltpu.SemaphoreType.DMA
    vmem = pl.BlockSpec(memory_space=pltpu.VMEM)
    flat = jax.ShapeDtypeStruct((layers * rows, cols), f32)
    field = pltpu.VMEM((FIELDS, rows + 2 * REACH, layers, cols), f32)
    layer = pltpu.VMEM((tall, layers, wide), f32)
    flows = 2 * FIELDS
    strip = pltpu.VMEM((4, flows + 1, half, cols), f32)
    pairs = [dma((4, 2))] * 2 + [dma((2,))] * 2 + [dma((4, 2))] * 2 + [dma((2, 2))] * 4
    pairs += [dma((nx - 1,))] * 2 + [dma((ny - 1,))] * 2
    new_depth, new_momentum, new_tracer = pl.pallas_call(
        functools.partial(kernel, nx, ny, rows, cols, layers),
        out_shape=(pltpu.VMEM((layers * rows, cols), f32), pltpu.VMEM((3, layers * rows, cols), f32), pltpu.VMEM((layers * rows, cols), f32)),
        in_specs=[pl.BlockSpec(memory_space=pltpu.HBM)] * 5,
        out_specs=(vmem, vmem, vmem),
        scratch_shapes=[
            pltpu.VMEM((5, layers * rows, cols), f32),
            pltpu.VMEM((rows, cols), jnp.int32),
            pltpu.SMEM(tile_wet.shape, jnp.int32),
            dma((5,)),
            pltpu.VMEM((3, 3, rows, layers, cols), f32),
            field, field, field,
            pltpu.VMEM((FIELDS, tall, layers, wide), f32),
            pltpu.VMEM((tall, 1, wide), f32),
            pltpu.VMEM((rows + 1, half, cols), f32),
            pltpu.VMEM((rows, half, cols), f32),
            pltpu.VMEM((2, half, cols), f32),
            strip, strip, strip,
            pltpu.VMEM((2, 2, 8, half, cols), f32),
            pltpu.VMEM((2, 2, half, cols), f32),
            pltpu.VMEM((flows, half, cols), f32),
            layer, layer, layer, layer, layer, layer, layer,
            pltpu.VMEM((2, 8, cols), f32),
            pltpu.VMEM((nx - 1, 8, cols), f32),
            pltpu.VMEM((ny - 1, 8, cols), f32),
            *pairs,
        ],
        compiler_params=pltpu.CompilerParams(
            collective_id=0, has_side_effects=True, vmem_limit_bytes=56 * 1024 * 1024
        ),
    )(
        tile_wet,
        depth.reshape(layers * rows, cols),
        momentum.reshape(3, layers * rows, cols),
        tracer.reshape(layers * rows, cols),
        cell_wet,
    )
    new_depth, new_momentum, new_tracer = pl.pallas_call(
        hand_on,
        out_shape=(flat, jax.ShapeDtypeStruct((3, layers * rows, cols), f32), flat),
        in_specs=[pl.BlockSpec(memory_space=pl.ANY)] * 3,
        out_specs=(pl.BlockSpec(memory_space=pl.ANY),) * 3,
        scratch_shapes=[dma((3,))],
        compiler_params=pltpu.CompilerParams(vmem_limit_bytes=8 * 1024 * 1024),
    )(new_depth, new_momentum, new_tracer)
    return (
        new_depth.reshape(depth.shape),
        new_momentum.reshape(momentum.shape),
        new_tracer.reshape(tracer.shape),
    )


def hand_on(a, b, c, x, y, z, sem):
    moves = [pltpu.make_async_copy(s, d, sem.at[k]) for k, (s, d) in enumerate(((a, x), (b, y), (c, z)))]
    for m in moves:
        m.start()
    for m in moves:
        m.wait()


def solution(mesh):
    placed = (
        P(None, "gx", "gy"),
        P(None, None, "gx", "gy"),
        P(None, "gx", "gy"),
        P("gx", "gy"),
        P(),
    )
    return jax.shard_map(
        functools.partial(body, mesh.shape["gx"], mesh.shape["gy"]),
        mesh=mesh,
        in_specs=placed,
        out_specs=(P(None, "gx", "gy"), P(None, None, "gx", "gy"), P(None, "gx", "gy")),
        check_vma=False,
    )
```

```python
import functools

import jax
import jax.numpy as jnp
from jax import lax
from jax.experimental import pallas as pl
from jax.experimental.pallas import tpu as pltpu
from jax.sharding import PartitionSpec as P

ITERS = 3
TILE = 128
REACH = 2
DEEP = 1 + ITERS
SEG = 2 * DEEP
FIELDS = 5

gravity = 9.81
time_step = 0.025
root = gravity**0.5
MESH = pl.DeviceIdType.MESH


def minmod(a, b):
    return jnp.maximum(jnp.minimum(a, jnp.maximum(b, 0.0)), jnp.minimum(b, 0.0))


def hll(left, right, weight, normal):
    hl, hr = left[0], right[0]
    rl, rr = lax.rsqrt(hl), lax.rsqrt(hr)
    ul, ur = left[normal] * (rl * rl), right[normal] * (rr * rr)
    al, ar = hl * rl, hr * rr
    lower = jnp.minimum(jnp.minimum(ul - al, ur - ar), 0.0)
    upper = jnp.maximum(jnp.maximum(ul + al, ur + ar), 0.0)
    scale = weight / (upper - lower)
    low, high = lower * scale, upper * scale
    take_left = high * (ul - lower)
    take_right = low * (upper - ur)
    flux = [take_left * l + take_right * r for l, r in zip(left, right)]
    flux[normal] = flux[normal] + 0.5 * (high * hl * hl - low * hr * hr)
    return flux


def lane_next(x):
    return pltpu.roll(x, x.shape[-1] - 1, 1)


def lane_prev(x):
    return pltpu.roll(x, 1, 1)


def halves(u):
    return [0.5 * x for x in u]


def minus(a, b):
    return [x - y for x, y in zip(a, b)]


def sides(u, before, after):
    s = [minmod(b, a) for b, a in zip(before, after)]
    return minus(u, s), [x + y for x, y in zip(u, s)]


def across_flux(u, v, weight):
    d = [lane_next(x) - x for x in v]
    right, left = sides(u, [lane_prev(x) for x in d], d)
    return hll(left, [lane_next(x) for x in right], weight, 2)


def kernel(
    nx, ny, rows, cols, layers,
    tile_hbm, depth_hbm, mom_hbm, tracer_hbm, wet_hbm,
    depth_out, mom_out, tracer_out,
    staged, wet_ref, tile_ref, load_sem, pushes,
    fa, fb, fc, res, wet, wet_rows, wet_cols, wet_edge, packed, from_l, from_r, from_c, wet_c, change,
    ce, cn, up, inv, z0, z1, z2, gather,
    send_row, recv_row, send_wet, recv_wet, send_col, recv_col,
    send_wc, recv_wc, send_cor, recv_cor, send_sum, recv_sum,
):
    R = DEEP
    H = REACH
    width = 2 * cols
    half = layers // 2
    flows = 2 * FIELDS
    gx, gy = lax.axis_index("gx"), lax.axis_index("gy")

    loads = [
        pltpu.make_async_copy(wet_hbm, wet_ref, load_sem.at[0]),
        pltpu.make_async_copy(tile_hbm, tile_ref, load_sem.at[4]),
        pltpu.make_async_copy(depth_hbm, staged.at[0], load_sem.at[1]),
        pltpu.make_async_copy(mom_hbm, staged.at[pl.ds(1, 3)], load_sem.at[2]),
        pltpu.make_async_copy(tracer_hbm, staged.at[4], load_sem.at[3]),
    ]

    barrier = pltpu.get_barrier_semaphore()
    has = {-1: gx > 0, 1: gx < nx - 1}
    side = {-1: gy > 0, 1: gy < ny - 1}
    near = [(a, b) for a in (1, nx - 1, 0) for b in (0, 1, ny - 1) if (a, b) != (0, 0)]
    peers = list(dict.fromkeys(near)) + [
        (a, b) for a in range(nx) for b in range(ny) if (a, b) not in near and (a, b) != (0, 0)]

    def peer(a, b):
        return (lax.rem(gx + a, nx), lax.rem(gy + b, ny))

    for n, (a, b) in enumerate(peers):
        pl.semaphore_signal(barrier, inc=1, device_id=peer(a, b), device_id_type=MESH)
        if n + 1 == len(near):
            for load in loads:
                load.start()

    f32 = jnp.float32
    for dx in (-1, 1):
        @pl.when(jnp.logical_not(has[dx]))
        def _(dx=dx):
            at = slice(0, H) if dx < 0 else slice(H + rows, rows + 2 * H)
            for x in (fa, fb, fc):
                x[0, at] = jnp.ones((H, layers, cols), f32)
                x[1:, at] = jnp.zeros((FIELDS - 1, H, layers, cols), f32)
            at = slice(0, R) if dx < 0 else slice(R + rows, rows + 2 * R)
            res[0, at, :, :cols] = jnp.ones((R, layers, cols), f32)
            res[1:4, at, :, :cols] = jnp.zeros((3, R, layers, cols), f32)
            wet[at, :, :cols] = jnp.zeros((R, 1, cols), f32)
    for dy, landing in ((-1, from_l), (1, from_r)):
        @pl.when(jnp.logical_not(side[dy]))
        def _(landing=landing):
            landing[:, :2] = jnp.ones((4, 2, half, cols), f32)
            landing[:, 2:] = jnp.zeros((4, flows - 1, half, cols), f32)
    for i, dx in enumerate((-1, 1)):
        for j, dy in enumerate((-1, 1)):
            @pl.when(jnp.logical_not(jnp.logical_and(has[dx], side[dy])))
            def _(i=i, j=j):
                from_c[i, j, :2] = jnp.ones((2, half, cols), f32)
                from_c[i, j, 2:] = jnp.zeros((6, half, cols), f32)
                wet_c[i, j] = jnp.zeros((half, cols), f32)

    def exchange(cond, src, dst, send, recv, back, device):
        args = dict(src_ref=src, dst_ref=dst, send_sem=send, device_id=device, device_id_type=MESH)
        return (cond, pltpu.make_async_remote_copy(recv_sem=recv, **args),
                pltpu.make_async_remote_copy(recv_sem=back, **args))

    started = []

    def begin(group):
        for cond, go, come in group:
            @pl.when(cond)
            def _(go=go):
                go.start()
        started.extend(group)

    def arrive(group):
        for cond, go, come in group:
            @pl.when(cond)
            def _(come=come):
                come.wait_recv()

    def row_copies(k, x, deep, part_of):
        group = []
        for i, dx in enumerate((-1, 1)):
            mine = deep if dx < 0 else rows
            theirs = deep + rows if dx < 0 else 0
            group.append(exchange(
                has[dx], part_of(x, mine), part_of(x, theirs),
                send_row.at[k, i], recv_row.at[k, i], recv_row.at[k, 1 - i], (gx + dx, gy)))
        return group

    def stage_rows(x, at):
        return x.at[:, pl.ds(at, H)]

    def result_rows(x, at):
        return x.at[pl.ds(0, 4), pl.ds(at, R), :, pl.ds(0, cols)]

    def column_copies(k, count):
        group = []
        for j, (dy, landing) in enumerate(((-1, from_r), (1, from_l))):
            group.append(exchange(
                side[dy], packed.at[k, pl.ds(0, count)], landing.at[k, pl.ds(0, count)],
                send_col.at[k, j], recv_col.at[k, j], recv_col.at[k, 1 - j], (gx, gy + dy)))
        return group

    def corner_copies(src, landing, send, recv):
        group = []
        for i, dx in enumerate((-1, 1)):
            for j, dy in enumerate((-1, 1)):
                group.append(exchange(
                    jnp.logical_and(has[dx], side[dy]), src, landing.at[1 - i, 1 - j],
                    send.at[i, j], recv.at[i, j], recv.at[1 - i, 1 - j], (gx + dx, gy + dy)))
        return group

    lane = lax.broadcasted_iota(jnp.int32, (half, cols), 1)
    seg = lane // SEG
    pos = lane % SEG
    own_right = pos < DEEP
    edge = jnp.logical_or(lane < H, lane >= cols - H)
    cuts = [slice(q * half, (q + 1) * half) for q in range(2)]

    def into(x, r, total):
        return jnp.where(seg == r, pltpu.roll(x, SEG * r + DEEP, 1), total)

    def out_of(x, r):
        return pltpu.roll(x, cols - DEEP - SEG * r, 1)

    for load in loads:
        load.wait()
    tile = tile_ref[(gx * rows) // TILE, (gy * cols) // TILE].astype(f32)
    for r in range(rows):
        wet[R + r, :, :cols] = wet_ref[r : r + 1, :].astype(f32) * tile

    def load_row(r, carry):
        at = pl.ds(r, layers, stride=rows)
        w = wet[R + r, :, :cols]
        carry = list(carry)
        for f in range(FIELDS):
            x = staged[f, at, :]
            if f == 0:
                x = x * w + (1.0 - w)
            elif f < 3:
                x = x * (1.0 / root)
            fa[f, H + r] = x
            for q in range(2):
                carry[2 * f + q] = into(x[cuts[q]], r, carry[2 * f + q])
        carry[flows] = into(jnp.broadcast_to(w, (half, cols)), r, carry[flows])
        return tuple(carry)

    blank = jnp.zeros((half, cols), f32)
    carry = (blank,) * (flows + 1)
    for lo, hi in ((0, H), (rows - H, rows)):
        carry = lax.fori_loop(lo, hi, load_row, carry, unroll=True)
    pl.semaphore_wait(barrier, len(peers))
    coming_rows = row_copies(0, fa, H, stage_rows)
    begin(coming_rows)
    wet_copies = []
    for i, dx in enumerate((-1, 1)):
        mine, theirs = (R, R + rows) if dx < 0 else (rows, 0)
        wet_copies.append(exchange(
            has[dx], wet.at[pl.ds(mine, R), :, pl.ds(0, cols)], wet.at[pl.ds(theirs, R), :, pl.ds(0, cols)],
            send_wet.at[i], recv_wet.at[i], recv_wet.at[1 - i], (gx + dx, gy)))
    begin(wet_copies)
    carry = lax.fori_loop(H, rows - H, load_row, carry, unroll=4)
    for n in range(flows + 1):
        packed[0, n] = carry[n]
    coming_cols = column_copies(0, flows + 1)
    begin(coming_cols)
    wet_corners = corner_copies(packed.at[0, flows], wet_c, send_wc, recv_wc)
    begin(wet_corners)

    inner = jnp.logical_and(lane >= 1, lane < cols - H)

    def column_weight(r, carry):
        w = jnp.broadcast_to(wet[R + r, :, :cols], (half, cols))
        wet_cols[r] = jnp.where(inner, (-time_step * root) * w * lane_next(w), 0.0)
        return carry

    def row_weight(r, carry):
        w = wet[R + r - 1, :, :cols] * wet[R + r, :, :cols]
        wet_rows[r] = jnp.broadcast_to((-time_step * root) * w, (half, cols))
        return carry

    lax.fori_loop(0, rows, column_weight, 0, unroll=4)
    lax.fori_loop(1, rows, row_weight, 0, unroll=5)

    def sweep(src, dst, deep, lo, hi, keep, unroll):
        for q in range(2):
            cut = cuts[q]

            def state(i):
                return [src[f, i + H, cut, :] for f in range(FIELDS)]

            def step(i, carry):
                flux_low, left, v0, v1, d = carry
                v2 = halves(state(i + 2))
                ahead = minus(v2, v1)
                right, following = sides(state(i + 1), d, ahead)
                flux_high = hll(left, right, wet_rows[i + 1], 1)
                u = state(i)
                across = across_flux(u, v0, wet_cols[i])
                for f in range(FIELDS):
                    rate = flux_high[f] - flux_low[f] + (across[f] - lane_prev(across[f]))
                    if keep is None:
                        new = u[f] + rate
                    elif keep == 0.75:
                        new = 0.75 * fa[f, i + H, cut, :] + 0.25 * (u[f] + rate)
                    else:
                        new = fa[f, i + H, cut, :] * (1.0 / 3.0) + (2.0 / 3.0) * (u[f] + rate)
                    dst[f, i + deep, cut, :cols] = new
                return flux_high, following, v1, v2, ahead

            a, b, c, e = [state(lo + o) for o in (-2, -1, 0, 1)]
            va, vb, vc, ve = [halves(x) for x in (a, b, c, e)]
            dab, dbc, dce = minus(vb, va), minus(vc, vb), minus(ve, vc)
            _, left = sides(b, dab, dbc)
            right, following = sides(c, dbc, dce)
            flux = hll(left, right, wet_rows[lo], 1)
            lax.fori_loop(lo, hi, step, (flux, following, vc, ve, dce), unroll=unroll)

    def edges(k, factor):
        for q in range(2):
            own = [packed[k, 2 * f + q] for f in range(FIELDS)]
            left = [jnp.where(own_right, from_l[k, 2 * f + q], own[f]) for f in range(FIELDS)]
            right = [jnp.where(own_right, own[f], from_r[k, 2 * f + q]) for f in range(FIELDS)]
            flux_l = across_flux(left, halves(left), wet_edge[0])
            flux_r = across_flux(right, halves(right), wet_edge[1])
            for f in range(FIELDS):
                a, b = flux_r[f] - lane_prev(flux_r[f]), flux_l[f] - lane_prev(flux_l[f])
                t = jnp.where(own_right, a, b)
                change[2 * f + q] = t if factor == 1.0 else factor * t

    def settle(dst, deep, last):
        def row(r, carry):
            carry = list(carry)
            for f in range(FIELDS):
                for q in range(2):
                    x = dst[f, r + deep, cuts[q], :cols]
                    x = x + jnp.where(edge, out_of(change[2 * f + q], r), 0.0)
                    if last and f in (1, 2):
                        x = x * root
                    dst[f, r + deep, cuts[q], :cols] = x
                    if not (last and f == 4):
                        carry[2 * f + q] = into(x, r, carry[2 * f + q])
            return tuple(carry)
        return row

    plan = ((fa, fb, H, None, 1.0), (fb, fc, H, 0.75, 0.25), (fc, res, R, 1.0 / 3.0, 2.0 / 3.0))
    for k, (src, dst, deep, keep, factor) in enumerate(plan):
        last = k == 2
        sweep(src, dst, deep, H, rows - H, keep, 6)
        if k == 0:
            arrive(wet_copies)
            for r in (0, rows):
                row_weight(r, 0)
        arrive(coming_rows)
        sweep(src, dst, deep, 0, H, keep, True)
        sweep(src, dst, deep, rows - H, rows, keep, True)
        arrive(coming_cols)
        if k == 0:
            own = packed[0, flows]
            for n, (w, first) in enumerate((
                    (jnp.where(own_right, from_l[0, flows], own), DEEP - 1),
                    (jnp.where(own_right, own, from_r[0, flows]), DEEP - 2))):
                used = jnp.logical_or(pos == first, pos == first + 1)
                wet_edge[n] = jnp.where(used, (-time_step * root) * w * lane_next(w), 0.0)
        edges(k, factor)
        row = settle(dst, deep, last)
        count = flows - 2 if last else flows
        carry = (blank,) * count
        for lo, hi in ((0, deep), (rows - deep, rows)):
            carry = lax.fori_loop(lo, hi, row, carry, unroll=True)
        coming_rows = row_copies(k + 1, dst, deep, result_rows if last else stage_rows)
        begin(coming_rows)
        carry = lax.fori_loop(deep, rows - deep, row, carry, unroll=4)
        for n in range(count):
            packed[k + 1, n] = carry[n]
        coming_cols = column_copies(k + 1, count)
        begin(coming_cols)
    coming_corners = corner_copies(packed.at[3, pl.ds(0, 8)], from_c, send_cor, recv_cor)
    begin(coming_corners)

    def unpack(left, right, wet_l, wet_r, base, shift):
        both = [jnp.where(own_right, left(n), right(n)) for n in range(8)]
        w = jnp.where(own_right, wet_l, wet_r)

        def row(r, carry):
            for f in range(4):
                for q in range(2):
                    res[f, r + base, cuts[q], cols:] = out_of(both[2 * f + q], r)
            wet[r + base, :, cols:] = out_of(w, r)[:1]
            return carry

        return row

    arrive(coming_cols)
    row = unpack(lambda n: from_l[3, n], lambda n: from_r[3, n], from_l[0, flows], from_r[0, flows], R, 0)
    lax.fori_loop(0, rows, row, 0, unroll=4)
    arrive(wet_corners)
    arrive(coming_corners)
    for i, (lo, base) in enumerate(((rows - R, R - rows), (0, R + rows))):
        row = unpack(lambda n: from_c[i, 0, n], lambda n: from_c[i, 1, n], wet_c[i, 0], wet_c[i, 1], base, 0)
        lax.fori_loop(lo, lo + R, row, 0, unroll=True)
    arrive(coming_rows)

    layer_id = lax.broadcasted_iota(jnp.int32, (layers, width), 0)
    top = layer_id == layers - 1

    def above(x):
        return pltpu.roll(x, layers - 1, 0)

    def below(x):
        return pltpu.roll(x, 1, 0)

    def prepare(r, low):
        h, w = res[0, r], wet[r]
        high = 0.5 * (h + res[0, r + 1]) * (w * wet[r + 1])
        across = 0.5 * (h + lane_next(h)) * (w * lane_next(jnp.broadcast_to(w, (layers, width))))
        total = jnp.where(top, h, h + above(h))
        upward = jnp.where(jnp.broadcast_to(w, total.shape) > 0.0, 2.0 / total, 0.0)
        inner = jnp.where(top, 0.0, upward)
        diagonal = 0.5 * h + low + high + lane_prev(across) + across + below(inner) + upward
        v = res[3, r]
        y = res[2, r]
        div = (
            0.5 * (res[1, r + 1] - res[1, r - 1])
            + 0.5 * (lane_next(y) - lane_prev(y))
            + (v - jnp.where(layer_id == 0, 0.0, below(v)))
        )
        force = -div * w
        inverse = jnp.where(diagonal == 0.0, 0.0, 1.0 / diagonal)
        ce[r] = high
        cn[r] = across
        up[r] = upward
        inv[r] = inverse
        z = force * inverse
        z0[r] = z
        return high, force, z

    def fold(x):
        return x[:half, :cols] + x[half:, :cols]

    first = R - ITERS
    ce[first - 1] = 0.5 * (res[0, first - 1] + res[0, first]) * (wet[first - 1] * wet[first])

    def prep_outer(r, low):
        return prepare(r, low)[0]

    def prep_inner(r, carry):
        low, acc = carry
        high, force, z = prepare(r, low)
        return high, acc + fold(force * z)

    zero = jnp.zeros((half, cols), jnp.float32)
    low = lax.fori_loop(first, R, prep_outer, ce[first - 1], unroll=True)
    low, m0 = lax.fori_loop(R, R + rows, prep_inner, (low, zero), unroll=4)
    lax.fori_loop(R + rows, R + rows + ITERS, prep_outer, low, unroll=True)

    def spread(z, r):
        x = z[r]
        c = cn[r]
        u = jnp.where(top, 0.0, up[r])
        return (
            ce[r - 1] * z[r - 1] + ce[r] * z[r + 1]
            + c * lane_next(x) + lane_prev(c * x)
            + u * above(x) + below(u * x)
        )

    def advance(z, target, reach):
        def outer(r, carry):
            target[r] = spread(z, r) * inv[r]
            return carry

        def inner(r, carry):
            odd, even = carry
            n = spread(z, r)
            y = n * inv[r]
            target[r] = y
            return odd + fold(z[r] * n), even + fold(y * n)

        lax.fori_loop(R - reach, R, outer, 0, unroll=True)
        sums = lax.fori_loop(R, R + rows, inner, (zero, zero), unroll=4)
        lax.fori_loop(R + rows, R + rows + reach, outer, 0, unroll=True)
        return sums

    m1, m2 = advance(z0, z1, 2)
    m3, m4 = advance(z1, z2, 1)
    m5 = lax.fori_loop(R, R + rows, lambda r, acc: acc + fold(z2[r] * spread(z2, r)), zero, unroll=4)

    row_id = lax.broadcasted_iota(jnp.int32, (8, cols), 0)
    lane_id = lax.broadcasted_iota(jnp.int32, (8, cols), 1)
    diagonal_at = row_id == lane_id
    table = blank
    for k, x in enumerate((m0, m1, m2, m3, m4, m5)):
        table = jnp.where(row_id == k, jnp.sum(x, axis=0, keepdims=True), table)
    table = jnp.where(diagonal_at, jnp.sum(table, axis=1, keepdims=True), 0.0)
    own = len(peers)
    gather[own : own + 1, :] = jnp.sum(table, axis=0, keepdims=True)
    for n, (a, b) in enumerate(reversed(peers)):
        pltpu.make_async_remote_copy(
            src_ref=gather.at[pl.ds(own, 1)], dst_ref=gather.at[pl.ds(n, 1)], send_sem=send_sum, recv_sem=recv_sum,
            device_id=peer(a, b), device_id_type=MESH).start()

    def push_of(k, z):
        def row(r, carry):
            q, c = z[r], cn[r]
            east = 0.5 * (ce[r] * (z[r + 1] - q) + ce[r - 1] * (q - z[r - 1]))
            slope = c * (lane_next(q) - q)
            north = 0.5 * (slope + lane_prev(slope))
            upward = up[r] * (jnp.where(top, 0.0, above(q)) - q)
            for n, push in enumerate((east, north, upward)):
                pushes[k, n, r - R] = push[:, :cols]
            return carry

        lax.fori_loop(R, R + rows, row, 0, unroll=4)

    def plain_out(r, carry):
        at = pl.ds(r - R, layers, stride=rows)
        depth_out[at, :] = jnp.where(jnp.broadcast_to(wet[r, :, :cols], (layers, cols)) > 0.0, res[0, r, :, :cols], staged[0, at, :])
        tracer_out[at, :] = res[4, r, :, :cols]
        return carry

    push_of(0, z0)
    push_of(1, z1)
    push_of(2, z2)
    lax.fori_loop(R, R + rows, plain_out, 0, unroll=4)
    all_sums = pltpu.make_async_remote_copy(
        src_ref=gather.at[pl.ds(0, own)], dst_ref=gather.at[pl.ds(0, own)], send_sem=send_sum, recv_sem=recv_sum,
        device_id=peer(1, 0), device_id_type=MESH)
    all_sums.wait_recv()
    table = jnp.sum(gather[...], axis=0, keepdims=True)
    table = jnp.where(diagonal_at, table, 0.0)
    sums = jnp.broadcast_to(jnp.sum(table, axis=1, keepdims=True), (8, cols))
    m = [sums[k : k + 1, :] for k in range(6)]

    def dots(a, b, table):
        out = None
        for i in range(3):
            for j in range(3):
                if a[i] is not None and b[j] is not None:
                    t = a[i] * b[j] * table[i + j]
                    out = t if out is None else out + t
        return out

    shifted = [m[k] - m[k + 1] for k in range(5)]

    def plus(a, b, f):
        out = []
        for x, y in zip(a, b):
            out.append(x if y is None else (f * y if x is None else x + f * y))
        return out

    def image(d):
        moved = [None, d[0], d[1]]
        return [x if y is None else (None if x is None and y is None else (-y if x is None else x - y)) for x, y in zip(d, moved)]

    one = jnp.ones_like(m[0])
    direction = [one, None, None]
    residual = [one, None, None]
    pressure = [None, None, None]
    energy = m[0]
    for sweep in range(ITERS):
        bottom = dots(direction, direction, shifted)
        size = energy / bottom
        pressure = plus(pressure, direction, size)
        if sweep + 1 < ITERS:
            residual = plus(residual, image(direction), -size)
            fresh = dots(residual, residual, m)
            direction = plus(residual, direction, fresh / energy)
            energy = fresh

    def correct(r, carry):
        at = pl.ds(r - R, layers, stride=rows)
        for n in range(3):
            push = pressure[0] * pushes[0, n, r - R]
            push = push + pressure[1] * pushes[1, n, r - R] + pressure[2] * pushes[2, n, r - R]
            mom_out[n, at, :] = res[1 + n, r, :, :cols] - push
        return carry

    lax.fori_loop(R, R + rows, correct, 0, unroll=4)
    all_sums.wait_send()
    for cond, go, come in started:
        @pl.when(cond)
        def _(go=go):
            go.wait_send()


def body(nx, ny, depth, momentum, tracer, cell_wet, tile_wet):
    layers, rows, cols = depth.shape
    assert TILE % rows == 0 and TILE % cols == 0 and cols == 128 and rows * SEG == cols and layers == 16
    f32 = jnp.float32
    tall = rows + 2 * DEEP
    wide = 2 * cols
    half = layers // 2
    dma = pltpu.SemaphoreType.DMA
    vmem = pl.BlockSpec(memory_space=pltpu.VMEM)
    flat = jax.ShapeDtypeStruct((layers * rows, cols), f32)
    field = pltpu.VMEM((FIELDS, rows + 2 * REACH, layers, cols), f32)
    layer = pltpu.VMEM((tall, layers, wide), f32)
    flows = 2 * FIELDS
    strip = pltpu.VMEM((4, flows + 1, half, cols), f32)
    pairs = [dma((4, 2))] * 2 + [dma((2,))] * 2 + [dma((4, 2))] * 2 + [dma((2, 2))] * 4
    pairs += [dma] * 2
    new_depth, new_momentum, new_tracer = pl.pallas_call(
        functools.partial(kernel, nx, ny, rows, cols, layers),
        out_shape=(pltpu.VMEM((layers * rows, cols), f32), pltpu.VMEM((3, layers * rows, cols), f32), pltpu.VMEM((layers * rows, cols), f32)),
        in_specs=[pl.BlockSpec(memory_space=pltpu.HBM)] * 5,
        out_specs=(vmem, vmem, vmem),
        scratch_shapes=[
            pltpu.VMEM((5, layers * rows, cols), f32),
            pltpu.VMEM((rows, cols), jnp.int32),
            pltpu.SMEM(tile_wet.shape, jnp.int32),
            dma((5,)),
            pltpu.VMEM((3, 3, rows, layers, cols), f32),
            field, field, field,
            pltpu.VMEM((FIELDS, tall, layers, wide), f32),
            pltpu.VMEM((tall, 1, wide), f32),
            pltpu.VMEM((rows + 1, half, cols), f32),
            pltpu.VMEM((rows, half, cols), f32),
            pltpu.VMEM((2, half, cols), f32),
            strip, strip, strip,
            pltpu.VMEM((2, 2, 8, half, cols), f32),
            pltpu.VMEM((2, 2, half, cols), f32),
            pltpu.VMEM((flows, half, cols), f32),
            layer, layer, layer, layer, layer, layer, layer,
            pltpu.VMEM((nx * ny, cols), f32),
            *pairs,
        ],
        compiler_params=pltpu.CompilerParams(
            collective_id=0, has_side_effects=True, vmem_limit_bytes=56 * 1024 * 1024
        ),
    )(
        tile_wet,
        depth.reshape(layers * rows, cols),
        momentum.reshape(3, layers * rows, cols),
        tracer.reshape(layers * rows, cols),
        cell_wet,
    )
    new_depth, new_momentum, new_tracer = pl.pallas_call(
        hand_on,
        out_shape=(flat, jax.ShapeDtypeStruct((3, layers * rows, cols), f32), flat),
        in_specs=[pl.BlockSpec(memory_space=pl.ANY)] * 3,
        out_specs=(pl.BlockSpec(memory_space=pl.ANY),) * 3,
        scratch_shapes=[dma((3,))],
        compiler_params=pltpu.CompilerParams(vmem_limit_bytes=8 * 1024 * 1024),
    )(new_depth, new_momentum, new_tracer)
    return (
        new_depth.reshape(depth.shape),
        new_momentum.reshape(momentum.shape),
        new_tracer.reshape(tracer.shape),
    )


def hand_on(a, b, c, x, y, z, sem):
    moves = [pltpu.make_async_copy(s, d, sem.at[k]) for k, (s, d) in enumerate(((a, x), (b, y), (c, z)))]
    for m in moves:
        m.start()
    for m in moves:
        m.wait()


def solution(mesh):
    placed = (
        P(None, "gx", "gy"),
        P(None, None, "gx", "gy"),
        P(None, "gx", "gy"),
        P("gx", "gy"),
        P(),
    )
    return jax.shard_map(
        functools.partial(body, mesh.shape["gx"], mesh.shape["gy"]),
        mesh=mesh,
        in_specs=placed,
        out_specs=(P(None, "gx", "gy"), P(None, None, "gx", "gy"), P(None, "gx", "gy")),
        check_vma=False,
    )
```

```python
import functools

import jax
import jax.numpy as jnp
from jax import lax
from jax.experimental import pallas as pl
from jax.experimental.pallas import tpu as pltpu
from jax.sharding import PartitionSpec as P

ITERS = 3
TILE = 128
REACH = 2
DEEP = 1 + ITERS
SEG = 2 * DEEP
FIELDS = 5

gravity = 9.81
time_step = 0.025
root = gravity**0.5
MESH = pl.DeviceIdType.MESH


def minmod(a, b):
    return jnp.maximum(jnp.minimum(a, jnp.maximum(b, 0.0)), jnp.minimum(b, 0.0))


def hll(left, right, weight, normal):
    hl, hr = left[0], right[0]
    rl, rr = lax.rsqrt(hl), lax.rsqrt(hr)
    ul, ur = left[normal] * (rl * rl), right[normal] * (rr * rr)
    al, ar = hl * rl, hr * rr
    lower = jnp.minimum(jnp.minimum(ul - al, ur - ar), 0.0)
    upper = jnp.maximum(jnp.maximum(ul + al, ur + ar), 0.0)
    scale = weight / (upper - lower)
    low, high = lower * scale, upper * scale
    take_left = high * (ul - lower)
    take_right = low * (upper - ur)
    flux = [take_left * l + take_right * r for l, r in zip(left, right)]
    flux[normal] = flux[normal] + 0.5 * (high * hl * hl - low * hr * hr)
    return flux


def lane_next(x):
    return pltpu.roll(x, x.shape[-1] - 1, 1)


def lane_prev(x):
    return pltpu.roll(x, 1, 1)


def halves(u):
    return [0.5 * x for x in u]


def minus(a, b):
    return [x - y for x, y in zip(a, b)]


def sides(u, before, after):
    s = [minmod(b, a) for b, a in zip(before, after)]
    return minus(u, s), [x + y for x, y in zip(u, s)]


def across_flux(u, v, weight):
    d = [lane_next(x) - x for x in v]
    right, left = sides(u, [lane_prev(x) for x in d], d)
    return hll(left, [lane_next(x) for x in right], weight, 2)


def kernel(
    nx, ny, rows, cols, layers,
    tile_hbm, depth_hbm, mom_hbm, tracer_hbm, wet_hbm,
    depth_out, mom_out, tracer_out,
    staged, wet_ref, tile_ref, load_sem, pushes,
    fa, fb, fc, res, wet, wet_rows, wet_cols, wet_edge, packed, from_l, from_r, from_c, wet_c, change,
    ce, cn, up, inv, z0, z1, z2, gather,
    send_row, recv_row, send_wet, recv_wet, send_col, recv_col,
    send_wc, recv_wc, send_cor, recv_cor, send_sum, recv_sum,
):
    R = DEEP
    H = REACH
    width = 2 * cols
    half = layers // 2
    flows = 2 * FIELDS
    gx, gy = lax.axis_index("gx"), lax.axis_index("gy")

    loads = [
        pltpu.make_async_copy(wet_hbm, wet_ref, load_sem.at[0]),
        pltpu.make_async_copy(tile_hbm, tile_ref, load_sem.at[4]),
        pltpu.make_async_copy(depth_hbm, staged.at[0], load_sem.at[1]),
        pltpu.make_async_copy(mom_hbm, staged.at[pl.ds(1, 3)], load_sem.at[2]),
        pltpu.make_async_copy(tracer_hbm, staged.at[4], load_sem.at[3]),
    ]

    barrier = pltpu.get_barrier_semaphore()
    has = {-1: gx > 0, 1: gx < nx - 1}
    side = {-1: gy > 0, 1: gy < ny - 1}
    near = [(a, b) for a in (1, nx - 1, 0) for b in (0, 1, ny - 1) if (a, b) != (0, 0)]
    peers = list(dict.fromkeys(near)) + [
        (a, b) for a in range(nx) for b in range(ny) if (a, b) not in near and (a, b) != (0, 0)]

    def peer(a, b):
        return (lax.rem(gx + a, nx), lax.rem(gy + b, ny))

    for n, (a, b) in enumerate(peers):
        pl.semaphore_signal(barrier, inc=1, device_id=peer(a, b), device_id_type=MESH)
        if n + 1 == len(near):
            for load in loads:
                load.start()

    f32 = jnp.float32
    for dx in (-1, 1):
        @pl.when(jnp.logical_not(has[dx]))
        def _(dx=dx):
            at = slice(0, H) if dx < 0 else slice(H + rows, rows + 2 * H)
            for x in (fa, fb, fc):
                x[0, at] = jnp.ones((H, layers, cols), f32)
                x[1:, at] = jnp.zeros((FIELDS - 1, H, layers, cols), f32)
            at = slice(0, R) if dx < 0 else slice(R + rows, rows + 2 * R)
            res[0, at, :, :cols] = jnp.ones((R, layers, cols), f32)
            res[1:4, at, :, :cols] = jnp.zeros((3, R, layers, cols), f32)
            wet[at, :, :cols] = jnp.zeros((R, 1, cols), f32)
    for dy, landing in ((-1, from_l), (1, from_r)):
        @pl.when(jnp.logical_not(side[dy]))
        def _(landing=landing):
            landing[:, :2] = jnp.ones((4, 2, half, cols), f32)
            landing[:, 2:] = jnp.zeros((4, flows - 1, half, cols), f32)
    for i, dx in enumerate((-1, 1)):
        for j, dy in enumerate((-1, 1)):
            @pl.when(jnp.logical_not(jnp.logical_and(has[dx], side[dy])))
            def _(i=i, j=j):
                from_c[i, j, :2] = jnp.ones((2, half, cols), f32)
                from_c[i, j, 2:] = jnp.zeros((6, half, cols), f32)
                wet_c[i, j] = jnp.zeros((half, cols), f32)

    def exchange(cond, src, dst, send, recv, back, device):
        args = dict(src_ref=src, dst_ref=dst, send_sem=send, device_id=device, device_id_type=MESH)
        return (cond, pltpu.make_async_remote_copy(recv_sem=recv, **args),
                pltpu.make_async_remote_copy(recv_sem=back, **args))

    started = []

    def begin(group):
        for cond, go, come in group:
            @pl.when(cond)
            def _(go=go):
                go.start()
        started.extend(group)

    def arrive(group):
        for cond, go, come in group:
            @pl.when(cond)
            def _(come=come):
                come.wait_recv()

    def row_copies(k, x, deep, part_of):
        group = []
        for i, dx in enumerate((-1, 1)):
            mine = deep if dx < 0 else rows
            theirs = deep + rows if dx < 0 else 0
            group.append(exchange(
                has[dx], part_of(x, mine), part_of(x, theirs),
                send_row.at[k, i], recv_row.at[k, i], recv_row.at[k, 1 - i], (gx + dx, gy)))
        return group

    def stage_rows(x, at):
        return x.at[:, pl.ds(at, H)]

    def result_rows(x, at):
        return x.at[pl.ds(0, 4), pl.ds(at, R), :, pl.ds(0, cols)]

    def column_copies(k, count):
        group = []
        for j, (dy, landing) in enumerate(((-1, from_r), (1, from_l))):
            group.append(exchange(
                side[dy], packed.at[k, pl.ds(0, count)], landing.at[k, pl.ds(0, count)],
                send_col.at[k, j], recv_col.at[k, j], recv_col.at[k, 1 - j], (gx, gy + dy)))
        return group

    def corner_copies(src, landing, send, recv):
        group = []
        for i, dx in enumerate((-1, 1)):
            for j, dy in enumerate((-1, 1)):
                group.append(exchange(
                    jnp.logical_and(has[dx], side[dy]), src, landing.at[1 - i, 1 - j],
                    send.at[i, j], recv.at[i, j], recv.at[1 - i, 1 - j], (gx + dx, gy + dy)))
        return group

    lane = lax.broadcasted_iota(jnp.int32, (half, cols), 1)
    seg = lane // SEG
    pos = lane % SEG
    own_right = pos < DEEP
    edge = jnp.logical_or(lane < H, lane >= cols - H)
    cuts = [slice(q * half, (q + 1) * half) for q in range(2)]

    def into(x, r, total):
        return jnp.where(seg == r, pltpu.roll(x, SEG * r + DEEP, 1), total)

    def out_of(x, r):
        return pltpu.roll(x, cols - DEEP - SEG * r, 1)

    for load in loads:
        load.wait()
    tile = tile_ref[(gx * rows) // TILE, (gy * cols) // TILE].astype(f32)
    for r in range(rows):
        wet[R + r, :, :cols] = wet_ref[r : r + 1, :].astype(f32) * tile

    def load_row(r, carry):
        at = pl.ds(r, layers, stride=rows)
        w = wet[R + r, :, :cols]
        carry = list(carry)
        for f in range(FIELDS):
            x = staged[f, at, :]
            if f == 0:
                x = x * w + (1.0 - w)
            elif f < 3:
                x = x * (1.0 / root)
            fa[f, H + r] = x
            for q in range(2):
                carry[2 * f + q] = into(x[cuts[q]], r, carry[2 * f + q])
        carry[flows] = into(jnp.broadcast_to(w, (half, cols)), r, carry[flows])
        return tuple(carry)

    blank = jnp.zeros((half, cols), f32)
    carry = (blank,) * (flows + 1)
    for lo, hi in ((0, H), (rows - H, rows)):
        carry = lax.fori_loop(lo, hi, load_row, carry, unroll=True)
    pl.semaphore_wait(barrier, len(peers))
    coming_rows = row_copies(0, fa, H, stage_rows)
    begin(coming_rows)
    wet_copies = []
    for i, dx in enumerate((-1, 1)):
        mine, theirs = (R, R + rows) if dx < 0 else (rows, 0)
        wet_copies.append(exchange(
            has[dx], wet.at[pl.ds(mine, R), :, pl.ds(0, cols)], wet.at[pl.ds(theirs, R), :, pl.ds(0, cols)],
            send_wet.at[i], recv_wet.at[i], recv_wet.at[1 - i], (gx + dx, gy)))
    begin(wet_copies)
    carry = lax.fori_loop(H, rows - H, load_row, carry, unroll=4)
    for n in range(flows + 1):
        packed[0, n] = carry[n]
    coming_cols = column_copies(0, flows + 1)
    begin(coming_cols)
    wet_corners = corner_copies(packed.at[0, flows], wet_c, send_wc, recv_wc)
    begin(wet_corners)

    inner = jnp.logical_and(lane >= 1, lane < cols - H)

    def column_weight(r, carry):
        w = jnp.broadcast_to(wet[R + r, :, :cols], (half, cols))
        wet_cols[r] = jnp.where(inner, (-time_step * root) * w * lane_next(w), 0.0)
        return carry

    def row_weight(r, carry):
        w = wet[R + r - 1, :, :cols] * wet[R + r, :, :cols]
        wet_rows[r] = jnp.broadcast_to((-time_step * root) * w, (half, cols))
        return carry

    lax.fori_loop(0, rows, column_weight, 0, unroll=4)
    lax.fori_loop(1, rows, row_weight, 0, unroll=5)

    def state(src, i, cut):
        return [src[f, i + H, cut, :] for f in range(FIELDS)]

    def blend(keep, i, cut, f, value):
        if keep is None:
            return value
        kept = fa[f, i + H, cut, :]
        if keep == 0.75:
            return 0.75 * kept + 0.25 * value
        return (1.0 / 3.0) * kept + (2.0 / 3.0) * value

    def sweep(src, dst, deep, keep):
        for cut in cuts:
            def store(i, rates, cut=cut):
                u = state(src, i, cut)
                across = across_flux(u, halves(u), wet_cols[i])
                for f in range(FIELDS):
                    rate = across[f] - lane_prev(across[f])
                    if rates is not None:
                        rate = rate + rates[f]
                    dst[f, i + deep, cut, :cols] = blend(keep, i, cut, f, u[f] + rate)

            def step(i, carry, cut=cut, store=store):
                flux_low, left, v1, d = carry
                v2 = halves(state(src, i + 2, cut))
                ahead = minus(v2, v1)
                right, following = sides(state(src, i + 1, cut), d, ahead)
                flux_high = hll(left, right, wet_rows[i + 1], 1)
                store(i, minus(flux_high, flux_low))
                return flux_high, following, v2, ahead

            a, b, c, e = [state(src, i, cut) for i in range(4)]
            va, vb, vc, ve = [halves(x) for x in (a, b, c, e)]
            dab, dbc, dce = minus(vb, va), minus(vc, vb), minus(ve, vc)
            _, left = sides(b, dab, dbc)
            right, following = sides(c, dbc, dce)
            flux = hll(left, right, wet_rows[H], 1)
            store(0, None)
            store(1, flux)
            flux, _, _, _ = lax.fori_loop(H, rows - H, step, (flux, following, ve, dce), unroll=6)
            store(rows - 2, [-x for x in flux])
            store(rows - 1, None)

    def ends(src, dst, deep, factor):
        for cut in cuts:
            for first in (-2, rows - 3):
                u = [state(src, first + n, cut) for n in range(5)]
                v = [halves(x) for x in u]
                d = [minus(y, x) for x, y in zip(v[:4], v[1:])]
                sided = [sides(u[n], d[n - 1], d[n]) for n in (1, 2, 3)]
                one = hll(sided[0][1], sided[1][0], wet_rows[first + 2], 1)
                two = hll(sided[1][1], sided[2][0], wet_rows[first + 3], 1)
                if first < 0:
                    changes = ((0, minus(two, one)), (1, [-x for x in two]))
                else:
                    changes = ((rows - 2, one), (rows - 1, minus(two, one)))
                for i, rates in changes:
                    for f in range(FIELDS):
                        rate = rates[f] if factor == 1.0 else factor * rates[f]
                        dst[f, i + deep, cut, :cols] = dst[f, i + deep, cut, :cols] + rate

    def edges(k, factor):
        for q in range(2):
            own = [packed[k, 2 * f + q] for f in range(FIELDS)]
            left = [jnp.where(own_right, from_l[k, 2 * f + q], own[f]) for f in range(FIELDS)]
            right = [jnp.where(own_right, own[f], from_r[k, 2 * f + q]) for f in range(FIELDS)]
            flux_l = across_flux(left, halves(left), wet_edge[0])
            flux_r = across_flux(right, halves(right), wet_edge[1])
            for f in range(FIELDS):
                a, b = flux_r[f] - lane_prev(flux_r[f]), flux_l[f] - lane_prev(flux_l[f])
                t = jnp.where(own_right, a, b)
                change[2 * f + q] = t if factor == 1.0 else factor * t

    def pack(dst, deep, count):
        def row(r, carry):
            return tuple(
                into(dst[n // 2, r + deep, cuts[n % 2], :cols], r, carry[n]) for n in range(count))
        return row

    def mend(dst, deep, last):
        def row(r, carry):
            for f in range(FIELDS):
                for q in range(2):
                    x = dst[f, r + deep, cuts[q], :cols]
                    x = x + jnp.where(edge, out_of(change[2 * f + q], r), 0.0)
                    dst[f, r + deep, cuts[q], :cols] = x * root if last and f in (1, 2) else x
            return carry
        return row

    plan = ((fa, fb, H, None, 1.0), (fb, fc, H, 0.75, 0.25), (fc, res, R, 1.0 / 3.0, 2.0 / 3.0))
    for k, (src, dst, deep, keep, factor) in enumerate(plan):
        last = k == 2
        count = flows - 2 if last else flows
        sweep(src, dst, deep, keep)
        pack_row, mend_row = pack(dst, deep, count), mend(dst, deep, last)
        carry = lax.fori_loop(H, rows - H, pack_row, (blank,) * count, unroll=4)
        if k == 0:
            arrive(wet_copies)
            for r in (0, rows):
                row_weight(r, 0)
        arrive(coming_rows)
        ends(src, dst, deep, factor)
        arrive(coming_cols)
        if k == 0:
            own = packed[0, flows]
            for n, (w, first) in enumerate((
                    (jnp.where(own_right, from_l[0, flows], own), DEEP - 1),
                    (jnp.where(own_right, own, from_r[0, flows]), DEEP - 2))):
                used = jnp.logical_or(pos == first, pos == first + 1)
                wet_edge[n] = jnp.where(used, (-time_step * root) * w * lane_next(w), 0.0)
        edges(k, factor)
        for lo, hi in ((0, H), (rows - H, rows)):
            carry = lax.fori_loop(lo, hi, pack_row, carry, unroll=True)
        for n in range(count):
            x = carry[n] + change[n]
            packed[k + 1, n] = x * root if last and n // 2 in (1, 2) else x
        for lo, hi in ((0, deep), (rows - deep, rows)):
            lax.fori_loop(lo, hi, mend_row, 0, unroll=True)
        coming_cols = column_copies(k + 1, count)
        begin(coming_cols)
        coming_rows = row_copies(k + 1, dst, deep, result_rows if last else stage_rows)
        begin(coming_rows)
        lax.fori_loop(deep, rows - deep, mend_row, 0, unroll=4)
    coming_corners = corner_copies(packed.at[3, pl.ds(0, 8)], from_c, send_cor, recv_cor)
    begin(coming_corners)

    def unpack(left, right, wet_l, wet_r, base, shift):
        both = [jnp.where(own_right, left(n), right(n)) for n in range(8)]
        w = jnp.where(own_right, wet_l, wet_r)

        def row(r, carry):
            for f in range(4):
                for q in range(2):
                    res[f, r + base, cuts[q], cols:] = out_of(both[2 * f + q], r)
            wet[r + base, :, cols:] = out_of(w, r)[:1]
            return carry

        return row

    arrive(coming_cols)
    row = unpack(lambda n: from_l[3, n], lambda n: from_r[3, n], from_l[0, flows], from_r[0, flows], R, 0)
    lax.fori_loop(0, rows, row, 0, unroll=4)
    arrive(wet_corners)
    arrive(coming_corners)
    for i, (lo, base) in enumerate(((rows - R, R - rows), (0, R + rows))):
        row = unpack(lambda n: from_c[i, 0, n], lambda n: from_c[i, 1, n], wet_c[i, 0], wet_c[i, 1], base, 0)
        lax.fori_loop(lo, lo + R, row, 0, unroll=True)
    arrive(coming_rows)

    layer_id = lax.broadcasted_iota(jnp.int32, (layers, width), 0)
    top = layer_id == layers - 1

    def above(x):
        return pltpu.roll(x, layers - 1, 0)

    def below(x):
        return pltpu.roll(x, 1, 0)

    def prepare(r, low):
        h, w = res[0, r], wet[r]
        high = 0.5 * (h + res[0, r + 1]) * (w * wet[r + 1])
        across = 0.5 * (h + lane_next(h)) * (w * lane_next(jnp.broadcast_to(w, (layers, width))))
        total = jnp.where(top, h, h + above(h))
        upward = jnp.where(jnp.broadcast_to(w, total.shape) > 0.0, 2.0 / total, 0.0)
        inner = jnp.where(top, 0.0, upward)
        diagonal = 0.5 * h + low + high + lane_prev(across) + across + below(inner) + upward
        v = res[3, r]
        y = res[2, r]
        div = (
            0.5 * (res[1, r + 1] - res[1, r - 1])
            + 0.5 * (lane_next(y) - lane_prev(y))
            + (v - jnp.where(layer_id == 0, 0.0, below(v)))
        )
        force = -div * w
        inverse = jnp.where(diagonal == 0.0, 0.0, 1.0 / diagonal)
        ce[r] = high
        cn[r] = across
        up[r] = upward
        inv[r] = inverse
        z = force * inverse
        z0[r] = z
        return high, force, z

    def fold(x):
        return x[:half, :cols] + x[half:, :cols]

    first = R - ITERS
    ce[first - 1] = 0.5 * (res[0, first - 1] + res[0, first]) * (wet[first - 1] * wet[first])

    def prep_outer(r, low):
        return prepare(r, low)[0]

    def prep_inner(r, carry):
        low, acc = carry
        high, force, z = prepare(r, low)
        return high, acc + fold(force * z)

    zero = jnp.zeros((half, cols), jnp.float32)
    low = lax.fori_loop(first, R, prep_outer, ce[first - 1], unroll=True)
    low, m0 = lax.fori_loop(R, R + rows, prep_inner, (low, zero), unroll=4)
    lax.fori_loop(R + rows, R + rows + ITERS, prep_outer, low, unroll=True)

    def spread(z, r):
        x = z[r]
        c = cn[r]
        u = jnp.where(top, 0.0, up[r])
        return (
            ce[r - 1] * z[r - 1] + ce[r] * z[r + 1]
            + c * lane_next(x) + lane_prev(c * x)
            + u * above(x) + below(u * x)
        )

    def advance(z, target, reach):
        def outer(r, carry):
            target[r] = spread(z, r) * inv[r]
            return carry

        def inner(r, carry):
            odd, even = carry
            n = spread(z, r)
            y = n * inv[r]
            target[r] = y
            return odd + fold(z[r] * n), even + fold(y * n)

        lax.fori_loop(R - reach, R, outer, 0, unroll=True)
        sums = lax.fori_loop(R, R + rows, inner, (zero, zero), unroll=4)
        lax.fori_loop(R + rows, R + rows + reach, outer, 0, unroll=True)
        return sums

    m1, m2 = advance(z0, z1, 2)
    m3, m4 = advance(z1, z2, 1)
    m5 = lax.fori_loop(R, R + rows, lambda r, acc: acc + fold(z2[r] * spread(z2, r)), zero, unroll=4)

    row_id = lax.broadcasted_iota(jnp.int32, (8, cols), 0)
    lane_id = lax.broadcasted_iota(jnp.int32, (8, cols), 1)
    diagonal_at = row_id == lane_id
    table = blank
    for k, x in enumerate((m0, m1, m2, m3, m4, m5)):
        table = jnp.where(row_id == k, jnp.sum(x, axis=0, keepdims=True), table)
    table = jnp.where(diagonal_at, jnp.sum(table, axis=1, keepdims=True), 0.0)
    own = len(peers)
    gather[own : own + 1, :] = jnp.sum(table, axis=0, keepdims=True)
    for n, (a, b) in enumerate(reversed(peers)):
        pltpu.make_async_remote_copy(
            src_ref=gather.at[pl.ds(own, 1)], dst_ref=gather.at[pl.ds(n, 1)], send_sem=send_sum, recv_sem=recv_sum,
            device_id=peer(a, b), device_id_type=MESH).start()

    def push_of(k, z):
        def row(r, carry):
            q, c = z[r], cn[r]
            east = 0.5 * (ce[r] * (z[r + 1] - q) + ce[r - 1] * (q - z[r - 1]))
            slope = c * (lane_next(q) - q)
            north = 0.5 * (slope + lane_prev(slope))
            upward = up[r] * (jnp.where(top, 0.0, above(q)) - q)
            for n, push in enumerate((east, north, upward)):
                pushes[k, n, r - R] = push[:, :cols]
            return carry

        lax.fori_loop(R, R + rows, row, 0, unroll=4)

    def plain_out(r, carry):
        at = pl.ds(r - R, layers, stride=rows)
        depth_out[at, :] = jnp.where(jnp.broadcast_to(wet[r, :, :cols], (layers, cols)) > 0.0, res[0, r, :, :cols], staged[0, at, :])
        tracer_out[at, :] = res[4, r, :, :cols]
        return carry

    push_of(0, z0)
    push_of(1, z1)
    push_of(2, z2)
    lax.fori_loop(R, R + rows, plain_out, 0, unroll=4)
    all_sums = pltpu.make_async_remote_copy(
        src_ref=gather.at[pl.ds(0, own)], dst_ref=gather.at[pl.ds(0, own)], send_sem=send_sum, recv_sem=recv_sum,
        device_id=peer(1, 0), device_id_type=MESH)
    all_sums.wait_recv()
    table = jnp.sum(gather[...], axis=0, keepdims=True)
    table = jnp.where(diagonal_at, table, 0.0)
    sums = jnp.broadcast_to(jnp.sum(table, axis=1, keepdims=True), (8, cols))
    m = [sums[k : k + 1, :] for k in range(6)]

    def dots(a, b, table):
        out = None
        for i in range(3):
            for j in range(3):
                if a[i] is not None and b[j] is not None:
                    t = a[i] * b[j] * table[i + j]
                    out = t if out is None else out + t
        return out

    shifted = [m[k] - m[k + 1] for k in range(5)]

    def plus(a, b, f):
        out = []
        for x, y in zip(a, b):
            out.append(x if y is None else (f * y if x is None else x + f * y))
        return out

    def image(d):
        moved = [None, d[0], d[1]]
        return [x if y is None else (None if x is None and y is None else (-y if x is None else x - y)) for x, y in zip(d, moved)]

    one = jnp.ones_like(m[0])
    direction = [one, None, None]
    residual = [one, None, None]
    pressure = [None, None, None]
    energy = m[0]
    for sweep in range(ITERS):
        bottom = dots(direction, direction, shifted)
        size = energy / bottom
        pressure = plus(pressure, direction, size)
        if sweep + 1 < ITERS:
            residual = plus(residual, image(direction), -size)
            fresh = dots(residual, residual, m)
            direction = plus(residual, direction, fresh / energy)
            energy = fresh

    def correct(r, carry):
        at = pl.ds(r - R, layers, stride=rows)
        for n in range(3):
            push = pressure[0] * pushes[0, n, r - R]
            push = push + pressure[1] * pushes[1, n, r - R] + pressure[2] * pushes[2, n, r - R]
            mom_out[n, at, :] = res[1 + n, r, :, :cols] - push
        return carry

    lax.fori_loop(R, R + rows, correct, 0, unroll=4)
    all_sums.wait_send()
    for cond, go, come in started:
        @pl.when(cond)
        def _(go=go):
            go.wait_send()


def body(nx, ny, depth, momentum, tracer, cell_wet, tile_wet):
    layers, rows, cols = depth.shape
    assert TILE % rows == 0 and TILE % cols == 0 and cols == 128 and rows * SEG == cols and layers == 16
    f32 = jnp.float32
    tall = rows + 2 * DEEP
    wide = 2 * cols
    half = layers // 2
    dma = pltpu.SemaphoreType.DMA
    vmem = pl.BlockSpec(memory_space=pltpu.VMEM)
    flat = jax.ShapeDtypeStruct((layers * rows, cols), f32)
    field = pltpu.VMEM((FIELDS, rows + 2 * REACH, layers, cols), f32)
    layer = pltpu.VMEM((tall, layers, wide), f32)
    flows = 2 * FIELDS
    strip = pltpu.VMEM((4, flows + 1, half, cols), f32)
    pairs = [dma((4, 2))] * 2 + [dma((2,))] * 2 + [dma((4, 2))] * 2 + [dma((2, 2))] * 4
    pairs += [dma] * 2
    new_depth, new_momentum, new_tracer = pl.pallas_call(
        functools.partial(kernel, nx, ny, rows, cols, layers),
        out_shape=(pltpu.VMEM((layers * rows, cols), f32), pltpu.VMEM((3, layers * rows, cols), f32), pltpu.VMEM((layers * rows, cols), f32)),
        in_specs=[pl.BlockSpec(memory_space=pltpu.HBM)] * 5,
        out_specs=(vmem, vmem, vmem),
        scratch_shapes=[
            pltpu.VMEM((5, layers * rows, cols), f32),
            pltpu.VMEM((rows, cols), jnp.int32),
            pltpu.SMEM(tile_wet.shape, jnp.int32),
            dma((5,)),
            pltpu.VMEM((3, 3, rows, layers, cols), f32),
            field, field, field,
            pltpu.VMEM((FIELDS, tall, layers, wide), f32),
            pltpu.VMEM((tall, 1, wide), f32),
            pltpu.VMEM((rows + 1, half, cols), f32),
            pltpu.VMEM((rows, half, cols), f32),
            pltpu.VMEM((2, half, cols), f32),
            strip, strip, strip,
            pltpu.VMEM((2, 2, 8, half, cols), f32),
            pltpu.VMEM((2, 2, half, cols), f32),
            pltpu.VMEM((flows, half, cols), f32),
            layer, layer, layer, layer, layer, layer, layer,
            pltpu.VMEM((nx * ny, cols), f32),
            *pairs,
        ],
        compiler_params=pltpu.CompilerParams(
            collective_id=0, has_side_effects=True, vmem_limit_bytes=56 * 1024 * 1024
        ),
    )(
        tile_wet,
        depth.reshape(layers * rows, cols),
        momentum.reshape(3, layers * rows, cols),
        tracer.reshape(layers * rows, cols),
        cell_wet,
    )
    new_depth, new_momentum, new_tracer = pl.pallas_call(
        hand_on,
        out_shape=(flat, jax.ShapeDtypeStruct((3, layers * rows, cols), f32), flat),
        in_specs=[pl.BlockSpec(memory_space=pl.ANY)] * 3,
        out_specs=(pl.BlockSpec(memory_space=pl.ANY),) * 3,
        scratch_shapes=[dma((3,))],
        compiler_params=pltpu.CompilerParams(vmem_limit_bytes=8 * 1024 * 1024),
    )(new_depth, new_momentum, new_tracer)
    return (
        new_depth.reshape(depth.shape),
        new_momentum.reshape(momentum.shape),
        new_tracer.reshape(tracer.shape),
    )


def hand_on(a, b, c, x, y, z, sem):
    moves = [pltpu.make_async_copy(s, d, sem.at[k]) for k, (s, d) in enumerate(((a, x), (b, y), (c, z)))]
    for m in moves:
        m.start()
    for m in moves:
        m.wait()


def solution(mesh):
    placed = (
        P(None, "gx", "gy"),
        P(None, None, "gx", "gy"),
        P(None, "gx", "gy"),
        P("gx", "gy"),
        P(),
    )
    return jax.shard_map(
        functools.partial(body, mesh.shape["gx"], mesh.shape["gy"]),
        mesh=mesh,
        in_specs=placed,
        out_specs=(P(None, "gx", "gy"), P(None, None, "gx", "gy"), P(None, "gx", "gy")),
        check_vma=False,
    )
```

```python
import functools

import jax
import jax.numpy as jnp
from jax import lax
from jax.experimental import pallas as pl
from jax.experimental.pallas import tpu as pltpu
from jax.sharding import PartitionSpec as P

ITERS = 3
TILE = 128
REACH = 2
DEEP = 1 + ITERS
SEG = 2 * DEEP
FIELDS = 5

gravity = 9.81
time_step = 0.025
root = gravity**0.5
MESH = pl.DeviceIdType.MESH


def minmod(a, b):
    return jnp.maximum(jnp.minimum(a, jnp.maximum(b, 0.0)), jnp.minimum(b, 0.0))


def hll(left, right, weight, normal):
    hl, hr = left[0], right[0]
    rl, rr = lax.rsqrt(hl), lax.rsqrt(hr)
    ul, ur = left[normal] * (rl * rl), right[normal] * (rr * rr)
    al, ar = hl * rl, hr * rr
    lower = jnp.minimum(jnp.minimum(ul - al, ur - ar), 0.0)
    upper = jnp.maximum(jnp.maximum(ul + al, ur + ar), 0.0)
    scale = weight / (upper - lower)
    low, high = lower * scale, upper * scale
    take_left = high * (ul - lower)
    take_right = low * (upper - ur)
    flux = [take_left * l + take_right * r for l, r in zip(left, right)]
    flux[normal] = flux[normal] + 0.5 * (high * hl * hl - low * hr * hr)
    return flux


def lane_next(x):
    return pltpu.roll(x, x.shape[-1] - 1, 1)


def lane_prev(x):
    return pltpu.roll(x, 1, 1)


def halves(u):
    return [0.5 * x for x in u]


def minus(a, b):
    return [x - y for x, y in zip(a, b)]


def sides(u, before, after):
    s = [minmod(b, a) for b, a in zip(before, after)]
    return minus(u, s), [x + y for x, y in zip(u, s)]


def across_flux(u, v, weight):
    d = [lane_next(x) - x for x in v]
    right, left = sides(u, [lane_prev(x) for x in d], d)
    return hll(left, [lane_next(x) for x in right], weight, 2)


def strip_flux(u, weight):
    v = halves(u)
    v1 = [lane_next(x) for x in v]
    v2 = [pltpu.roll(x, x.shape[-1] - 2, 1) for x in v]
    d0, d1, d2 = minus(v, [lane_prev(x) for x in v]), minus(v1, v), minus(v2, v1)
    _, left = sides(u, d0, d1)
    right, _ = sides([x + x for x in v1], d1, d2)
    return hll(left, right, weight, 2)


def kernel(
    nx, ny, rows, cols, layers,
    tile_hbm, depth_hbm, mom_hbm, tracer_hbm, wet_hbm,
    depth_out, mom_out, tracer_out,
    staged, wet_ref, tile_ref, load_sem, pushes,
    fa, fb, fc, res, wet, wet_rows, wet_cols, wet_edge, packed, from_l, from_r, from_c, wet_c, change,
    ce, cn, up, inv, z0, z1, z2, wet_strip, patch, beyond, slopes, gather,
    send_row, recv_row, send_wet, recv_wet, send_col, recv_col,
    send_wc, recv_wc, send_cor, recv_cor, send_sum, recv_sum,
):
    R = DEEP
    H = REACH
    width = 2 * cols
    half = layers // 2
    flows = 2 * FIELDS
    gx, gy = lax.axis_index("gx"), lax.axis_index("gy")

    loads = [
        pltpu.make_async_copy(wet_hbm, wet_ref, load_sem.at[0]),
        pltpu.make_async_copy(tile_hbm, tile_ref, load_sem.at[4]),
        pltpu.make_async_copy(depth_hbm, staged.at[0], load_sem.at[1]),
        pltpu.make_async_copy(mom_hbm, staged.at[pl.ds(1, 3)], load_sem.at[2]),
        pltpu.make_async_copy(tracer_hbm, staged.at[4], load_sem.at[3]),
    ]

    barrier = pltpu.get_barrier_semaphore()
    has = {-1: gx > 0, 1: gx < nx - 1}
    side = {-1: gy > 0, 1: gy < ny - 1}
    near = [(a, b) for a in (1, nx - 1, 0) for b in (0, 1, ny - 1) if (a, b) != (0, 0)]
    peers = list(dict.fromkeys(near)) + [
        (a, b) for a in range(nx) for b in range(ny) if (a, b) not in near and (a, b) != (0, 0)]

    def peer(a, b):
        return (lax.rem(gx + a, nx), lax.rem(gy + b, ny))

    for n, (a, b) in enumerate(peers):
        pl.semaphore_signal(barrier, inc=1, device_id=peer(a, b), device_id_type=MESH)
        if n + 1 == len(near):
            for load in loads:
                load.start()

    f32 = jnp.float32
    for dx in (-1, 1):
        @pl.when(jnp.logical_not(has[dx]))
        def _(dx=dx):
            at = slice(0, H) if dx < 0 else slice(H + rows, rows + 2 * H)
            for x in (fa, fb, fc):
                x[0, at] = jnp.ones((H, layers, cols), f32)
                x[1:, at] = jnp.zeros((FIELDS - 1, H, layers, cols), f32)
            at = slice(0, R) if dx < 0 else slice(R + rows, rows + 2 * R)
            res[0, at, :, :cols] = jnp.ones((R, layers, cols), f32)
            res[1:4, at, :, :cols] = jnp.zeros((3, R, layers, cols), f32)
            wet[at, :, :cols] = jnp.zeros((R, 1, cols), f32)
    for dy, landing in ((-1, from_l), (1, from_r)):
        @pl.when(jnp.logical_not(side[dy]))
        def _(landing=landing):
            landing[:, :2] = jnp.ones((4, 2, half, cols), f32)
            landing[:, 2:] = jnp.zeros((4, flows - 1, half, cols), f32)
    for i, dx in enumerate((-1, 1)):
        for j, dy in enumerate((-1, 1)):
            @pl.when(jnp.logical_not(jnp.logical_and(has[dx], side[dy])))
            def _(i=i, j=j):
                from_c[i, j, :2] = jnp.ones((2, half, cols), f32)
                from_c[i, j, 2:] = jnp.zeros((6, half, cols), f32)
                wet_c[i, j] = jnp.zeros((half, cols), f32)

    def exchange(cond, src, dst, send, recv, back, device):
        args = dict(src_ref=src, dst_ref=dst, send_sem=send, device_id=device, device_id_type=MESH)
        return (cond, pltpu.make_async_remote_copy(recv_sem=recv, **args),
                pltpu.make_async_remote_copy(recv_sem=back, **args))

    started = []

    def begin(group):
        for cond, go, come in group:
            @pl.when(cond)
            def _(go=go):
                go.start()
        started.extend(group)

    def arrive(group):
        for cond, go, come in group:
            @pl.when(cond)
            def _(come=come):
                come.wait_recv()

    def row_copies(k, x, deep, part_of):
        group = []
        for i, dx in enumerate((-1, 1)):
            mine = deep if dx < 0 else rows
            theirs = deep + rows if dx < 0 else 0
            group.append(exchange(
                has[dx], part_of(x, mine), part_of(x, theirs),
                send_row.at[k, i], recv_row.at[k, i], recv_row.at[k, 1 - i], (gx + dx, gy)))
        return group

    def stage_rows(x, at):
        return x.at[:, pl.ds(at, H)]

    def result_rows(x, at):
        return x.at[pl.ds(0, 4), pl.ds(at, R), :, pl.ds(0, cols)]

    def column_copies(k, count):
        group = []
        for j, (dy, landing) in enumerate(((-1, from_r), (1, from_l))):
            group.append(exchange(
                side[dy], packed.at[k, pl.ds(0, count)], landing.at[k, pl.ds(0, count)],
                send_col.at[k, j], recv_col.at[k, j], recv_col.at[k, 1 - j], (gx, gy + dy)))
        return group

    def corner_copies(src, landing, send, recv):
        group = []
        for i, dx in enumerate((-1, 1)):
            for j, dy in enumerate((-1, 1)):
                group.append(exchange(
                    jnp.logical_and(has[dx], side[dy]), src, landing.at[1 - i, 1 - j],
                    send.at[i, j], recv.at[i, j], recv.at[1 - i, 1 - j], (gx + dx, gy + dy)))
        return group

    lane = lax.broadcasted_iota(jnp.int32, (half, cols), 1)
    seg = lane // SEG
    pos = lane % SEG
    own_right = pos < DEEP
    edge = jnp.logical_or(lane < H, lane >= cols - H)
    cuts = [slice(q * half, (q + 1) * half) for q in range(2)]

    def into(x, r, total):
        return jnp.where(seg == r, pltpu.roll(x, SEG * r + DEEP, 1), total)

    def out_of(x, r):
        return pltpu.roll(x, cols - DEEP - SEG * r, 1)

    for load in loads:
        load.wait()
    tile = tile_ref[(gx * rows) // TILE, (gy * cols) // TILE].astype(f32)
    for r in range(rows):
        wet[R + r, :, :cols] = wet_ref[r : r + 1, :].astype(f32) * tile

    def load_row(r, carry):
        at = pl.ds(r, layers, stride=rows)
        w = wet[R + r, :, :cols]
        carry = list(carry)
        for f in range(FIELDS):
            x = staged[f, at, :]
            if f == 0:
                x = x * w + (1.0 - w)
            elif f < 3:
                x = x * (1.0 / root)
            fa[f, H + r] = x
            for q in range(2):
                carry[2 * f + q] = into(x[cuts[q]], r, carry[2 * f + q])
        carry[flows] = into(jnp.broadcast_to(w, (half, cols)), r, carry[flows])
        return tuple(carry)

    blank = jnp.zeros((half, cols), f32)
    carry = (blank,) * (flows + 1)
    for lo, hi in ((0, H), (rows - H, rows)):
        carry = lax.fori_loop(lo, hi, load_row, carry, unroll=True)
    pl.semaphore_wait(barrier, len(peers))
    coming_rows = row_copies(0, fa, H, stage_rows)
    begin(coming_rows)
    wet_copies = []
    for i, dx in enumerate((-1, 1)):
        mine, theirs = (R, R + rows) if dx < 0 else (rows, 0)
        wet_copies.append(exchange(
            has[dx], wet.at[pl.ds(mine, R), :, pl.ds(0, cols)], wet.at[pl.ds(theirs, R), :, pl.ds(0, cols)],
            send_wet.at[i], recv_wet.at[i], recv_wet.at[1 - i], (gx + dx, gy)))
    begin(wet_copies)
    carry = lax.fori_loop(H, rows - H, load_row, carry, unroll=12)
    for n in range(flows + 1):
        packed[0, n] = carry[n]
    coming_cols = column_copies(0, flows + 1)
    begin(coming_cols)
    wet_corners = corner_copies(packed.at[0, flows], wet_c, send_wc, recv_wc)
    begin(wet_corners)

    inner = jnp.logical_and(lane >= 1, lane < cols - H)

    def column_weight(r, carry):
        w = jnp.broadcast_to(wet[R + r, :, :cols], (half, cols))
        wet_cols[r] = jnp.where(inner, (-time_step * root) * w * lane_next(w), 0.0)
        return carry

    def row_weight(r, carry):
        w = wet[R + r - 1, :, :cols] * wet[R + r, :, :cols]
        wet_rows[r] = jnp.broadcast_to((-time_step * root) * w, (half, cols))
        return carry

    lax.fori_loop(0, rows, column_weight, 0, unroll=4)
    lax.fori_loop(1, rows, row_weight, 0, unroll=5)

    def state(src, i, cut):
        return [src[f, i + H, cut, :] for f in range(FIELDS)]

    def blend(keep, i, cut, f, value):
        if keep is None:
            return value
        kept = fa[f, i + H, cut, :]
        if keep == 0.75:
            return 0.75 * kept + 0.25 * value
        return (1.0 / 3.0) * kept + (2.0 / 3.0) * value

    def sweep(src, dst, deep, keep):
        for cut in cuts:
            def store(i, rates, cut=cut):
                u = state(src, i, cut)
                across = across_flux(u, halves(u), wet_cols[i])
                for f in range(FIELDS):
                    rate = across[f] - lane_prev(across[f])
                    if rates is not None:
                        rate = rate + rates[f]
                    dst[f, i + deep, cut, :cols] = blend(keep, i, cut, f, u[f] + rate)

            def step(i, carry, cut=cut, store=store):
                flux_low, left, v1, d = carry
                v2 = halves(state(src, i + 2, cut))
                ahead = minus(v2, v1)
                right, following = sides(state(src, i + 1, cut), d, ahead)
                flux_high = hll(left, right, wet_rows[i + 1], 1)
                store(i, minus(flux_high, flux_low))
                return flux_high, following, v2, ahead

            a, b, c, e = [state(src, i, cut) for i in range(4)]
            va, vb, vc, ve = [halves(x) for x in (a, b, c, e)]
            dab, dbc, dce = minus(vb, va), minus(vc, vb), minus(ve, vc)
            _, left = sides(b, dab, dbc)
            right, following = sides(c, dbc, dce)
            flux = hll(left, right, wet_rows[H], 1)
            store(0, None)
            store(1, flux)
            flux, _, _, _ = lax.fori_loop(H, rows - H, step, (flux, following, ve, dce), unroll=6)
            store(rows - 2, [-x for x in flux])
            store(rows - 1, None)

    def ends(src, dst, deep, factor):
        for cut in cuts:
            for first in (-2, rows - 3):
                u = [state(src, first + n, cut) for n in range(5)]
                v = [halves(x) for x in u]
                d = [minus(y, x) for x, y in zip(v[:4], v[1:])]
                sided = [sides(u[n], d[n - 1], d[n]) for n in (1, 2, 3)]
                one = hll(sided[0][1], sided[1][0], wet_rows[first + 2], 1)
                two = hll(sided[1][1], sided[2][0], wet_rows[first + 3], 1)
                if first < 0:
                    changes = ((0, minus(two, one)), (1, [-x for x in two]))
                else:
                    changes = ((rows - 2, one), (rows - 1, minus(two, one)))
                for i, rates in changes:
                    for f in range(FIELDS):
                        rate = rates[f] if factor == 1.0 else factor * rates[f]
                        dst[f, i + deep, cut, :cols] = dst[f, i + deep, cut, :cols] + rate

    def edges(k, factor):
        for q in range(2):
            own = [packed[k, 2 * f + q] for f in range(FIELDS)]
            left = [jnp.where(own_right, from_l[k, 2 * f + q], own[f]) for f in range(FIELDS)]
            right = [jnp.where(own_right, own[f], from_r[k, 2 * f + q]) for f in range(FIELDS)]
            flux_l, flux_r = strip_flux(left, wet_edge[0]), strip_flux(right, wet_edge[1])
            for f in range(FIELDS):
                a, b = flux_r[f] - lane_prev(flux_r[f]), flux_l[f] - lane_prev(flux_l[f])
                t = jnp.where(own_right, a, b)
                change[2 * f + q] = t if factor == 1.0 else factor * t

    def pack(dst, deep, count):
        def row(r, carry):
            return tuple(
                into(dst[n // 2, r + deep, cuts[n % 2], :cols], r, carry[n]) for n in range(count))
        return row

    def mend(dst, deep, last):
        def row(r, carry):
            for f in range(FIELDS):
                for q in range(2):
                    x = dst[f, r + deep, cuts[q], :cols]
                    x = x + jnp.where(edge, out_of(change[2 * f + q], r), 0.0)
                    dst[f, r + deep, cuts[q], :cols] = x * root if last and f in (1, 2) else x
            return carry
        return row

    plan = ((fa, fb, H, None, 1.0), (fb, fc, H, 0.75, 0.25), (fc, res, R, 1.0 / 3.0, 2.0 / 3.0))
    for k, (src, dst, deep, keep, factor) in enumerate(plan):
        last = k == 2
        count = flows - 2 if last else flows
        sweep(src, dst, deep, keep)
        pack_row, mend_row = pack(dst, deep, count), mend(dst, deep, last)
        carry = lax.fori_loop(H, rows - H, pack_row, (blank,) * count, unroll=4)
        if k == 0:
            arrive(wet_copies)
            for r in (0, rows):
                row_weight(r, 0)
        arrive(coming_rows)
        ends(src, dst, deep, factor)
        arrive(coming_cols)
        if k == 0:
            own = packed[0, flows]
            for n, (w, first) in enumerate((
                    (jnp.where(own_right, from_l[0, flows], own), DEEP - 1),
                    (jnp.where(own_right, own, from_r[0, flows]), DEEP - 2))):
                used = jnp.logical_or(pos == first, pos == first + 1)
                wet_edge[n] = jnp.where(used, (-time_step * root) * w * lane_next(w), 0.0)
        edges(k, factor)
        for lo, hi in ((0, H), (rows - H, rows)):
            carry = lax.fori_loop(lo, hi, pack_row, carry, unroll=True)
        for n in range(count):
            x = carry[n] + change[n]
            packed[k + 1, n] = x * root if last and n // 2 in (1, 2) else x
        for lo, hi in ((0, deep), (rows - deep, rows)):
            lax.fori_loop(lo, hi, mend_row, 0, unroll=True)
        coming_cols = column_copies(k + 1, count)
        begin(coming_cols)
        coming_rows = row_copies(k + 1, dst, deep, result_rows if last else stage_rows)
        begin(coming_rows)
        lax.fori_loop(deep, rows - deep, mend_row, 0, unroll=4)
    coming_corners = corner_copies(packed.at[3, pl.ds(0, 8)], from_c, send_cor, recv_cor)
    begin(coming_corners)

    layer_id = lax.broadcasted_iota(jnp.int32, (layers, cols), 0)
    top = layer_id == layers - 1
    lane_all = lax.broadcasted_iota(jnp.int32, (layers, cols), 1)
    at_start, at_end = lane_all == 0, lane_all == cols - 1
    at_edge = jnp.logical_or(at_start, at_end)

    def above(x):
        return pltpu.roll(x, layers - 1, 0)

    def below(x):
        return pltpu.roll(x, 1, 0)

    def upward_of(h, w, top):
        return jnp.where(w > 0.0, 2.0 / jnp.where(top, h, h + above(h)), 0.0)

    def high_of(r):
        return 0.5 * (res[0, r] + res[0, r + 1]) * (wet[r] * wet[r + 1])

    def prepare(r):
        h, w = res[0, r], jnp.broadcast_to(wet[r], (layers, cols))
        high = high_of(r)
        across = 0.5 * (h + lane_next(h)) * (w * lane_next(w))
        upward = upward_of(h, w, top)
        inner = jnp.where(top, 0.0, upward)
        diagonal = 0.5 * h + ce[r - 1] + high + lane_prev(across) + across + below(inner) + upward
        v = res[3, r]
        y = res[2, r]
        div = (
            0.5 * (res[1, r + 1] - res[1, r - 1])
            + 0.5 * (lane_next(y) - lane_prev(y))
            + (v - jnp.where(layer_id == 0, 0.0, below(v)))
        )
        ce[r] = high
        cn[r] = across
        up[r] = upward
        inv[r] = jnp.where(diagonal == 0.0, 0.0, 1.0 / diagonal)
        z0[r] = -div * w

    def prepare_loop(r, carry):
        prepare(r)
        return carry

    ce[R] = high_of(R)
    lax.fori_loop(R + 1, R + rows - 1, prepare_loop, 0, unroll=7)

    def wide_of(main, halo):
        return jnp.concatenate([main, halo], axis=1)

    def halo_pack(x):
        total = blank
        for n in range(R):
            total = into(x(R + rows + n), n, total)
            total = into(x(n), rows - R + n, total)
        return total

    lower_rows = seg < rows // 2

    def strips_of(l, own, r, halo, corner):
        far_l = jnp.where(lower_rows, corner(1, 0), corner(0, 0))
        far_r = jnp.where(lower_rows, corner(1, 1), corner(0, 1))
        return (
            wide_of(jnp.where(own_right, l, own), jnp.where(own_right, far_l, halo)),
            wide_of(jnp.where(own_right, own, r), jnp.where(own_right, halo, far_r)))

    arrive(wet_corners)
    wet_halo = halo_pack(lambda r: jnp.broadcast_to(wet[r], (half, cols)))
    for n, w in enumerate(strips_of(
            from_l[0, flows], packed[0, flows], from_r[0, flows], wet_halo, lambda i, j: wet_c[i, j])):
        wet_strip[n] = w

    arrive(coming_cols)
    arrive(coming_corners)
    arrive(coming_rows)

    fields = []
    for f in range(4):
        parts = []
        for q in range(2):
            n = 2 * f + q
            parts.append(strips_of(
                from_l[3, n], packed[3, n], from_r[3, n],
                halo_pack(lambda r: res[f, r, cuts[q], :]), lambda i, j: from_c[i, j, n]))
        fields.append([jnp.concatenate([parts[0][n], parts[1][n]], axis=0) for n in range(2)])

    wide_layer = lax.broadcasted_iota(jnp.int32, (layers, width), 0)
    wide_top = wide_layer == layers - 1
    wide_pos = lax.broadcasted_iota(jnp.int32, (layers, width), 1) % SEG < DEEP

    def row_next(x):
        return pltpu.roll(x, width - SEG, 1)

    def row_prev(x):
        return pltpu.roll(x, SEG, 1)

    systems = []
    for n in range(2):
        h, x, y, v = [fields[f][n] for f in range(4)]
        w = jnp.concatenate([wet_strip[n], wet_strip[n]], axis=0)
        high = 0.5 * (h + row_next(h)) * (w * row_next(w))
        low = row_prev(high)
        across = 0.5 * (h + lane_next(h)) * (w * lane_next(w))
        back = lane_prev(across)
        upward = upward_of(h, w, wide_top)
        inner = jnp.where(wide_top, 0.0, upward)
        diagonal = 0.5 * h + low + high + back + across + below(inner) + upward
        inverse = jnp.where(diagonal == 0.0, 0.0, 1.0 / diagonal)
        div = (
            0.5 * (row_next(x) - row_prev(x))
            + 0.5 * (lane_next(y) - lane_prev(y))
            + (v - jnp.where(wide_layer == 0, 0.0, below(v)))
        )
        force = -div * w
        z = force * inverse
        levels = [z]
        for _ in range(2):
            z = inverse * (
                low * row_prev(z) + high * row_next(z) + across * lane_next(z) + back * lane_prev(z)
                + inner * above(z) + below(inner * z))
            levels.append(z)
        systems.append((across, inverse, force, levels))
    left, right = systems
    for n in range(3):
        patch[n] = jnp.where(wide_pos, right[n], left[n])
    for k in range(3):
        zl, zr = left[3][k], right[3][k]
        beyond[k] = jnp.where(wide_pos, left[0] * zl, zr)
        slopes[k] = jnp.where(wide_pos, left[0] * (lane_next(zl) - zl), zr)

    def seen(strip, k, r, page):
        shift = {0: R, 1: R + rows, -1: R - rows}[page]
        lanes = slice(0, cols) if page == 0 else slice(cols, width)
        return out_of(strip[k, :, lanes], r - shift)

    def complete(r, page):
        cn[r] = jnp.where(at_edge, seen(patch, 0, r, page), cn[r])
        inverse = jnp.where(at_edge, seen(patch, 1, r, page), inv[r])
        force = jnp.where(at_edge, seen(patch, 2, r, page), z0[r])
        z = force * inverse
        inv[r] = inverse
        z0[r] = z
        return force * z

    def fold(x):
        return x[:half] + x[half:]

    first = R - ITERS
    ce[first - 1] = high_of(first - 1)
    for r in (*range(first, R + 1), *range(R + rows - 1, R + rows + ITERS)):
        prepare(r)
    for r in range(first, R):
        complete(r, -1)
        complete(r + ITERS + rows, 1)
    m0 = lax.fori_loop(R, R + rows, lambda r, acc: acc + fold(complete(r, 0)), blank, unroll=16)

    def next_in(x, edges_of):
        return lane_next(jnp.where(at_start, edges_of, x))

    def prev_in(x, edges_of):
        return lane_prev(jnp.where(at_end, edges_of, x))

    def spread(k, z, r, page):
        x = z[r]
        c = cn[r]
        u = jnp.where(top, 0.0, up[r])
        out = seen(beyond, k, r, page)
        return (
            ce[r - 1] * z[r - 1] + ce[r] * z[r + 1]
            + c * next_in(x, out) + prev_in(c * x, out)
            + u * above(x) + below(u * x)
        )

    def advance(k, z, target, reach):
        def inner(r, carry):
            odd, even = carry
            n = spread(k, z, r, 0)
            y = n * inv[r]
            target[r] = y
            return odd + fold(z[r] * n), even + fold(y * n)

        for r in range(reach):
            target[R - 1 - r] = spread(k, z, R - 1 - r, -1) * inv[R - 1 - r]
            target[R + rows + r] = spread(k, z, R + rows + r, 1) * inv[R + rows + r]
        return lax.fori_loop(R, R + rows, inner, (blank, blank), unroll=16)

    m1, m2 = advance(0, z0, z1, 2)
    m3, m4 = advance(1, z1, z2, 1)
    m5 = lax.fori_loop(
        R, R + rows, lambda r, acc: acc + fold(z2[r] * spread(2, z2, r, 0)), blank, unroll=16)

    row_id = lax.broadcasted_iota(jnp.int32, (8, cols), 0)
    lane_id = lax.broadcasted_iota(jnp.int32, (8, cols), 1)
    diagonal_at = row_id == lane_id
    table = blank
    for k, x in enumerate((m0, m1, m2, m3, m4, m5)):
        table = jnp.where(row_id == k, jnp.sum(x, axis=0, keepdims=True), table)
    table = jnp.where(diagonal_at, jnp.sum(table, axis=1, keepdims=True), 0.0)
    own = len(peers)
    gather[own : own + 1, :] = jnp.sum(table, axis=0, keepdims=True)
    for n, (a, b) in enumerate(reversed(peers)):
        pltpu.make_async_remote_copy(
            src_ref=gather.at[pl.ds(own, 1)], dst_ref=gather.at[pl.ds(n, 1)], send_sem=send_sum, recv_sem=recv_sum,
            device_id=peer(a, b), device_id_type=MESH).start()

    def push_of(k, z):
        def row(r, carry):
            q, c = z[r], cn[r]
            east = 0.5 * (ce[r] * (z[r + 1] - q) + ce[r - 1] * (q - z[r - 1]))
            out = seen(slopes, k, r, 0)
            slope = c * (next_in(q, out) - q)
            north = 0.5 * (slope + prev_in(slope, out))
            upward = up[r] * (jnp.where(top, 0.0, above(q)) - q)
            for n, push in enumerate((east, north, upward)):
                pushes[k, n, r - R] = push
            return carry

        lax.fori_loop(R, R + rows, row, 0, unroll=4)

    def plain_out(r, carry):
        at = pl.ds(r - R, layers, stride=rows)
        depth_out[at, :] = jnp.where(jnp.broadcast_to(wet[r, :, :cols], (layers, cols)) > 0.0, res[0, r, :, :cols], staged[0, at, :])
        tracer_out[at, :] = res[4, r, :, :cols]
        return carry

    push_of(0, z0)
    push_of(1, z1)
    push_of(2, z2)
    lax.fori_loop(R, R + rows, plain_out, 0, unroll=4)
    all_sums = pltpu.make_async_remote_copy(
        src_ref=gather.at[pl.ds(0, own)], dst_ref=gather.at[pl.ds(0, own)], send_sem=send_sum, recv_sem=recv_sum,
        device_id=peer(1, 0), device_id_type=MESH)
    all_sums.wait_recv()
    table = jnp.sum(gather[...], axis=0, keepdims=True)
    table = jnp.where(diagonal_at, table, 0.0)
    sums = jnp.broadcast_to(jnp.sum(table, axis=1, keepdims=True), (8, cols))
    m = [sums[k : k + 1, :] for k in range(6)]

    def dots(a, b, table):
        out = None
        for i in range(3):
            for j in range(3):
                if a[i] is not None and b[j] is not None:
                    t = a[i] * b[j] * table[i + j]
                    out = t if out is None else out + t
        return out

    shifted = [m[k] - m[k + 1] for k in range(5)]

    def plus(a, b, f):
        out = []
        for x, y in zip(a, b):
            out.append(x if y is None else (f * y if x is None else x + f * y))
        return out

    def image(d):
        moved = [None, d[0], d[1]]
        return [x if y is None else (None if x is None and y is None else (-y if x is None else x - y)) for x, y in zip(d, moved)]

    one = jnp.ones_like(m[0])
    direction = [one, None, None]
    residual = [one, None, None]
    pressure = [None, None, None]
    energy = m[0]
    for sweep in range(ITERS):
        bottom = dots(direction, direction, shifted)
        size = energy / bottom
        pressure = plus(pressure, direction, size)
        if sweep + 1 < ITERS:
            residual = plus(residual, image(direction), -size)
            fresh = dots(residual, residual, m)
            direction = plus(residual, direction, fresh / energy)
            energy = fresh

    def correct(r, carry):
        at = pl.ds(r - R, layers, stride=rows)
        for n in range(3):
            push = pressure[0] * pushes[0, n, r - R]
            push = push + pressure[1] * pushes[1, n, r - R] + pressure[2] * pushes[2, n, r - R]
            mom_out[n, at, :] = res[1 + n, r, :, :cols] - push
        return carry

    lax.fori_loop(R, R + rows, correct, 0, unroll=4)
    all_sums.wait_send()
    for cond, go, come in started:
        @pl.when(cond)
        def _(go=go):
            go.wait_send()


def body(nx, ny, depth, momentum, tracer, cell_wet, tile_wet):
    layers, rows, cols = depth.shape
    assert TILE % rows == 0 and TILE % cols == 0 and cols == 128 and rows * SEG == cols and layers == 16
    f32 = jnp.float32
    tall = rows + 2 * DEEP
    wide = 2 * cols
    half = layers // 2
    dma = pltpu.SemaphoreType.DMA
    vmem = pl.BlockSpec(memory_space=pltpu.VMEM)
    flat = jax.ShapeDtypeStruct((layers * rows, cols), f32)
    field = pltpu.VMEM((FIELDS, rows + 2 * REACH, layers, cols), f32)
    layer = pltpu.VMEM((tall, layers, cols), f32)
    three = pltpu.VMEM((3, layers, wide), f32)
    flows = 2 * FIELDS
    strip = pltpu.VMEM((4, flows + 1, half, cols), f32)
    pairs = [dma((4, 2))] * 2 + [dma((2,))] * 2 + [dma((4, 2))] * 2 + [dma((2, 2))] * 4
    pairs += [dma] * 2
    new_depth, new_momentum, new_tracer = pl.pallas_call(
        functools.partial(kernel, nx, ny, rows, cols, layers),
        out_shape=(pltpu.VMEM((layers * rows, cols), f32), pltpu.VMEM((3, layers * rows, cols), f32), pltpu.VMEM((layers * rows, cols), f32)),
        in_specs=[pl.BlockSpec(memory_space=pltpu.HBM)] * 5,
        out_specs=(vmem, vmem, vmem),
        scratch_shapes=[
            pltpu.VMEM((5, layers * rows, cols), f32),
            pltpu.VMEM((rows, cols), jnp.int32),
            pltpu.SMEM(tile_wet.shape, jnp.int32),
            dma((5,)),
            pltpu.VMEM((3, 3, rows, layers, cols), f32),
            field, field, field,
            pltpu.VMEM((FIELDS, tall, layers, cols), f32),
            pltpu.VMEM((tall, 1, cols), f32),
            pltpu.VMEM((rows + 1, half, cols), f32),
            pltpu.VMEM((rows, half, cols), f32),
            pltpu.VMEM((2, half, cols), f32),
            strip, strip, strip,
            pltpu.VMEM((2, 2, 8, half, cols), f32),
            pltpu.VMEM((2, 2, half, cols), f32),
            pltpu.VMEM((flows, half, cols), f32),
            layer, layer, layer, layer, layer, layer, layer,
            pltpu.VMEM((2, half, wide), f32),
            three, three, three,
            pltpu.VMEM((nx * ny, cols), f32),
            *pairs,
        ],
        compiler_params=pltpu.CompilerParams(
            collective_id=0, has_side_effects=True, vmem_limit_bytes=56 * 1024 * 1024
        ),
    )(
        tile_wet,
        depth.reshape(layers * rows, cols),
        momentum.reshape(3, layers * rows, cols),
        tracer.reshape(layers * rows, cols),
        cell_wet,
    )
    new_depth, new_momentum, new_tracer = pl.pallas_call(
        hand_on,
        out_shape=(flat, jax.ShapeDtypeStruct((3, layers * rows, cols), f32), flat),
        in_specs=[pl.BlockSpec(memory_space=pl.ANY)] * 3,
        out_specs=(pl.BlockSpec(memory_space=pl.ANY),) * 3,
        scratch_shapes=[dma((3,))],
        compiler_params=pltpu.CompilerParams(vmem_limit_bytes=8 * 1024 * 1024),
    )(new_depth, new_momentum, new_tracer)
    return (
        new_depth.reshape(depth.shape),
        new_momentum.reshape(momentum.shape),
        new_tracer.reshape(tracer.shape),
    )


def hand_on(a, b, c, x, y, z, sem):
    moves = [pltpu.make_async_copy(s, d, sem.at[k]) for k, (s, d) in enumerate(((a, x), (b, y), (c, z)))]
    for m in moves:
        m.start()
    for m in moves:
        m.wait()


def solution(mesh):
    placed = (
        P(None, "gx", "gy"),
        P(None, None, "gx", "gy"),
        P(None, "gx", "gy"),
        P("gx", "gy"),
        P(),
    )
    return jax.shard_map(
        functools.partial(body, mesh.shape["gx"], mesh.shape["gy"]),
        mesh=mesh,
        in_specs=placed,
        out_specs=(P(None, "gx", "gy"), P(None, None, "gx", "gy"), P(None, "gx", "gy")),
        check_vma=False,
    )
```

```python
import functools

import jax
import jax.numpy as jnp
from jax import lax
from jax.experimental import pallas as pl
from jax.experimental.pallas import tpu as pltpu
from jax.sharding import PartitionSpec as P

ITERS = 3
TILE = 128
REACH = 2
DEEP = 1 + ITERS
SEG = 2 * DEEP
FIELDS = 5

gravity = 9.81
time_step = 0.025
root = gravity**0.5
MESH = pl.DeviceIdType.MESH


def minmod(a, b):
    return jnp.maximum(jnp.minimum(a, jnp.maximum(b, 0.0)), jnp.minimum(b, 0.0))


def hll(left, right, weight, normal):
    hl, hr = left[0], right[0]
    rl, rr = lax.rsqrt(hl), lax.rsqrt(hr)
    ul, ur = left[normal] * (rl * rl), right[normal] * (rr * rr)
    al, ar = hl * rl, hr * rr
    lower = jnp.minimum(jnp.minimum(ul - al, ur - ar), 0.0)
    upper = jnp.maximum(jnp.maximum(ul + al, ur + ar), 0.0)
    scale = weight / (upper - lower)
    low, high = lower * scale, upper * scale
    take_left = high * (ul - lower)
    take_right = low * (upper - ur)
    flux = [take_left * l + take_right * r for l, r in zip(left, right)]
    flux[normal] = flux[normal] + 0.5 * (high * hl * hl - low * hr * hr)
    return flux


def lane_next(x):
    return pltpu.roll(x, x.shape[-1] - 1, 1)


def lane_prev(x):
    return pltpu.roll(x, 1, 1)


def halves(u):
    return [0.5 * x for x in u]


def minus(a, b):
    return [x - y for x, y in zip(a, b)]


def sides(u, before, after):
    s = [minmod(b, a) for b, a in zip(before, after)]
    return minus(u, s), [x + y for x, y in zip(u, s)]


def across_flux(u, v, weight):
    d = [lane_next(x) - x for x in v]
    right, left = sides(u, [lane_prev(x) for x in d], d)
    return hll(left, [lane_next(x) for x in right], weight, 2)


def strip_flux(u, weight):
    v = halves(u)
    v1 = [lane_next(x) for x in v]
    v2 = [pltpu.roll(x, x.shape[-1] - 2, 1) for x in v]
    d0, d1, d2 = minus(v, [lane_prev(x) for x in v]), minus(v1, v), minus(v2, v1)
    _, left = sides(u, d0, d1)
    right, _ = sides([x + x for x in v1], d1, d2)
    return hll(left, right, weight, 2)


def kernel(
    nx, ny, rows, cols, layers,
    tile_hbm, depth_hbm, mom_hbm, tracer_hbm, wet_hbm,
    depth_out, mom_out, tracer_out,
    staged, wet_ref, tile_ref, load_sem, pushes,
    fa, fb, fc, res, wet, wet_rows, wet_cols, wet_edge, packed, from_l, from_r, from_c, wet_c, change,
    ce, cn, up, inv, z0, z1, z2, wet_strip, patch, beyond, slopes, gather,
    send_row, recv_row, send_wet, recv_wet, send_col, recv_col,
    send_wc, recv_wc, send_cor, recv_cor, send_sum, recv_sum,
):
    R = DEEP
    H = REACH
    width = 2 * cols
    half = layers // 2
    flows = 2 * FIELDS
    gx, gy = lax.axis_index("gx"), lax.axis_index("gy")

    loads = [
        pltpu.make_async_copy(wet_hbm, wet_ref, load_sem.at[0]),
        pltpu.make_async_copy(tile_hbm, tile_ref, load_sem.at[4]),
        pltpu.make_async_copy(depth_hbm, staged.at[0], load_sem.at[1]),
        pltpu.make_async_copy(mom_hbm, staged.at[pl.ds(1, 3)], load_sem.at[2]),
        pltpu.make_async_copy(tracer_hbm, staged.at[4], load_sem.at[3]),
    ]

    barrier = pltpu.get_barrier_semaphore()
    has = {-1: gx > 0, 1: gx < nx - 1}
    side = {-1: gy > 0, 1: gy < ny - 1}
    near = [(a, b) for a in (1, nx - 1, 0) for b in (0, 1, ny - 1) if (a, b) != (0, 0)]
    peers = list(dict.fromkeys(near)) + [
        (a, b) for a in range(nx) for b in range(ny) if (a, b) not in near and (a, b) != (0, 0)]

    def peer(a, b):
        return (lax.rem(gx + a, nx), lax.rem(gy + b, ny))

    for n, (a, b) in enumerate(peers):
        pl.semaphore_signal(barrier, inc=1, device_id=peer(a, b), device_id_type=MESH)
        if n + 1 == len(near):
            for load in loads:
                load.start()

    f32 = jnp.float32
    for dx in (-1, 1):
        @pl.when(jnp.logical_not(has[dx]))
        def _(dx=dx):
            at = slice(0, H) if dx < 0 else slice(H + rows, rows + 2 * H)
            for x in (fa, fb, fc):
                x[0, at] = jnp.ones((H, layers, cols), f32)
                x[1:, at] = jnp.zeros((FIELDS - 1, H, layers, cols), f32)
            at = slice(0, R) if dx < 0 else slice(R + rows, rows + 2 * R)
            res[0, at, :, :cols] = jnp.ones((R, layers, cols), f32)
            res[1:4, at, :, :cols] = jnp.zeros((3, R, layers, cols), f32)
            wet[at, :, :cols] = jnp.zeros((R, 1, cols), f32)
    for dy, landing in ((-1, from_l), (1, from_r)):
        @pl.when(jnp.logical_not(side[dy]))
        def _(landing=landing):
            landing[:, :2] = jnp.ones((4, 2, half, cols), f32)
            landing[:, 2:] = jnp.zeros((4, flows - 1, half, cols), f32)
    for i, dx in enumerate((-1, 1)):
        for j, dy in enumerate((-1, 1)):
            @pl.when(jnp.logical_not(jnp.logical_and(has[dx], side[dy])))
            def _(i=i, j=j):
                from_c[i, j, :2] = jnp.ones((2, half, cols), f32)
                from_c[i, j, 2:] = jnp.zeros((6, half, cols), f32)
                wet_c[i, j] = jnp.zeros((half, cols), f32)

    def exchange(cond, src, dst, send, recv, back, device):
        args = dict(src_ref=src, dst_ref=dst, send_sem=send, device_id=device, device_id_type=MESH)
        return (cond, pltpu.make_async_remote_copy(recv_sem=recv, **args),
                pltpu.make_async_remote_copy(recv_sem=back, **args))

    started = []

    def begin(group):
        for cond, go, come in group:
            @pl.when(cond)
            def _(go=go):
                go.start()
        started.extend(group)

    def arrive(group):
        for cond, go, come in group:
            @pl.when(cond)
            def _(come=come):
                come.wait_recv()

    def row_copies(k, x, deep, part_of):
        group = []
        for i, dx in enumerate((-1, 1)):
            mine = deep if dx < 0 else rows
            theirs = deep + rows if dx < 0 else 0
            group.append(exchange(
                has[dx], part_of(x, mine), part_of(x, theirs),
                send_row.at[k, i], recv_row.at[k, i], recv_row.at[k, 1 - i], (gx + dx, gy)))
        return group

    def stage_rows(x, at):
        return x.at[:, pl.ds(at, H)]

    def result_rows(x, at):
        return x.at[pl.ds(0, 4), pl.ds(at, R), :, pl.ds(0, cols)]

    def column_copies(k, count):
        group = []
        for j, (dy, landing) in enumerate(((-1, from_r), (1, from_l))):
            group.append(exchange(
                side[dy], packed.at[k, pl.ds(0, count)], landing.at[k, pl.ds(0, count)],
                send_col.at[k, j], recv_col.at[k, j], recv_col.at[k, 1 - j], (gx, gy + dy)))
        return group

    def corner_copies(src, landing, send, recv):
        group = []
        for i, dx in enumerate((-1, 1)):
            for j, dy in enumerate((-1, 1)):
                group.append(exchange(
                    jnp.logical_and(has[dx], side[dy]), src, landing.at[1 - i, 1 - j],
                    send.at[i, j], recv.at[i, j], recv.at[1 - i, 1 - j], (gx + dx, gy + dy)))
        return group

    lane = lax.broadcasted_iota(jnp.int32, (half, cols), 1)
    seg = lane // SEG
    pos = lane % SEG
    own_right = pos < DEEP
    edge = jnp.logical_or(lane < H, lane >= cols - H)
    cuts = [slice(q * half, (q + 1) * half) for q in range(2)]

    def into(x, r, total):
        return jnp.where(seg == r, pltpu.roll(x, SEG * r + DEEP, 1), total)

    def out_of(x, r):
        return pltpu.roll(x, cols - DEEP - SEG * r, 1)

    for load in loads:
        load.wait()
    tile = tile_ref[(gx * rows) // TILE, (gy * cols) // TILE].astype(f32)
    for r in range(rows):
        wet[R + r, :, :cols] = wet_ref[r : r + 1, :].astype(f32) * tile

    def load_row(r, carry):
        at = pl.ds(r, layers, stride=rows)
        w = wet[R + r, :, :cols]
        carry = list(carry)
        for f in range(FIELDS):
            x = staged[f, at, :]
            if f == 0:
                x = x * w + (1.0 - w)
            elif f < 3:
                x = x * (1.0 / root)
            fa[f, H + r] = x
            for q in range(2):
                carry[2 * f + q] = into(x[cuts[q]], r, carry[2 * f + q])
        carry[flows] = into(jnp.broadcast_to(w, (half, cols)), r, carry[flows])
        return tuple(carry)

    blank = jnp.zeros((half, cols), f32)
    carry = (blank,) * (flows + 1)
    for lo, hi in ((0, H), (rows - H, rows)):
        carry = lax.fori_loop(lo, hi, load_row, carry, unroll=True)
    pl.semaphore_wait(barrier, len(peers))
    coming_rows = row_copies(0, fa, H, stage_rows)
    begin(coming_rows)
    wet_copies = []
    for i, dx in enumerate((-1, 1)):
        mine, theirs = (R, R + rows) if dx < 0 else (rows, 0)
        wet_copies.append(exchange(
            has[dx], wet.at[pl.ds(mine, R), :, pl.ds(0, cols)], wet.at[pl.ds(theirs, R), :, pl.ds(0, cols)],
            send_wet.at[i], recv_wet.at[i], recv_wet.at[1 - i], (gx + dx, gy)))
    begin(wet_copies)
    carry = lax.fori_loop(H, rows - H, load_row, carry, unroll=12)
    for n in range(flows + 1):
        packed[0, n] = carry[n]
    coming_cols = column_copies(0, flows + 1)
    begin(coming_cols)
    wet_corners = corner_copies(packed.at[0, flows], wet_c, send_wc, recv_wc)
    begin(wet_corners)

    inner = jnp.logical_and(lane >= 1, lane < cols - H)

    def column_weight(r, carry):
        w = jnp.broadcast_to(wet[R + r, :, :cols], (half, cols))
        wet_cols[r] = jnp.where(inner, (-time_step * root) * w * lane_next(w), 0.0)
        return carry

    def row_weight(r, carry):
        w = wet[R + r - 1, :, :cols] * wet[R + r, :, :cols]
        wet_rows[r] = jnp.broadcast_to((-time_step * root) * w, (half, cols))
        return carry

    lax.fori_loop(0, rows, column_weight, 0, unroll=4)
    lax.fori_loop(1, rows, row_weight, 0, unroll=5)

    def state(src, i, cut):
        return [src[f, i + H, cut, :] for f in range(FIELDS)]

    def blend(keep, i, cut, f, value):
        if keep is None:
            return value
        kept = fa[f, i + H, cut, :]
        if keep == 0.75:
            return 0.75 * kept + 0.25 * value
        return (1.0 / 3.0) * kept + (2.0 / 3.0) * value

    def sweep(src, dst, deep, keep):
        for cut in cuts:
            def store(i, rates, cut=cut):
                u = state(src, i, cut)
                across = across_flux(u, halves(u), wet_cols[i])
                for f in range(FIELDS):
                    rate = across[f] - lane_prev(across[f])
                    if rates is not None:
                        rate = rate + rates[f]
                    dst[f, i + deep, cut, :cols] = blend(keep, i, cut, f, u[f] + rate)

            def step(i, carry, cut=cut, store=store):
                flux_low, left, v1, d = carry
                v2 = halves(state(src, i + 2, cut))
                ahead = minus(v2, v1)
                right, following = sides(state(src, i + 1, cut), d, ahead)
                flux_high = hll(left, right, wet_rows[i + 1], 1)
                store(i, minus(flux_high, flux_low))
                return flux_high, following, v2, ahead

            a, b, c, e = [state(src, i, cut) for i in range(4)]
            va, vb, vc, ve = [halves(x) for x in (a, b, c, e)]
            dab, dbc, dce = minus(vb, va), minus(vc, vb), minus(ve, vc)
            _, left = sides(b, dab, dbc)
            right, following = sides(c, dbc, dce)
            flux = hll(left, right, wet_rows[H], 1)
            store(0, None)
            store(1, flux)
            flux, _, _, _ = lax.fori_loop(H, rows - H, step, (flux, following, ve, dce), unroll=6)
            store(rows - 2, [-x for x in flux])
            store(rows - 1, None)

    def ends(src, dst, deep, factor):
        for cut in cuts:
            for first in (-2, rows - 3):
                u = [state(src, first + n, cut) for n in range(5)]
                v = [halves(x) for x in u]
                d = [minus(y, x) for x, y in zip(v[:4], v[1:])]
                sided = [sides(u[n], d[n - 1], d[n]) for n in (1, 2, 3)]
                one = hll(sided[0][1], sided[1][0], wet_rows[first + 2], 1)
                two = hll(sided[1][1], sided[2][0], wet_rows[first + 3], 1)
                if first < 0:
                    changes = ((0, minus(two, one)), (1, [-x for x in two]))
                else:
                    changes = ((rows - 2, one), (rows - 1, minus(two, one)))
                for i, rates in changes:
                    for f in range(FIELDS):
                        rate = rates[f] if factor == 1.0 else factor * rates[f]
                        dst[f, i + deep, cut, :cols] = dst[f, i + deep, cut, :cols] + rate

    def edges(k, factor):
        for q in range(2):
            own = [packed[k, 2 * f + q] for f in range(FIELDS)]
            left = [jnp.where(own_right, from_l[k, 2 * f + q], own[f]) for f in range(FIELDS)]
            right = [jnp.where(own_right, own[f], from_r[k, 2 * f + q]) for f in range(FIELDS)]
            flux_l, flux_r = strip_flux(left, wet_edge[0]), strip_flux(right, wet_edge[1])
            for f in range(FIELDS):
                a, b = flux_r[f] - lane_prev(flux_r[f]), flux_l[f] - lane_prev(flux_l[f])
                t = jnp.where(own_right, a, b)
                change[2 * f + q] = t if factor == 1.0 else factor * t

    def pack(dst, deep, count):
        def row(r, carry):
            return tuple(
                into(dst[n // 2, r + deep, cuts[n % 2], :cols], r, carry[n]) for n in range(count))
        return row

    def mend(dst, deep, last):
        def row(r, carry):
            for f in range(FIELDS):
                for q in range(2):
                    x = dst[f, r + deep, cuts[q], :cols]
                    x = x + jnp.where(edge, out_of(change[2 * f + q], r), 0.0)
                    dst[f, r + deep, cuts[q], :cols] = x * root if last and f in (1, 2) else x
            return carry
        return row

    plan = ((fa, fb, H, None, 1.0), (fb, fc, H, 0.75, 0.25), (fc, res, R, 1.0 / 3.0, 2.0 / 3.0))
    for k, (src, dst, deep, keep, factor) in enumerate(plan):
        last = k == 2
        count = flows - 2 if last else flows
        sweep(src, dst, deep, keep)
        pack_row, mend_row = pack(dst, deep, count), mend(dst, deep, last)
        carry = lax.fori_loop(H, rows - H, pack_row, (blank,) * count, unroll=4)
        if k == 0:
            arrive(wet_copies)
            for r in (0, rows):
                row_weight(r, 0)
        arrive(coming_rows)
        arrive(coming_cols)
        ends(src, dst, deep, factor)
        if k == 0:
            own = packed[0, flows]
            for n, (w, first) in enumerate((
                    (jnp.where(own_right, from_l[0, flows], own), DEEP - 1),
                    (jnp.where(own_right, own, from_r[0, flows]), DEEP - 2))):
                used = jnp.logical_or(pos == first, pos == first + 1)
                wet_edge[n] = jnp.where(used, (-time_step * root) * w * lane_next(w), 0.0)
        edges(k, factor)
        for lo, hi in ((0, H), (rows - H, rows)):
            carry = lax.fori_loop(lo, hi, pack_row, carry, unroll=True)
        for n in range(count):
            x = carry[n] + change[n]
            packed[k + 1, n] = x * root if last and n // 2 in (1, 2) else x
        for lo, hi in ((0, deep), (rows - deep, rows)):
            lax.fori_loop(lo, hi, mend_row, 0, unroll=True)
        coming_cols = column_copies(k + 1, count)
        begin(coming_cols)
        coming_rows = row_copies(k + 1, dst, deep, result_rows if last else stage_rows)
        begin(coming_rows)
        lax.fori_loop(deep, rows - deep, mend_row, 0, unroll=4)
    coming_corners = corner_copies(packed.at[3, pl.ds(0, 8)], from_c, send_cor, recv_cor)
    begin(coming_corners)

    layer_id = lax.broadcasted_iota(jnp.int32, (layers, cols), 0)
    top = layer_id == layers - 1
    lane_all = lax.broadcasted_iota(jnp.int32, (layers, cols), 1)
    at_start, at_end = lane_all == 0, lane_all == cols - 1
    at_edge = jnp.logical_or(at_start, at_end)

    def above(x):
        return pltpu.roll(x, layers - 1, 0)

    def below(x):
        return pltpu.roll(x, 1, 0)

    def upward_of(h, w, top):
        return jnp.where(w > 0.0, 2.0 / jnp.where(top, h, h + above(h)), 0.0)

    def high_of(r):
        return 0.5 * (res[0, r] + res[0, r + 1]) * (wet[r] * wet[r + 1])

    def prepare(r):
        h, w = res[0, r], jnp.broadcast_to(wet[r], (layers, cols))
        high = high_of(r)
        across = 0.5 * (h + lane_next(h)) * (w * lane_next(w))
        upward = upward_of(h, w, top)
        inner = jnp.where(top, 0.0, upward)
        diagonal = 0.5 * h + ce[r - 1] + high + lane_prev(across) + across + below(inner) + upward
        v = res[3, r]
        y = res[2, r]
        div = (
            0.5 * (res[1, r + 1] - res[1, r - 1])
            + 0.5 * (lane_next(y) - lane_prev(y))
            + (v - jnp.where(layer_id == 0, 0.0, below(v)))
        )
        ce[r] = high
        cn[r] = across
        up[r] = upward
        inv[r] = jnp.where(diagonal == 0.0, 0.0, 1.0 / diagonal)
        z0[r] = -div * w

    def prepare_loop(r, carry):
        prepare(r)
        return carry

    ce[R] = high_of(R)
    lax.fori_loop(R + 1, R + rows - 1, prepare_loop, 0, unroll=7)

    def wide_of(main, halo):
        return jnp.concatenate([main, halo], axis=1)

    def halo_pack(x):
        total = blank
        for n in range(R):
            total = into(x(R + rows + n), n, total)
            total = into(x(n), rows - R + n, total)
        return total

    lower_rows = seg < rows // 2

    def strips_of(l, own, r, halo, corner):
        far_l = jnp.where(lower_rows, corner(1, 0), corner(0, 0))
        far_r = jnp.where(lower_rows, corner(1, 1), corner(0, 1))
        return (
            wide_of(jnp.where(own_right, l, own), jnp.where(own_right, far_l, halo)),
            wide_of(jnp.where(own_right, own, r), jnp.where(own_right, halo, far_r)))

    arrive(wet_corners)
    wet_halo = halo_pack(lambda r: jnp.broadcast_to(wet[r], (half, cols)))
    for n, w in enumerate(strips_of(
            from_l[0, flows], packed[0, flows], from_r[0, flows], wet_halo, lambda i, j: wet_c[i, j])):
        wet_strip[n] = w

    arrive(coming_cols)
    arrive(coming_corners)
    arrive(coming_rows)

    fields = []
    for f in range(4):
        parts = []
        for q in range(2):
            n = 2 * f + q
            parts.append(strips_of(
                from_l[3, n], packed[3, n], from_r[3, n],
                halo_pack(lambda r: res[f, r, cuts[q], :]), lambda i, j: from_c[i, j, n]))
        fields.append([jnp.concatenate([parts[0][n], parts[1][n]], axis=0) for n in range(2)])

    wide_layer = lax.broadcasted_iota(jnp.int32, (layers, width), 0)
    wide_top = wide_layer == layers - 1
    wide_pos = lax.broadcasted_iota(jnp.int32, (layers, width), 1) % SEG < DEEP

    def row_next(x):
        return pltpu.roll(x, width - SEG, 1)

    def row_prev(x):
        return pltpu.roll(x, SEG, 1)

    systems = []
    for n in range(2):
        h, x, y, v = [fields[f][n] for f in range(4)]
        w = jnp.concatenate([wet_strip[n], wet_strip[n]], axis=0)
        high = 0.5 * (h + row_next(h)) * (w * row_next(w))
        low = row_prev(high)
        across = 0.5 * (h + lane_next(h)) * (w * lane_next(w))
        back = lane_prev(across)
        upward = upward_of(h, w, wide_top)
        inner = jnp.where(wide_top, 0.0, upward)
        diagonal = 0.5 * h + low + high + back + across + below(inner) + upward
        inverse = jnp.where(diagonal == 0.0, 0.0, 1.0 / diagonal)
        div = (
            0.5 * (row_next(x) - row_prev(x))
            + 0.5 * (lane_next(y) - lane_prev(y))
            + (v - jnp.where(wide_layer == 0, 0.0, below(v)))
        )
        force = -div * w
        z = force * inverse
        levels = [z]
        for _ in range(2):
            z = inverse * (
                low * row_prev(z) + high * row_next(z) + across * lane_next(z) + back * lane_prev(z)
                + inner * above(z) + below(inner * z))
            levels.append(z)
        systems.append((across, inverse, force, levels))
    left, right = systems
    for n in range(3):
        patch[n] = jnp.where(wide_pos, right[n], left[n])
    for k in range(3):
        zl, zr = left[3][k], right[3][k]
        beyond[k] = jnp.where(wide_pos, left[0] * zl, zr)
        slopes[k] = jnp.where(wide_pos, left[0] * (lane_next(zl) - zl), zr)

    face_ends = jnp.zeros((layers, cols), f32)
    for across, _, _, levels in systems:
        z, c = levels[2][:, :cols], across[:, :cols]
        face_ends = face_ends + c * z * lane_next(z)
    face_ends = jnp.where(lane_all % SEG == DEEP - 1, face_ends, 0.0)

    def seen(strip, k, r, page):
        shift = {0: R, 1: R + rows, -1: R - rows}[page]
        lanes = slice(0, cols) if page == 0 else slice(cols, width)
        return out_of(strip[k, :, lanes], r - shift)

    def complete(r, page):
        cn[r] = jnp.where(at_edge, seen(patch, 0, r, page), cn[r])
        inverse = jnp.where(at_edge, seen(patch, 1, r, page), inv[r])
        force = jnp.where(at_edge, seen(patch, 2, r, page), z0[r])
        z = force * inverse
        inv[r] = inverse
        z0[r] = z
        return force * z

    def fold(x):
        return x[:half] + x[half:]

    first = R - ITERS
    ce[first - 1] = high_of(first - 1)
    for r in (*range(first, R + 1), *range(R + rows - 1, R + rows + ITERS)):
        prepare(r)
    for r in range(first, R):
        complete(r, -1)
        complete(r + ITERS + rows, 1)
    m0 = lax.fori_loop(R, R + rows, lambda r, acc: acc + fold(complete(r, 0)), blank, unroll=16)

    def next_in(x, edges_of):
        return lane_next(jnp.where(at_start, edges_of, x))

    def prev_in(x, edges_of):
        return lane_prev(jnp.where(at_end, edges_of, x))

    def spread(k, z, r, page):
        x = z[r]
        c = cn[r]
        u = jnp.where(top, 0.0, up[r])
        out = seen(beyond, k, r, page)
        return (
            ce[r - 1] * z[r - 1] + ce[r] * z[r + 1]
            + c * next_in(x, out) + prev_in(c * x, out)
            + u * above(x) + below(u * x)
        )

    def advance(k, z, target, reach):
        def inner(r, carry):
            odd, even = carry
            n = spread(k, z, r, 0)
            y = n * inv[r]
            target[r] = y
            return odd + fold(z[r] * n), even + fold(y * n)

        for r in range(reach):
            target[R - 1 - r] = spread(k, z, R - 1 - r, -1) * inv[R - 1 - r]
            target[R + rows + r] = spread(k, z, R + rows + r, 1) * inv[R + rows + r]
        return lax.fori_loop(R, R + rows, inner, (blank, blank), unroll=16)

    m1, m2 = advance(0, z0, z1, 2)
    m3, m4 = advance(1, z1, z2, 1)
    def faces(r, acc):
        x = z2[r]
        u = jnp.where(top, 0.0, up[r])
        t = ce[r] * z2[r + 1] + jnp.where(at_end, 0.0, cn[r]) * lane_next(x) + u * above(x)
        return acc + fold(x * t)

    m5 = lax.fori_loop(R, R + rows, faces, blank, unroll=16)
    beyond_low = ce[R - 1] * z2[R - 1] * z2[R]
    beyond_high = ce[R + rows - 1] * z2[R + rows - 1] * z2[R + rows]
    m5 = 2.0 * m5 + fold(beyond_low - beyond_high + face_ends)

    row_id = lax.broadcasted_iota(jnp.int32, (8, cols), 0)
    lane_id = lax.broadcasted_iota(jnp.int32, (8, cols), 1)
    diagonal_at = row_id == lane_id
    table = blank
    for k, x in enumerate((m0, m1, m2, m3, m4, m5)):
        table = jnp.where(row_id == k, jnp.sum(x, axis=0, keepdims=True), table)
    table = jnp.where(diagonal_at, jnp.sum(table, axis=1, keepdims=True), 0.0)
    own = len(peers)
    gather[own : own + 1, :] = jnp.sum(table, axis=0, keepdims=True)
    for n, (a, b) in enumerate(reversed(peers)):
        pltpu.make_async_remote_copy(
            src_ref=gather.at[pl.ds(own, 1)], dst_ref=gather.at[pl.ds(n, 1)], send_sem=send_sum, recv_sem=recv_sum,
            device_id=peer(a, b), device_id_type=MESH).start()

    def push_of(k, z):
        def row(r, carry):
            q, c = z[r], cn[r]
            east = 0.5 * (ce[r] * (z[r + 1] - q) + ce[r - 1] * (q - z[r - 1]))
            out = seen(slopes, k, r, 0)
            slope = c * (next_in(q, out) - q)
            north = 0.5 * (slope + prev_in(slope, out))
            upward = up[r] * (jnp.where(top, 0.0, above(q)) - q)
            for n, push in enumerate((east, north, upward)):
                pushes[k, n, r - R] = push
            return carry

        lax.fori_loop(R, R + rows, row, 0, unroll=4)

    def plain_out(r, carry):
        at = pl.ds(r - R, layers, stride=rows)
        depth_out[at, :] = jnp.where(jnp.broadcast_to(wet[r, :, :cols], (layers, cols)) > 0.0, res[0, r, :, :cols], staged[0, at, :])
        tracer_out[at, :] = res[4, r, :, :cols]
        return carry

    push_of(0, z0)
    push_of(1, z1)
    push_of(2, z2)
    lax.fori_loop(R, R + rows, plain_out, 0, unroll=4)
    all_sums = pltpu.make_async_remote_copy(
        src_ref=gather.at[pl.ds(0, own)], dst_ref=gather.at[pl.ds(0, own)], send_sem=send_sum, recv_sem=recv_sum,
        device_id=peer(1, 0), device_id_type=MESH)
    all_sums.wait_recv()
    table = jnp.sum(gather[...], axis=0, keepdims=True)
    table = jnp.where(diagonal_at, table, 0.0)
    sums = jnp.broadcast_to(jnp.sum(table, axis=1, keepdims=True), (8, cols))
    m = [sums[k : k + 1, :] for k in range(6)]

    def dots(a, b, table):
        out = None
        for i in range(3):
            for j in range(3):
                if a[i] is not None and b[j] is not None:
                    t = a[i] * b[j] * table[i + j]
                    out = t if out is None else out + t
        return out

    shifted = [m[k] - m[k + 1] for k in range(5)]

    def plus(a, b, f):
        out = []
        for x, y in zip(a, b):
            out.append(x if y is None else (f * y if x is None else x + f * y))
        return out

    def image(d):
        moved = [None, d[0], d[1]]
        return [x if y is None else (None if x is None and y is None else (-y if x is None else x - y)) for x, y in zip(d, moved)]

    one = jnp.ones_like(m[0])
    direction = [one, None, None]
    residual = [one, None, None]
    pressure = [None, None, None]
    energy = m[0]
    for sweep in range(ITERS):
        bottom = dots(direction, direction, shifted)
        size = energy / bottom
        pressure = plus(pressure, direction, size)
        if sweep + 1 < ITERS:
            residual = plus(residual, image(direction), -size)
            fresh = dots(residual, residual, m)
            direction = plus(residual, direction, fresh / energy)
            energy = fresh

    def correct(r, carry):
        at = pl.ds(r - R, layers, stride=rows)
        for n in range(3):
            push = pressure[0] * pushes[0, n, r - R]
            push = push + pressure[1] * pushes[1, n, r - R] + pressure[2] * pushes[2, n, r - R]
            mom_out[n, at, :] = res[1 + n, r, :, :cols] - push
        return carry

    lax.fori_loop(R, R + rows, correct, 0, unroll=4)
    all_sums.wait_send()
    for cond, go, come in started:
        @pl.when(cond)
        def _(go=go):
            go.wait_send()


def body(nx, ny, depth, momentum, tracer, cell_wet, tile_wet):
    layers, rows, cols = depth.shape
    assert TILE % rows == 0 and TILE % cols == 0 and cols == 128 and rows * SEG == cols and layers == 16
    f32 = jnp.float32
    tall = rows + 2 * DEEP
    wide = 2 * cols
    half = layers // 2
    dma = pltpu.SemaphoreType.DMA
    vmem = pl.BlockSpec(memory_space=pltpu.VMEM)
    flat = jax.ShapeDtypeStruct((layers * rows, cols), f32)
    field = pltpu.VMEM((FIELDS, rows + 2 * REACH, layers, cols), f32)
    layer = pltpu.VMEM((tall, layers, cols), f32)
    three = pltpu.VMEM((3, layers, wide), f32)
    flows = 2 * FIELDS
    strip = pltpu.VMEM((4, flows + 1, half, cols), f32)
    pairs = [dma((4, 2))] * 2 + [dma((2,))] * 2 + [dma((4, 2))] * 2 + [dma((2, 2))] * 4
    pairs += [dma] * 2
    new_depth, new_momentum, new_tracer = pl.pallas_call(
        functools.partial(kernel, nx, ny, rows, cols, layers),
        out_shape=(pltpu.VMEM((layers * rows, cols), f32), pltpu.VMEM((3, layers * rows, cols), f32), pltpu.VMEM((layers * rows, cols), f32)),
        in_specs=[pl.BlockSpec(memory_space=pltpu.HBM)] * 5,
        out_specs=(vmem, vmem, vmem),
        scratch_shapes=[
            pltpu.VMEM((5, layers * rows, cols), f32),
            pltpu.VMEM((rows, cols), jnp.int32),
            pltpu.SMEM(tile_wet.shape, jnp.int32),
            dma((5,)),
            pltpu.VMEM((3, 3, rows, layers, cols), f32),
            field, field, field,
            pltpu.VMEM((FIELDS, tall, layers, cols), f32),
            pltpu.VMEM((tall, 1, cols), f32),
            pltpu.VMEM((rows + 1, half, cols), f32),
            pltpu.VMEM((rows, half, cols), f32),
            pltpu.VMEM((2, half, cols), f32),
            strip, strip, strip,
            pltpu.VMEM((2, 2, 8, half, cols), f32),
            pltpu.VMEM((2, 2, half, cols), f32),
            pltpu.VMEM((flows, half, cols), f32),
            layer, layer, layer, layer, layer, layer, layer,
            pltpu.VMEM((2, half, wide), f32),
            three, three, three,
            pltpu.VMEM((nx * ny, cols), f32),
            *pairs,
        ],
        compiler_params=pltpu.CompilerParams(
            collective_id=0, has_side_effects=True, vmem_limit_bytes=56 * 1024 * 1024
        ),
    )(
        tile_wet,
        depth.reshape(layers * rows, cols),
        momentum.reshape(3, layers * rows, cols),
        tracer.reshape(layers * rows, cols),
        cell_wet,
    )
    new_depth, new_momentum, new_tracer = pl.pallas_call(
        hand_on,
        out_shape=(flat, jax.ShapeDtypeStruct((3, layers * rows, cols), f32), flat),
        in_specs=[pl.BlockSpec(memory_space=pl.ANY)] * 3,
        out_specs=(pl.BlockSpec(memory_space=pl.ANY),) * 3,
        scratch_shapes=[dma((3,))],
        compiler_params=pltpu.CompilerParams(vmem_limit_bytes=8 * 1024 * 1024),
    )(new_depth, new_momentum, new_tracer)
    return (
        new_depth.reshape(depth.shape),
        new_momentum.reshape(momentum.shape),
        new_tracer.reshape(tracer.shape),
    )


def hand_on(a, b, c, x, y, z, sem):
    moves = [pltpu.make_async_copy(s, d, sem.at[k]) for k, (s, d) in enumerate(((a, x), (b, y), (c, z)))]
    for m in moves:
        m.start()
    for m in moves:
        m.wait()


def solution(mesh):
    placed = (
        P(None, "gx", "gy"),
        P(None, None, "gx", "gy"),
        P(None, "gx", "gy"),
        P("gx", "gy"),
        P(),
    )
    return jax.shard_map(
        functools.partial(body, mesh.shape["gx"], mesh.shape["gy"]),
        mesh=mesh,
        in_specs=placed,
        out_specs=(P(None, "gx", "gy"), P(None, None, "gx", "gy"), P(None, "gx", "gy")),
        check_vma=False,
    )
```

```python
import functools

import jax
import jax.numpy as jnp
from jax import lax
from jax.experimental import pallas as pl
from jax.experimental.pallas import tpu as pltpu
from jax.sharding import PartitionSpec as P

ITERS = 3
TILE = 128
REACH = 2
DEEP = 1 + ITERS
SEG = 2 * DEEP
FIELDS = 5

gravity = 9.81
time_step = 0.025
root = gravity**0.5
MESH = pl.DeviceIdType.MESH


def minmod(a, b):
    return jnp.maximum(jnp.minimum(a, jnp.maximum(b, 0.0)), jnp.minimum(b, 0.0))


def hll(left, right, weight, normal):
    hl, hr = left[0], right[0]
    rl, rr = lax.rsqrt(hl), lax.rsqrt(hr)
    ul, ur = left[normal] * (rl * rl), right[normal] * (rr * rr)
    al, ar = hl * rl, hr * rr
    lower = jnp.minimum(jnp.minimum(ul - al, ur - ar), 0.0)
    upper = jnp.maximum(jnp.maximum(ul + al, ur + ar), 0.0)
    scale = weight / (upper - lower)
    low, high = lower * scale, upper * scale
    take_left = high * (ul - lower)
    take_right = low * (upper - ur)
    flux = [take_left * l + take_right * r for l, r in zip(left, right)]
    flux[normal] = flux[normal] + 0.5 * (high * hl * hl - low * hr * hr)
    return flux


def lane_next(x):
    return pltpu.roll(x, x.shape[-1] - 1, 1)


def lane_prev(x):
    return pltpu.roll(x, 1, 1)


def halves(u):
    return [0.5 * x for x in u]


def minus(a, b):
    return [x - y for x, y in zip(a, b)]


def sides(u, before, after):
    s = [minmod(b, a) for b, a in zip(before, after)]
    return minus(u, s), [x + y for x, y in zip(u, s)]


def across_flux(u, v, weight):
    d = [lane_next(x) - x for x in v]
    right, left = sides(u, [lane_prev(x) for x in d], d)
    return hll(left, [lane_next(x) for x in right], weight, 2)


def strip_flux(u, weight):
    v = halves(u)
    v1 = [lane_next(x) for x in v]
    v2 = [pltpu.roll(x, x.shape[-1] - 2, 1) for x in v]
    d0, d1, d2 = minus(v, [lane_prev(x) for x in v]), minus(v1, v), minus(v2, v1)
    _, left = sides(u, d0, d1)
    right, _ = sides([x + x for x in v1], d1, d2)
    return hll(left, right, weight, 2)


def kernel(
    nx, ny, rows, cols, layers,
    tile_hbm, depth_hbm, mom_hbm, tracer_hbm, wet_hbm,
    depth_out, mom_out, tracer_out,
    staged, wet_ref, tile_ref, load_sem, pushes,
    fa, fb, fc, res, wet, wet_rows, wet_cols, wet_edge, packed, squeezed, from_l, from_r, from_c, wet_c, change,
    ce, cn, up, inv, z0, z1, z2, wet_strip, patch, beyond, slopes, gather,
    send_row, recv_row, send_wet, recv_wet, send_col, recv_col,
    send_wc, recv_wc, send_cor, recv_cor, send_sum, recv_sum,
):
    R = DEEP
    H = REACH
    width = 2 * cols
    half = layers // 2
    flows = 2 * FIELDS
    gx, gy = lax.axis_index("gx"), lax.axis_index("gy")

    loads = [
        pltpu.make_async_copy(wet_hbm, wet_ref, load_sem.at[0]),
        pltpu.make_async_copy(tile_hbm, tile_ref, load_sem.at[4]),
        pltpu.make_async_copy(depth_hbm, staged.at[0], load_sem.at[1]),
        pltpu.make_async_copy(mom_hbm, staged.at[pl.ds(1, 3)], load_sem.at[2]),
        pltpu.make_async_copy(tracer_hbm, staged.at[4], load_sem.at[3]),
    ]

    barrier = pltpu.get_barrier_semaphore()
    has = {-1: gx > 0, 1: gx < nx - 1}
    side = {-1: gy > 0, 1: gy < ny - 1}
    near = [(a, b) for a in (1, nx - 1, 0) for b in (0, 1, ny - 1) if (a, b) != (0, 0)]
    peers = list(dict.fromkeys(near)) + [
        (a, b) for a in range(nx) for b in range(ny) if (a, b) not in near and (a, b) != (0, 0)]

    def peer(a, b):
        return (lax.rem(gx + a, nx), lax.rem(gy + b, ny))

    for n, (a, b) in enumerate(peers):
        pl.semaphore_signal(barrier, inc=1, device_id=peer(a, b), device_id_type=MESH)
        if n + 1 == len(near):
            for load in loads:
                load.start()

    f32 = jnp.float32
    for dx in (-1, 1):
        @pl.when(jnp.logical_not(has[dx]))
        def _(dx=dx):
            at = slice(0, H) if dx < 0 else slice(H + rows, rows + 2 * H)
            for x in (fa, fb, fc):
                x[0, at] = jnp.ones((H, layers, cols), f32)
                x[1:, at] = jnp.zeros((FIELDS - 1, H, layers, cols), f32)
            at = slice(0, R) if dx < 0 else slice(R + rows, rows + 2 * R)
            res[0, at, :, :cols] = jnp.ones((R, layers, cols), f32)
            res[1:4, at, :, :cols] = jnp.zeros((3, R, layers, cols), f32)
            wet[at, :, :cols] = jnp.zeros((R, 1, cols), f32)
    for dy, landing in ((-1, from_l), (1, from_r)):
        @pl.when(jnp.logical_not(side[dy]))
        def _(landing=landing):
            landing[:3, :1] = jnp.ones((3, 1, half, cols), f32)
            landing[:3, 1:] = jnp.zeros((3, flows, half, cols), f32)
            landing[3, :2] = jnp.ones((2, half, cols), f32)
            landing[3, 2:] = jnp.zeros((flows - 1, half, cols), f32)
    for i, dx in enumerate((-1, 1)):
        for j, dy in enumerate((-1, 1)):
            @pl.when(jnp.logical_not(jnp.logical_and(has[dx], side[dy])))
            def _(i=i, j=j):
                from_c[i, j, :2] = jnp.ones((2, half, cols), f32)
                from_c[i, j, 2:] = jnp.zeros((6, half, cols), f32)
                wet_c[i, j] = jnp.zeros((half, cols), f32)

    def exchange(cond, src, dst, send, recv, back, device):
        args = dict(src_ref=src, dst_ref=dst, send_sem=send, device_id=device, device_id_type=MESH)
        return (cond, pltpu.make_async_remote_copy(recv_sem=recv, **args),
                pltpu.make_async_remote_copy(recv_sem=back, **args))

    started = []

    def begin(group):
        for cond, go, come in group:
            @pl.when(cond)
            def _(go=go):
                go.start()
        started.extend(group)

    def arrive(group):
        for cond, go, come in group:
            @pl.when(cond)
            def _(come=come):
                come.wait_recv()

    def row_copies(k, x, deep, part_of):
        group = []
        for i, dx in enumerate((-1, 1)):
            mine = deep if dx < 0 else rows
            theirs = deep + rows if dx < 0 else 0
            group.append(exchange(
                has[dx], part_of(x, mine), part_of(x, theirs),
                send_row.at[k, i], recv_row.at[k, i], recv_row.at[k, 1 - i], (gx + dx, gy)))
        return group

    def stage_rows(x, at):
        return x.at[:, pl.ds(at, H)]

    def result_rows(x, at):
        return x.at[pl.ds(0, 4), pl.ds(at, R), :, pl.ds(0, cols)]

    def column_copies(k, count):
        group = []
        source = packed.at[k, pl.ds(0, count)] if k == 3 else squeezed.at[k, pl.ds(0, count)]
        for j, (dy, landing) in enumerate(((-1, from_r), (1, from_l))):
            group.append(exchange(
                side[dy], source, landing.at[k, pl.ds(0, count)],
                send_col.at[k, j], recv_col.at[k, j], recv_col.at[k, 1 - j], (gx, gy + dy)))
        return group

    def corner_copies(src, landing, send, recv):
        group = []
        for i, dx in enumerate((-1, 1)):
            for j, dy in enumerate((-1, 1)):
                group.append(exchange(
                    jnp.logical_and(has[dx], side[dy]), src, landing.at[1 - i, 1 - j],
                    send.at[i, j], recv.at[i, j], recv.at[1 - i, 1 - j], (gx + dx, gy + dy)))
        return group

    lane = lax.broadcasted_iota(jnp.int32, (half, cols), 1)
    seg = lane // SEG
    pos = lane % SEG
    own_right = pos < DEEP
    edge = jnp.logical_or(lane < H, lane >= cols - H)
    cuts = [slice(q * half, (q + 1) * half) for q in range(2)]

    def into(x, r, total):
        return jnp.where(seg == r, pltpu.roll(x, SEG * r + DEEP, 1), total)

    def out_of(x, r):
        return pltpu.roll(x, cols - DEEP - SEG * r, 1)

    middle = jnp.logical_and(pos >= H, pos < DEEP + H)

    def squeeze(k, values):
        for f in range(FIELDS):
            squeezed[k, f] = jnp.where(middle, values[2 * f], pltpu.roll(values[2 * f + 1], DEEP, 1))

    def spread_out(x, q):
        return pltpu.roll(x, cols - DEEP, 1) if q else x

    for load in loads:
        load.wait()
    tile = tile_ref[(gx * rows) // TILE, (gy * cols) // TILE].astype(f32)
    for r in range(rows):
        wet[R + r, :, :cols] = wet_ref[r : r + 1, :].astype(f32) * tile

    def load_row(r, carry):
        at = pl.ds(r, layers, stride=rows)
        w = wet[R + r, :, :cols]
        carry = list(carry)
        for f in range(FIELDS):
            x = staged[f, at, :]
            if f == 0:
                x = x * w + (1.0 - w)
            elif f < 3:
                x = x * (1.0 / root)
            fa[f, H + r] = x
            for q in range(2):
                carry[2 * f + q] = into(x[cuts[q]], r, carry[2 * f + q])
        carry[flows] = into(jnp.broadcast_to(w, (half, cols)), r, carry[flows])
        return tuple(carry)

    blank = jnp.zeros((half, cols), f32)
    carry = (blank,) * (flows + 1)
    for lo, hi in ((0, H), (rows - H, rows)):
        carry = lax.fori_loop(lo, hi, load_row, carry, unroll=True)
    pl.semaphore_wait(barrier, len(peers))
    coming_rows = row_copies(0, fa, H, stage_rows)
    begin(coming_rows)
    wet_copies = []
    for i, dx in enumerate((-1, 1)):
        mine, theirs = (R, R + rows) if dx < 0 else (rows, 0)
        wet_copies.append(exchange(
            has[dx], wet.at[pl.ds(mine, R), :, pl.ds(0, cols)], wet.at[pl.ds(theirs, R), :, pl.ds(0, cols)],
            send_wet.at[i], recv_wet.at[i], recv_wet.at[1 - i], (gx + dx, gy)))
    begin(wet_copies)
    carry = lax.fori_loop(H, rows - H, load_row, carry, unroll=12)
    for n in range(flows + 1):
        packed[0, n] = carry[n]
    squeeze(0, carry)
    squeezed[0, FIELDS] = carry[flows]
    coming_cols = column_copies(0, FIELDS + 1)
    begin(coming_cols)
    wet_corners = corner_copies(packed.at[0, flows], wet_c, send_wc, recv_wc)
    begin(wet_corners)

    inner = jnp.logical_and(lane >= 1, lane < cols - H)

    def column_weight(r, carry):
        w = jnp.broadcast_to(wet[R + r, :, :cols], (half, cols))
        wet_cols[r] = jnp.where(inner, (-time_step * root) * w * lane_next(w), 0.0)
        return carry

    def row_weight(r, carry):
        w = wet[R + r - 1, :, :cols] * wet[R + r, :, :cols]
        wet_rows[r] = jnp.broadcast_to((-time_step * root) * w, (half, cols))
        return carry

    lax.fori_loop(0, rows, column_weight, 0, unroll=4)
    lax.fori_loop(1, rows, row_weight, 0, unroll=5)

    def state(src, i, cut):
        return [src[f, i + H, cut, :] for f in range(FIELDS)]

    def blend(keep, i, cut, f, value):
        if keep is None:
            return value
        kept = fa[f, i + H, cut, :]
        if keep == 0.75:
            return 0.75 * kept + 0.25 * value
        return (1.0 / 3.0) * kept + (2.0 / 3.0) * value

    def sweep(src, dst, deep, keep):
        for cut in cuts:
            def store(i, rates, cut=cut):
                u = state(src, i, cut)
                across = across_flux(u, halves(u), wet_cols[i])
                for f in range(FIELDS):
                    rate = across[f] - lane_prev(across[f])
                    if rates is not None:
                        rate = rate + rates[f]
                    dst[f, i + deep, cut, :cols] = blend(keep, i, cut, f, u[f] + rate)

            def step(i, carry, cut=cut, store=store):
                flux_low, left, v1, d = carry
                v2 = halves(state(src, i + 2, cut))
                ahead = minus(v2, v1)
                right, following = sides(state(src, i + 1, cut), d, ahead)
                flux_high = hll(left, right, wet_rows[i + 1], 1)
                store(i, minus(flux_high, flux_low))
                return flux_high, following, v2, ahead

            a, b, c, e = [state(src, i, cut) for i in range(4)]
            va, vb, vc, ve = [halves(x) for x in (a, b, c, e)]
            dab, dbc, dce = minus(vb, va), minus(vc, vb), minus(ve, vc)
            _, left = sides(b, dab, dbc)
            right, following = sides(c, dbc, dce)
            flux = hll(left, right, wet_rows[H], 1)
            store(0, None)
            store(1, flux)
            flux, _, _, _ = lax.fori_loop(H, rows - H, step, (flux, following, ve, dce), unroll=6)
            store(rows - 2, [-x for x in flux])
            store(rows - 1, None)

    def ends(src, dst, deep, factor):
        for cut in cuts:
            for first in (-2, rows - 3):
                u = [state(src, first + n, cut) for n in range(5)]
                v = [halves(x) for x in u]
                d = [minus(y, x) for x, y in zip(v[:4], v[1:])]
                sided = [sides(u[n], d[n - 1], d[n]) for n in (1, 2, 3)]
                one = hll(sided[0][1], sided[1][0], wet_rows[first + 2], 1)
                two = hll(sided[1][1], sided[2][0], wet_rows[first + 3], 1)
                if first < 0:
                    changes = ((0, minus(two, one)), (1, [-x for x in two]))
                else:
                    changes = ((rows - 2, one), (rows - 1, minus(two, one)))
                for i, rates in changes:
                    for f in range(FIELDS):
                        rate = rates[f] if factor == 1.0 else factor * rates[f]
                        dst[f, i + deep, cut, :cols] = dst[f, i + deep, cut, :cols] + rate

    def edges(k, factor):
        for q in range(2):
            own = [packed[k, 2 * f + q] for f in range(FIELDS)]
            left = [jnp.where(own_right, spread_out(from_l[k, f], q), own[f]) for f in range(FIELDS)]
            right = [jnp.where(own_right, own[f], spread_out(from_r[k, f], q)) for f in range(FIELDS)]
            flux_l, flux_r = strip_flux(left, wet_edge[0]), strip_flux(right, wet_edge[1])
            for f in range(FIELDS):
                a, b = flux_r[f] - lane_prev(flux_r[f]), flux_l[f] - lane_prev(flux_l[f])
                t = jnp.where(own_right, a, b)
                change[2 * f + q] = t if factor == 1.0 else factor * t

    def pack(dst, deep, count):
        def row(r, carry):
            return tuple(
                into(dst[n // 2, r + deep, cuts[n % 2], :cols], r, carry[n]) for n in range(count))
        return row

    def mend(dst, deep, last):
        def row(r, carry):
            for f in range(FIELDS):
                for q in range(2):
                    x = dst[f, r + deep, cuts[q], :cols]
                    x = x + jnp.where(edge, out_of(change[2 * f + q], r), 0.0)
                    dst[f, r + deep, cuts[q], :cols] = x * root if last and f in (1, 2) else x
            return carry
        return row

    plan = ((fa, fb, H, None, 1.0), (fb, fc, H, 0.75, 0.25), (fc, res, R, 1.0 / 3.0, 2.0 / 3.0))
    for k, (src, dst, deep, keep, factor) in enumerate(plan):
        last = k == 2
        count = flows - 2 if last else flows
        sweep(src, dst, deep, keep)
        pack_row, mend_row = pack(dst, deep, count), mend(dst, deep, last)
        carry = lax.fori_loop(H, rows - H, pack_row, (blank,) * count, unroll=4)
        if k == 0:
            arrive(wet_copies)
            for r in (0, rows):
                row_weight(r, 0)
        arrive(coming_rows)
        arrive(coming_cols)
        ends(src, dst, deep, factor)
        if k == 0:
            own = packed[0, flows]
            for n, (w, first) in enumerate((
                    (jnp.where(own_right, from_l[0, FIELDS], own), DEEP - 1),
                    (jnp.where(own_right, own, from_r[0, FIELDS]), DEEP - 2))):
                used = jnp.logical_or(pos == first, pos == first + 1)
                wet_edge[n] = jnp.where(used, (-time_step * root) * w * lane_next(w), 0.0)
        edges(k, factor)
        for lo, hi in ((0, H), (rows - H, rows)):
            carry = lax.fori_loop(lo, hi, pack_row, carry, unroll=True)
        ahead = [carry[n] + change[n] for n in range(count)]
        for n in range(count):
            packed[k + 1, n] = ahead[n] * root if last and n // 2 in (1, 2) else ahead[n]
        if not last:
            squeeze(k + 1, ahead)
        for lo, hi in ((0, deep), (rows - deep, rows)):
            lax.fori_loop(lo, hi, mend_row, 0, unroll=True)
        coming_cols = column_copies(k + 1, count if last else FIELDS)
        begin(coming_cols)
        coming_rows = row_copies(k + 1, dst, deep, result_rows if last else stage_rows)
        begin(coming_rows)
        lax.fori_loop(deep, rows - deep, mend_row, 0, unroll=4)
    coming_corners = corner_copies(packed.at[3, pl.ds(0, 8)], from_c, send_cor, recv_cor)
    begin(coming_corners)

    layer_id = lax.broadcasted_iota(jnp.int32, (layers, cols), 0)
    top = layer_id == layers - 1
    lane_all = lax.broadcasted_iota(jnp.int32, (layers, cols), 1)
    at_start, at_end = lane_all == 0, lane_all == cols - 1
    at_edge = jnp.logical_or(at_start, at_end)

    def above(x):
        return pltpu.roll(x, layers - 1, 0)

    def below(x):
        return pltpu.roll(x, 1, 0)

    def upward_of(h, w, top):
        return jnp.where(w > 0.0, 2.0 / jnp.where(top, h, h + above(h)), 0.0)

    def high_of(r):
        return 0.5 * (res[0, r] + res[0, r + 1]) * (wet[r] * wet[r + 1])

    def prepare(r):
        h, w = res[0, r], jnp.broadcast_to(wet[r], (layers, cols))
        high = high_of(r)
        across = 0.5 * (h + lane_next(h)) * (w * lane_next(w))
        upward = upward_of(h, w, top)
        inner = jnp.where(top, 0.0, upward)
        diagonal = 0.5 * h + ce[r - 1] + high + lane_prev(across) + across + below(inner) + upward
        v = res[3, r]
        y = res[2, r]
        div = (
            0.5 * (res[1, r + 1] - res[1, r - 1])
            + 0.5 * (lane_next(y) - lane_prev(y))
            + (v - jnp.where(layer_id == 0, 0.0, below(v)))
        )
        ce[r] = high
        cn[r] = across
        up[r] = upward
        inv[r] = jnp.where(diagonal == 0.0, 0.0, 1.0 / diagonal)
        z0[r] = -div * w

    def prepare_loop(r, carry):
        prepare(r)
        return carry

    ce[R] = high_of(R)
    lax.fori_loop(R + 1, R + rows - 1, prepare_loop, 0, unroll=7)

    def wide_of(main, halo):
        return jnp.concatenate([main, halo], axis=1)

    def halo_pack(x):
        total = blank
        for n in range(R):
            total = into(x(R + rows + n), n, total)
            total = into(x(n), rows - R + n, total)
        return total

    lower_rows = seg < rows // 2

    def strips_of(l, own, r, halo, corner):
        far_l = jnp.where(lower_rows, corner(1, 0), corner(0, 0))
        far_r = jnp.where(lower_rows, corner(1, 1), corner(0, 1))
        return (
            wide_of(jnp.where(own_right, l, own), jnp.where(own_right, far_l, halo)),
            wide_of(jnp.where(own_right, own, r), jnp.where(own_right, halo, far_r)))

    arrive(wet_corners)
    wet_halo = halo_pack(lambda r: jnp.broadcast_to(wet[r], (half, cols)))
    for n, w in enumerate(strips_of(
            from_l[0, FIELDS], packed[0, flows], from_r[0, FIELDS], wet_halo, lambda i, j: wet_c[i, j])):
        wet_strip[n] = w

    arrive(coming_cols)
    arrive(coming_corners)
    arrive(coming_rows)

    fields = []
    for f in range(4):
        parts = []
        for q in range(2):
            n = 2 * f + q
            parts.append(strips_of(
                from_l[3, n], packed[3, n], from_r[3, n],
                halo_pack(lambda r: res[f, r, cuts[q], :]), lambda i, j: from_c[i, j, n]))
        fields.append([jnp.concatenate([parts[0][n], parts[1][n]], axis=0) for n in range(2)])

    wide_layer = lax.broadcasted_iota(jnp.int32, (layers, width), 0)
    wide_top = wide_layer == layers - 1
    wide_pos = lax.broadcasted_iota(jnp.int32, (layers, width), 1) % SEG < DEEP

    def row_next(x):
        return pltpu.roll(x, width - SEG, 1)

    def row_prev(x):
        return pltpu.roll(x, SEG, 1)

    systems = []
    for n in range(2):
        h, x, y, v = [fields[f][n] for f in range(4)]
        w = jnp.concatenate([wet_strip[n], wet_strip[n]], axis=0)
        high = 0.5 * (h + row_next(h)) * (w * row_next(w))
        low = row_prev(high)
        across = 0.5 * (h + lane_next(h)) * (w * lane_next(w))
        back = lane_prev(across)
        upward = upward_of(h, w, wide_top)
        inner = jnp.where(wide_top, 0.0, upward)
        diagonal = 0.5 * h + low + high + back + across + below(inner) + upward
        inverse = jnp.where(diagonal == 0.0, 0.0, 1.0 / diagonal)
        div = (
            0.5 * (row_next(x) - row_prev(x))
            + 0.5 * (lane_next(y) - lane_prev(y))
            + (v - jnp.where(wide_layer == 0, 0.0, below(v)))
        )
        force = -div * w
        z = force * inverse
        levels = [z]
        for _ in range(2):
            z = inverse * (
                low * row_prev(z) + high * row_next(z) + across * lane_next(z) + back * lane_prev(z)
                + inner * above(z) + below(inner * z))
            levels.append(z)
        systems.append((across, inverse, force, levels))
    left, right = systems
    for n in range(3):
        patch[n] = jnp.where(wide_pos, right[n], left[n])
    for k in range(3):
        zl, zr = left[3][k], right[3][k]
        beyond[k] = jnp.where(wide_pos, left[0] * zl, zr)
        slopes[k] = jnp.where(wide_pos, left[0] * (lane_next(zl) - zl), zr)

    face_ends = jnp.zeros((layers, cols), f32)
    for across, _, _, levels in systems:
        z, c = levels[2][:, :cols], across[:, :cols]
        face_ends = face_ends + c * z * lane_next(z)
    face_ends = jnp.where(lane_all % SEG == DEEP - 1, face_ends, 0.0)

    def seen(strip, k, r, page):
        shift = {0: R, 1: R + rows, -1: R - rows}[page]
        lanes = slice(0, cols) if page == 0 else slice(cols, width)
        return out_of(strip[k, :, lanes], r - shift)

    def complete(r, page):
        cn[r] = jnp.where(at_edge, seen(patch, 0, r, page), cn[r])
        inverse = jnp.where(at_edge, seen(patch, 1, r, page), inv[r])
        force = jnp.where(at_edge, seen(patch, 2, r, page), z0[r])
        z = force * inverse
        inv[r] = inverse
        z0[r] = z
        return force * z

    def fold(x):
        return x[:half] + x[half:]

    first = R - ITERS
    ce[first - 1] = high_of(first - 1)
    for r in (*range(first, R + 1), *range(R + rows - 1, R + rows + ITERS)):
        prepare(r)
    for r in range(first, R):
        complete(r, -1)
        complete(r + ITERS + rows, 1)
    m0 = lax.fori_loop(R, R + rows, lambda r, acc: acc + fold(complete(r, 0)), blank, unroll=16)

    def next_in(x, edges_of):
        return lane_next(jnp.where(at_start, edges_of, x))

    def prev_in(x, edges_of):
        return lane_prev(jnp.where(at_end, edges_of, x))

    def spread(k, z, r, page):
        x = z[r]
        c = cn[r]
        u = jnp.where(top, 0.0, up[r])
        out = seen(beyond, k, r, page)
        return (
            ce[r - 1] * z[r - 1] + ce[r] * z[r + 1]
            + c * next_in(x, out) + prev_in(c * x, out)
            + u * above(x) + below(u * x)
        )

    def advance(k, z, target, reach):
        def inner(r, carry):
            odd, even = carry
            n = spread(k, z, r, 0)
            y = n * inv[r]
            target[r] = y
            return odd + fold(z[r] * n), even + fold(y * n)

        for r in range(reach):
            target[R - 1 - r] = spread(k, z, R - 1 - r, -1) * inv[R - 1 - r]
            target[R + rows + r] = spread(k, z, R + rows + r, 1) * inv[R + rows + r]
        return lax.fori_loop(R, R + rows, inner, (blank, blank), unroll=16)

    m1, m2 = advance(0, z0, z1, 2)
    m3, m4 = advance(1, z1, z2, 1)
    def faces(r, acc):
        x = z2[r]
        u = jnp.where(top, 0.0, up[r])
        t = ce[r] * z2[r + 1] + jnp.where(at_end, 0.0, cn[r]) * lane_next(x) + u * above(x)
        return acc + fold(x * t)

    m5 = lax.fori_loop(R, R + rows, faces, blank, unroll=16)
    beyond_low = ce[R - 1] * z2[R - 1] * z2[R]
    beyond_high = ce[R + rows - 1] * z2[R + rows - 1] * z2[R + rows]
    m5 = 2.0 * m5 + fold(beyond_low - beyond_high + face_ends)

    row_id = lax.broadcasted_iota(jnp.int32, (8, cols), 0)
    lane_id = lax.broadcasted_iota(jnp.int32, (8, cols), 1)
    diagonal_at = row_id == lane_id
    table = blank
    for k, x in enumerate((m0, m1, m2, m3, m4, m5)):
        table = jnp.where(row_id == k, jnp.sum(x, axis=0, keepdims=True), table)
    table = jnp.where(diagonal_at, jnp.sum(table, axis=1, keepdims=True), 0.0)
    own = len(peers)
    gather[own : own + 1, :] = jnp.sum(table, axis=0, keepdims=True)
    for n, (a, b) in enumerate(reversed(peers)):
        pltpu.make_async_remote_copy(
            src_ref=gather.at[pl.ds(own, 1)], dst_ref=gather.at[pl.ds(n, 1)], send_sem=send_sum, recv_sem=recv_sum,
            device_id=peer(a, b), device_id_type=MESH).start()

    def push_of(k, z):
        def row(r, carry):
            q, c = z[r], cn[r]
            east = 0.5 * (ce[r] * (z[r + 1] - q) + ce[r - 1] * (q - z[r - 1]))
            out = seen(slopes, k, r, 0)
            slope = c * (next_in(q, out) - q)
            north = 0.5 * (slope + prev_in(slope, out))
            upward = up[r] * (jnp.where(top, 0.0, above(q)) - q)
            for n, push in enumerate((east, north, upward)):
                pushes[k, n, r - R] = push
            return carry

        lax.fori_loop(R, R + rows, row, 0, unroll=4)

    def plain_out(r, carry):
        at = pl.ds(r - R, layers, stride=rows)
        depth_out[at, :] = jnp.where(jnp.broadcast_to(wet[r, :, :cols], (layers, cols)) > 0.0, res[0, r, :, :cols], staged[0, at, :])
        tracer_out[at, :] = res[4, r, :, :cols]
        return carry

    push_of(0, z0)
    push_of(1, z1)
    push_of(2, z2)
    lax.fori_loop(R, R + rows, plain_out, 0, unroll=4)
    all_sums = pltpu.make_async_remote_copy(
        src_ref=gather.at[pl.ds(0, own)], dst_ref=gather.at[pl.ds(0, own)], send_sem=send_sum, recv_sem=recv_sum,
        device_id=peer(1, 0), device_id_type=MESH)
    all_sums.wait_recv()
    table = jnp.sum(gather[...], axis=0, keepdims=True)
    table = jnp.where(diagonal_at, table, 0.0)
    sums = jnp.broadcast_to(jnp.sum(table, axis=1, keepdims=True), (8, cols))
    m = [sums[k : k + 1, :] for k in range(6)]

    def dots(a, b, table):
        out = None
        for i in range(3):
            for j in range(3):
                if a[i] is not None and b[j] is not None:
                    t = a[i] * b[j] * table[i + j]
                    out = t if out is None else out + t
        return out

    shifted = [m[k] - m[k + 1] for k in range(5)]

    def plus(a, b, f):
        out = []
        for x, y in zip(a, b):
            out.append(x if y is None else (f * y if x is None else x + f * y))
        return out

    def image(d):
        moved = [None, d[0], d[1]]
        return [x if y is None else (None if x is None and y is None else (-y if x is None else x - y)) for x, y in zip(d, moved)]

    one = jnp.ones_like(m[0])
    direction = [one, None, None]
    residual = [one, None, None]
    pressure = [None, None, None]
    energy = m[0]
    for sweep in range(ITERS):
        bottom = dots(direction, direction, shifted)
        size = energy / bottom
        pressure = plus(pressure, direction, size)
        if sweep + 1 < ITERS:
            residual = plus(residual, image(direction), -size)
            fresh = dots(residual, residual, m)
            direction = plus(residual, direction, fresh / energy)
            energy = fresh

    def correct(r, carry):
        at = pl.ds(r - R, layers, stride=rows)
        for n in range(3):
            push = pressure[0] * pushes[0, n, r - R]
            push = push + pressure[1] * pushes[1, n, r - R] + pressure[2] * pushes[2, n, r - R]
            mom_out[n, at, :] = res[1 + n, r, :, :cols] - push
        return carry

    lax.fori_loop(R, R + rows, correct, 0, unroll=4)
    all_sums.wait_send()
    for cond, go, come in started:
        @pl.when(cond)
        def _(go=go):
            go.wait_send()


def body(nx, ny, depth, momentum, tracer, cell_wet, tile_wet):
    layers, rows, cols = depth.shape
    assert TILE % rows == 0 and TILE % cols == 0 and cols == 128 and rows * SEG == cols and layers == 16
    f32 = jnp.float32
    tall = rows + 2 * DEEP
    wide = 2 * cols
    half = layers // 2
    dma = pltpu.SemaphoreType.DMA
    vmem = pl.BlockSpec(memory_space=pltpu.VMEM)
    flat = jax.ShapeDtypeStruct((layers * rows, cols), f32)
    field = pltpu.VMEM((FIELDS, rows + 2 * REACH, layers, cols), f32)
    layer = pltpu.VMEM((tall, layers, cols), f32)
    three = pltpu.VMEM((3, layers, wide), f32)
    flows = 2 * FIELDS
    strip = pltpu.VMEM((4, flows + 1, half, cols), f32)
    pairs = [dma((4, 2))] * 2 + [dma((2,))] * 2 + [dma((4, 2))] * 2 + [dma((2, 2))] * 4
    pairs += [dma] * 2
    new_depth, new_momentum, new_tracer = pl.pallas_call(
        functools.partial(kernel, nx, ny, rows, cols, layers),
        out_shape=(pltpu.VMEM((layers * rows, cols), f32), pltpu.VMEM((3, layers * rows, cols), f32), pltpu.VMEM((layers * rows, cols), f32)),
        in_specs=[pl.BlockSpec(memory_space=pltpu.HBM)] * 5,
        out_specs=(vmem, vmem, vmem),
        scratch_shapes=[
            pltpu.VMEM((5, layers * rows, cols), f32),
            pltpu.VMEM((rows, cols), jnp.int32),
            pltpu.SMEM(tile_wet.shape, jnp.int32),
            dma((5,)),
            pltpu.VMEM((3, 3, rows, layers, cols), f32),
            field, field, field,
            pltpu.VMEM((FIELDS, tall, layers, cols), f32),
            pltpu.VMEM((tall, 1, cols), f32),
            pltpu.VMEM((rows + 1, half, cols), f32),
            pltpu.VMEM((rows, half, cols), f32),
            pltpu.VMEM((2, half, cols), f32),
            strip,
            pltpu.VMEM((3, FIELDS + 1, half, cols), f32),
            strip, strip,
            pltpu.VMEM((2, 2, 8, half, cols), f32),
            pltpu.VMEM((2, 2, half, cols), f32),
            pltpu.VMEM((flows, half, cols), f32),
            layer, layer, layer, layer, layer, layer, layer,
            pltpu.VMEM((2, half, wide), f32),
            three, three, three,
            pltpu.VMEM((nx * ny, cols), f32),
            *pairs,
        ],
        compiler_params=pltpu.CompilerParams(
            collective_id=0, has_side_effects=True, vmem_limit_bytes=56 * 1024 * 1024
        ),
    )(
        tile_wet,
        depth.reshape(layers * rows, cols),
        momentum.reshape(3, layers * rows, cols),
        tracer.reshape(layers * rows, cols),
        cell_wet,
    )
    new_depth, new_momentum, new_tracer = pl.pallas_call(
        hand_on,
        out_shape=(flat, jax.ShapeDtypeStruct((3, layers * rows, cols), f32), flat),
        in_specs=[pl.BlockSpec(memory_space=pl.ANY)] * 3,
        out_specs=(pl.BlockSpec(memory_space=pl.ANY),) * 3,
        scratch_shapes=[dma((3,))],
        compiler_params=pltpu.CompilerParams(vmem_limit_bytes=8 * 1024 * 1024),
    )(new_depth, new_momentum, new_tracer)
    return (
        new_depth.reshape(depth.shape),
        new_momentum.reshape(momentum.shape),
        new_tracer.reshape(tracer.shape),
    )


def hand_on(a, b, c, x, y, z, sem):
    moves = [pltpu.make_async_copy(s, d, sem.at[k]) for k, (s, d) in enumerate(((a, x), (b, y), (c, z)))]
    for m in moves:
        m.start()
    for m in moves:
        m.wait()


def solution(mesh):
    placed = (
        P(None, "gx", "gy"),
        P(None, None, "gx", "gy"),
        P(None, "gx", "gy"),
        P("gx", "gy"),
        P(),
    )
    return jax.shard_map(
        functools.partial(body, mesh.shape["gx"], mesh.shape["gy"]),
        mesh=mesh,
        in_specs=placed,
        out_specs=(P(None, "gx", "gy"), P(None, None, "gx", "gy"), P(None, "gx", "gy")),
        check_vma=False,
    )
```

```python
import functools

import jax
import jax.numpy as jnp
from jax import lax
from jax.experimental import pallas as pl
from jax.experimental.pallas import tpu as pltpu
from jax.sharding import PartitionSpec as P

ITERS = 3
TILE = 128
REACH = 2
DEEP = 1 + ITERS
SEG = 2 * DEEP
FIELDS = 5

gravity = 9.81
time_step = 0.025
root = gravity**0.5
MESH = pl.DeviceIdType.MESH


def minmod(a, b):
    return jnp.maximum(jnp.minimum(a, jnp.maximum(b, 0.0)), jnp.minimum(b, 0.0))


def hll(left, right, weight, normal):
    hl, hr = left[0], right[0]
    rl, rr = lax.rsqrt(hl), lax.rsqrt(hr)
    ul, ur = left[normal] * (rl * rl), right[normal] * (rr * rr)
    al, ar = hl * rl, hr * rr
    lower = jnp.minimum(jnp.minimum(ul - al, ur - ar), 0.0)
    upper = jnp.maximum(jnp.maximum(ul + al, ur + ar), 0.0)
    scale = weight / (upper - lower)
    low, high = lower * scale, upper * scale
    take_left = high * (ul - lower)
    take_right = low * (upper - ur)
    flux = [take_left * l + take_right * r for l, r in zip(left, right)]
    flux[normal] = flux[normal] + 0.5 * (high * hl * hl - low * hr * hr)
    return flux


def lane_next(x):
    return pltpu.roll(x, x.shape[-1] - 1, 1)


def lane_prev(x):
    return pltpu.roll(x, 1, 1)


def halves(u):
    return [0.5 * x for x in u]


def minus(a, b):
    return [x - y for x, y in zip(a, b)]


def sides(u, before, after):
    s = [minmod(b, a) for b, a in zip(before, after)]
    return minus(u, s), [x + y for x, y in zip(u, s)]


def across_flux(u, v, weight):
    d = [lane_next(x) - x for x in v]
    right, left = sides(u, [lane_prev(x) for x in d], d)
    return hll(left, [lane_next(x) for x in right], weight, 2)


def strip_flux(u, weight):
    v = halves(u)
    v1 = [lane_next(x) for x in v]
    v2 = [pltpu.roll(x, x.shape[-1] - 2, 1) for x in v]
    d0, d1, d2 = minus(v, [lane_prev(x) for x in v]), minus(v1, v), minus(v2, v1)
    _, left = sides(u, d0, d1)
    right, _ = sides([x + x for x in v1], d1, d2)
    return hll(left, right, weight, 2)


def kernel(
    nx, ny, rows, cols, layers,
    tile_hbm, depth_hbm, mom_hbm, tracer_hbm, wet_hbm,
    depth_out, mom_out, tracer_out,
    staged, wet_ref, tile_ref, load_sem, pushes,
    fa, fb, fc, res, wet, wet_rows, wet_cols, wet_edge, packed, squeezed, corner_out, from_l, from_r, from_c, wet_c, change,
    ce, cn, up, inv, z0, z1, z2, wet_strip, patch, beyond, slopes, gather,
    send_row, recv_row, send_wet, recv_wet, send_col, recv_col,
    send_wc, recv_wc, send_cor, recv_cor, send_sum, recv_sum,
):
    R = DEEP
    H = REACH
    width = 2 * cols
    half = layers // 2
    flows = 2 * FIELDS
    gx, gy = lax.axis_index("gx"), lax.axis_index("gy")

    loads = [
        pltpu.make_async_copy(wet_hbm, wet_ref, load_sem.at[0]),
        pltpu.make_async_copy(tile_hbm, tile_ref, load_sem.at[4]),
        pltpu.make_async_copy(depth_hbm, staged.at[0], load_sem.at[1]),
        pltpu.make_async_copy(mom_hbm, staged.at[pl.ds(1, 3)], load_sem.at[2]),
        pltpu.make_async_copy(tracer_hbm, staged.at[4], load_sem.at[3]),
    ]

    barrier = pltpu.get_barrier_semaphore()
    has = {-1: gx > 0, 1: gx < nx - 1}
    side = {-1: gy > 0, 1: gy < ny - 1}
    near = [(a, b) for a in (1, nx - 1, 0) for b in (0, 1, ny - 1) if (a, b) != (0, 0)]
    peers = list(dict.fromkeys(near)) + [
        (a, b) for a in range(nx) for b in range(ny) if (a, b) not in near and (a, b) != (0, 0)]

    def peer(a, b):
        return (lax.rem(gx + a, nx), lax.rem(gy + b, ny))

    for n, (a, b) in enumerate(peers):
        pl.semaphore_signal(barrier, inc=1, device_id=peer(a, b), device_id_type=MESH)
        if n + 1 == len(near):
            for load in loads:
                load.start()

    f32 = jnp.float32
    for dx in (-1, 1):
        @pl.when(jnp.logical_not(has[dx]))
        def _(dx=dx):
            at = slice(0, H) if dx < 0 else slice(H + rows, rows + 2 * H)
            for x in (fa, fb, fc):
                x[0, at] = jnp.ones((H, layers, cols), f32)
                x[1:, at] = jnp.zeros((FIELDS - 1, H, layers, cols), f32)
            at = slice(0, R) if dx < 0 else slice(R + rows, rows + 2 * R)
            res[0, at, :, :cols] = jnp.ones((R, layers, cols), f32)
            res[1:4, at, :, :cols] = jnp.zeros((3, R, layers, cols), f32)
            wet[at, :, :cols] = jnp.zeros((R, 1, cols), f32)
    for dy, landing in ((-1, from_l), (1, from_r)):
        @pl.when(jnp.logical_not(side[dy]))
        def _(landing=landing):
            landing[:3, :1] = jnp.ones((3, 1, half, cols), f32)
            landing[:3, 1:] = jnp.zeros((3, flows, half, cols), f32)
            landing[3, :2] = jnp.ones((2, half, cols), f32)
            landing[3, 2:] = jnp.zeros((flows - 1, half, cols), f32)
    for i, dx in enumerate((-1, 1)):
        for j, dy in enumerate((-1, 1)):
            @pl.when(jnp.logical_not(jnp.logical_and(has[dx], side[dy])))
            def _(i=i, j=j):
                depth_slots = lax.broadcasted_iota(jnp.int32, (half, cols), 1) < 2 * R * SEG
                from_c[i, j, 0] = jnp.where(depth_slots, 1.0, 0.0)
                from_c[i, j, 1] = jnp.zeros((half, cols), f32)
                wet_c[i, j] = jnp.zeros((half, cols), f32)

    def exchange(cond, src, dst, send, recv, back, device):
        args = dict(src_ref=src, dst_ref=dst, send_sem=send, device_id=device, device_id_type=MESH)
        return (cond, pltpu.make_async_remote_copy(recv_sem=recv, **args),
                pltpu.make_async_remote_copy(recv_sem=back, **args))

    started = []

    def begin(group):
        for cond, go, come in group:
            @pl.when(cond)
            def _(go=go):
                go.start()
        started.extend(group)

    def arrive(group):
        for cond, go, come in group:
            @pl.when(cond)
            def _(come=come):
                come.wait_recv()

    def row_copies(k, x, deep, part_of):
        group = []
        for i, dx in enumerate((-1, 1)):
            mine = deep if dx < 0 else rows
            theirs = deep + rows if dx < 0 else 0
            group.append(exchange(
                has[dx], part_of(x, mine), part_of(x, theirs),
                send_row.at[k, i], recv_row.at[k, i], recv_row.at[k, 1 - i], (gx + dx, gy)))
        return group

    def stage_rows(x, at):
        return x.at[:, pl.ds(at, H)]

    def result_rows(x, at):
        return x.at[pl.ds(0, 4), pl.ds(at, R), :, pl.ds(0, cols)]

    def column_copies(k, count):
        group = []
        source = packed.at[k, pl.ds(0, count)] if k == 3 else squeezed.at[k, pl.ds(0, count)]
        for j, (dy, landing) in enumerate(((-1, from_r), (1, from_l))):
            group.append(exchange(
                side[dy], source, landing.at[k, pl.ds(0, count)],
                send_col.at[k, j], recv_col.at[k, j], recv_col.at[k, 1 - j], (gx, gy + dy)))
        return group

    def corner_copies(src, landing, send, recv):
        group = []
        for i, dx in enumerate((-1, 1)):
            for j, dy in enumerate((-1, 1)):
                group.append(exchange(
                    jnp.logical_and(has[dx], side[dy]), src(i), landing.at[1 - i, 1 - j],
                    send.at[i, j], recv.at[i, j], recv.at[1 - i, 1 - j], (gx + dx, gy + dy)))
        return group

    lane = lax.broadcasted_iota(jnp.int32, (half, cols), 1)
    seg = lane // SEG
    pos = lane % SEG
    own_right = pos < DEEP
    edge = jnp.logical_or(lane < H, lane >= cols - H)
    cuts = [slice(q * half, (q + 1) * half) for q in range(2)]

    def into(x, r, total):
        return jnp.where(seg == r, pltpu.roll(x, SEG * r + DEEP, 1), total)

    def out_of(x, r):
        return pltpu.roll(x, cols - DEEP - SEG * r, 1)

    middle = jnp.logical_and(pos >= H, pos < DEEP + H)

    def squeeze(k, values):
        for f in range(FIELDS):
            squeezed[k, f] = jnp.where(middle, values[2 * f], pltpu.roll(values[2 * f + 1], DEEP, 1))

    def spread_out(x, q):
        return pltpu.roll(x, cols - DEEP, 1) if q else x

    for load in loads:
        load.wait()
    tile = tile_ref[(gx * rows) // TILE, (gy * cols) // TILE].astype(f32)
    for r in range(rows):
        wet[R + r, :, :cols] = wet_ref[r : r + 1, :].astype(f32) * tile

    def load_row(r, carry):
        at = pl.ds(r, layers, stride=rows)
        w = wet[R + r, :, :cols]
        carry = list(carry)
        for f in range(FIELDS):
            x = staged[f, at, :]
            if f == 0:
                x = x * w + (1.0 - w)
            elif f < 3:
                x = x * (1.0 / root)
            fa[f, H + r] = x
            for q in range(2):
                carry[2 * f + q] = into(x[cuts[q]], r, carry[2 * f + q])
        carry[flows] = into(jnp.broadcast_to(w, (half, cols)), r, carry[flows])
        return tuple(carry)

    blank = jnp.zeros((half, cols), f32)
    carry = (blank,) * (flows + 1)
    for lo, hi in ((0, H), (rows - H, rows)):
        carry = lax.fori_loop(lo, hi, load_row, carry, unroll=True)
    pl.semaphore_wait(barrier, len(peers))
    coming_rows = row_copies(0, fa, H, stage_rows)
    begin(coming_rows)
    wet_copies = []
    for i, dx in enumerate((-1, 1)):
        mine, theirs = (R, R + rows) if dx < 0 else (rows, 0)
        wet_copies.append(exchange(
            has[dx], wet.at[pl.ds(mine, R), :, pl.ds(0, cols)], wet.at[pl.ds(theirs, R), :, pl.ds(0, cols)],
            send_wet.at[i], recv_wet.at[i], recv_wet.at[1 - i], (gx + dx, gy)))
    begin(wet_copies)
    carry = lax.fori_loop(H, rows - H, load_row, carry, unroll=12)
    for n in range(flows + 1):
        packed[0, n] = carry[n]
    squeeze(0, carry)
    squeezed[0, FIELDS] = carry[flows]
    coming_cols = column_copies(0, FIELDS + 1)
    begin(coming_cols)
    wet_corners = corner_copies(lambda i: packed.at[0, flows], wet_c, send_wc, recv_wc)
    begin(wet_corners)

    inner = jnp.logical_and(lane >= 1, lane < cols - H)

    def column_weight(r, carry):
        w = jnp.broadcast_to(wet[R + r, :, :cols], (half, cols))
        wet_cols[r] = jnp.where(inner, (-time_step * root) * w * lane_next(w), 0.0)
        return carry

    def row_weight(r, carry):
        w = wet[R + r - 1, :, :cols] * wet[R + r, :, :cols]
        wet_rows[r] = jnp.broadcast_to((-time_step * root) * w, (half, cols))
        return carry

    lax.fori_loop(0, rows, column_weight, 0, unroll=4)
    lax.fori_loop(1, rows, row_weight, 0, unroll=5)

    def state(src, i, cut):
        return [src[f, i + H, cut, :] for f in range(FIELDS)]

    def blend(keep, i, cut, f, value):
        if keep is None:
            return value
        kept = fa[f, i + H, cut, :]
        if keep == 0.75:
            return 0.75 * kept + 0.25 * value
        return (1.0 / 3.0) * kept + (2.0 / 3.0) * value

    def sweep(src, dst, deep, keep):
        for cut in cuts:
            def store(i, rates, cut=cut):
                u = state(src, i, cut)
                across = across_flux(u, halves(u), wet_cols[i])
                for f in range(FIELDS):
                    rate = across[f] - lane_prev(across[f])
                    if rates is not None:
                        rate = rate + rates[f]
                    dst[f, i + deep, cut, :cols] = blend(keep, i, cut, f, u[f] + rate)

            def step(i, carry, cut=cut, store=store):
                flux_low, left, v1, d = carry
                v2 = halves(state(src, i + 2, cut))
                ahead = minus(v2, v1)
                right, following = sides(state(src, i + 1, cut), d, ahead)
                flux_high = hll(left, right, wet_rows[i + 1], 1)
                store(i, minus(flux_high, flux_low))
                return flux_high, following, v2, ahead

            a, b, c, e = [state(src, i, cut) for i in range(4)]
            va, vb, vc, ve = [halves(x) for x in (a, b, c, e)]
            dab, dbc, dce = minus(vb, va), minus(vc, vb), minus(ve, vc)
            _, left = sides(b, dab, dbc)
            right, following = sides(c, dbc, dce)
            flux = hll(left, right, wet_rows[H], 1)
            store(0, None)
            store(1, flux)
            flux, _, _, _ = lax.fori_loop(H, rows - H, step, (flux, following, ve, dce), unroll=6)
            store(rows - 2, [-x for x in flux])
            store(rows - 1, None)

    def ends(src, dst, deep, factor):
        for cut in cuts:
            for first in (-2, rows - 3):
                u = [state(src, first + n, cut) for n in range(5)]
                v = [halves(x) for x in u]
                d = [minus(y, x) for x, y in zip(v[:4], v[1:])]
                sided = [sides(u[n], d[n - 1], d[n]) for n in (1, 2, 3)]
                one = hll(sided[0][1], sided[1][0], wet_rows[first + 2], 1)
                two = hll(sided[1][1], sided[2][0], wet_rows[first + 3], 1)
                if first < 0:
                    changes = ((0, minus(two, one)), (1, [-x for x in two]))
                else:
                    changes = ((rows - 2, one), (rows - 1, minus(two, one)))
                for i, rates in changes:
                    for f in range(FIELDS):
                        rate = rates[f] if factor == 1.0 else factor * rates[f]
                        dst[f, i + deep, cut, :cols] = dst[f, i + deep, cut, :cols] + rate

    def edges(k, factor):
        for q in range(2):
            own = [packed[k, 2 * f + q] for f in range(FIELDS)]
            left = [jnp.where(own_right, spread_out(from_l[k, f], q), own[f]) for f in range(FIELDS)]
            right = [jnp.where(own_right, own[f], spread_out(from_r[k, f], q)) for f in range(FIELDS)]
            flux_l, flux_r = strip_flux(left, wet_edge[0]), strip_flux(right, wet_edge[1])
            for f in range(FIELDS):
                a, b = flux_r[f] - lane_prev(flux_r[f]), flux_l[f] - lane_prev(flux_l[f])
                t = jnp.where(own_right, a, b)
                change[2 * f + q] = t if factor == 1.0 else factor * t

    def pack(dst, deep, count):
        def row(r, carry):
            return tuple(
                into(dst[n // 2, r + deep, cuts[n % 2], :cols], r, carry[n]) for n in range(count))
        return row

    def mend(dst, deep, last):
        def row(r, carry):
            for f in range(FIELDS):
                for q in range(2):
                    x = dst[f, r + deep, cuts[q], :cols]
                    x = x + jnp.where(edge, out_of(change[2 * f + q], r), 0.0)
                    dst[f, r + deep, cuts[q], :cols] = x * root if last and f in (1, 2) else x
            return carry
        return row

    plan = ((fa, fb, H, None, 1.0), (fb, fc, H, 0.75, 0.25), (fc, res, R, 1.0 / 3.0, 2.0 / 3.0))
    for k, (src, dst, deep, keep, factor) in enumerate(plan):
        last = k == 2
        count = flows - 2 if last else flows
        sweep(src, dst, deep, keep)
        pack_row, mend_row = pack(dst, deep, count), mend(dst, deep, last)
        carry = lax.fori_loop(H, rows - H, pack_row, (blank,) * count, unroll=4)
        if k == 0:
            arrive(wet_copies)
            for r in (0, rows):
                row_weight(r, 0)
        arrive(coming_rows)
        arrive(coming_cols)
        ends(src, dst, deep, factor)
        if k == 0:
            own = packed[0, flows]
            for n, (w, first) in enumerate((
                    (jnp.where(own_right, from_l[0, FIELDS], own), DEEP - 1),
                    (jnp.where(own_right, own, from_r[0, FIELDS]), DEEP - 2))):
                used = jnp.logical_or(pos == first, pos == first + 1)
                wet_edge[n] = jnp.where(used, (-time_step * root) * w * lane_next(w), 0.0)
        edges(k, factor)
        for lo, hi in ((0, H), (rows - H, rows)):
            carry = lax.fori_loop(lo, hi, pack_row, carry, unroll=True)
        ahead = [carry[n] + change[n] for n in range(count)]
        for n in range(count):
            packed[k + 1, n] = ahead[n] * root if last and n // 2 in (1, 2) else ahead[n]
        if not last:
            squeeze(k + 1, ahead)
        for lo, hi in ((0, deep), (rows - deep, rows)):
            lax.fori_loop(lo, hi, mend_row, 0, unroll=True)
        coming_cols = column_copies(k + 1, count if last else FIELDS)
        begin(coming_cols)
        coming_rows = row_copies(k + 1, dst, deep, result_rows if last else stage_rows)
        begin(coming_rows)
        lax.fori_loop(deep, rows - deep, mend_row, 0, unroll=4)
    block = R * SEG
    quarter = lane // block

    def moved(x, start, end):
        shift = (end - start) * block % cols
        return pltpu.roll(x, shift, 1) if shift else x

    for i, start in enumerate((0, 3)):
        for g in range(2):
            total = blank
            for t in range(4):
                total = jnp.where(quarter == t, moved(packed[3, 4 * g + t], start, t), total)
            corner_out[i, g] = total

    def corner_of(i, j, n):
        end = 0 if i else 3
        return jnp.where(quarter == end, moved(from_c[i, j, n // 4], n % 4, end), 1.0)

    coming_corners = corner_copies(lambda i: corner_out.at[i], from_c, send_cor, recv_cor)
    begin(coming_corners)

    layer_id = lax.broadcasted_iota(jnp.int32, (layers, cols), 0)
    top = layer_id == layers - 1
    lane_all = lax.broadcasted_iota(jnp.int32, (layers, cols), 1)
    at_start, at_end = lane_all == 0, lane_all == cols - 1
    at_edge = jnp.logical_or(at_start, at_end)

    def above(x):
        return pltpu.roll(x, layers - 1, 0)

    def below(x):
        return pltpu.roll(x, 1, 0)

    def upward_of(h, w, top):
        return jnp.where(w > 0.0, 2.0 / jnp.where(top, h, h + above(h)), 0.0)

    def high_of(r):
        return 0.5 * (res[0, r] + res[0, r + 1]) * (wet[r] * wet[r + 1])

    def prepare(r):
        h, w = res[0, r], jnp.broadcast_to(wet[r], (layers, cols))
        high = high_of(r)
        across = 0.5 * (h + lane_next(h)) * (w * lane_next(w))
        upward = upward_of(h, w, top)
        inner = jnp.where(top, 0.0, upward)
        diagonal = 0.5 * h + ce[r - 1] + high + lane_prev(across) + across + below(inner) + upward
        v = res[3, r]
        y = res[2, r]
        div = (
            0.5 * (res[1, r + 1] - res[1, r - 1])
            + 0.5 * (lane_next(y) - lane_prev(y))
            + (v - jnp.where(layer_id == 0, 0.0, below(v)))
        )
        ce[r] = high
        cn[r] = across
        up[r] = upward
        inv[r] = jnp.where(diagonal == 0.0, 0.0, 1.0 / diagonal)
        z0[r] = -div * w

    def prepare_loop(r, carry):
        prepare(r)
        return carry

    ce[R] = high_of(R)
    lax.fori_loop(R + 1, R + rows - 1, prepare_loop, 0, unroll=7)

    def wide_of(main, halo):
        return jnp.concatenate([main, halo], axis=1)

    def halo_pack(x):
        total = blank
        for n in range(R):
            total = into(x(R + rows + n), n, total)
            total = into(x(n), rows - R + n, total)
        return total

    lower_rows = seg < rows // 2

    def strips_of(l, own, r, halo, corner):
        far_l = jnp.where(lower_rows, corner(1, 0), corner(0, 0))
        far_r = jnp.where(lower_rows, corner(1, 1), corner(0, 1))
        return (
            wide_of(jnp.where(own_right, l, own), jnp.where(own_right, far_l, halo)),
            wide_of(jnp.where(own_right, own, r), jnp.where(own_right, halo, far_r)))

    arrive(wet_corners)
    wet_halo = halo_pack(lambda r: jnp.broadcast_to(wet[r], (half, cols)))
    for n, w in enumerate(strips_of(
            from_l[0, FIELDS], packed[0, flows], from_r[0, FIELDS], wet_halo, lambda i, j: wet_c[i, j])):
        wet_strip[n] = w

    arrive(coming_cols)
    arrive(coming_corners)
    arrive(coming_rows)

    fields = []
    for f in range(4):
        parts = []
        for q in range(2):
            n = 2 * f + q
            parts.append(strips_of(
                from_l[3, n], packed[3, n], from_r[3, n],
                halo_pack(lambda r: res[f, r, cuts[q], :]), lambda i, j: corner_of(i, j, n)))
        fields.append([jnp.concatenate([parts[0][n], parts[1][n]], axis=0) for n in range(2)])

    wide_layer = lax.broadcasted_iota(jnp.int32, (layers, width), 0)
    wide_top = wide_layer == layers - 1
    wide_pos = lax.broadcasted_iota(jnp.int32, (layers, width), 1) % SEG < DEEP

    def row_next(x):
        return pltpu.roll(x, width - SEG, 1)

    def row_prev(x):
        return pltpu.roll(x, SEG, 1)

    systems = []
    for n in range(2):
        h, x, y, v = [fields[f][n] for f in range(4)]
        w = jnp.concatenate([wet_strip[n], wet_strip[n]], axis=0)
        high = 0.5 * (h + row_next(h)) * (w * row_next(w))
        low = row_prev(high)
        across = 0.5 * (h + lane_next(h)) * (w * lane_next(w))
        back = lane_prev(across)
        upward = upward_of(h, w, wide_top)
        inner = jnp.where(wide_top, 0.0, upward)
        diagonal = 0.5 * h + low + high + back + across + below(inner) + upward
        inverse = jnp.where(diagonal == 0.0, 0.0, 1.0 / diagonal)
        div = (
            0.5 * (row_next(x) - row_prev(x))
            + 0.5 * (lane_next(y) - lane_prev(y))
            + (v - jnp.where(wide_layer == 0, 0.0, below(v)))
        )
        force = -div * w
        z = force * inverse
        levels = [z]
        for _ in range(2):
            z = inverse * (
                low * row_prev(z) + high * row_next(z) + across * lane_next(z) + back * lane_prev(z)
                + inner * above(z) + below(inner * z))
            levels.append(z)
        systems.append((across, inverse, force, levels))
    left, right = systems
    for n in range(3):
        patch[n] = jnp.where(wide_pos, right[n], left[n])
    for k in range(3):
        zl, zr = left[3][k], right[3][k]
        beyond[k] = jnp.where(wide_pos, left[0] * zl, zr)
        slopes[k] = jnp.where(wide_pos, left[0] * (lane_next(zl) - zl), zr)

    face_ends = jnp.zeros((layers, cols), f32)
    for across, _, _, levels in systems:
        z, c = levels[2][:, :cols], across[:, :cols]
        face_ends = face_ends + c * z * lane_next(z)
    face_ends = jnp.where(lane_all % SEG == DEEP - 1, face_ends, 0.0)

    def seen(strip, k, r, page):
        shift = {0: R, 1: R + rows, -1: R - rows}[page]
        lanes = slice(0, cols) if page == 0 else slice(cols, width)
        return out_of(strip[k, :, lanes], r - shift)

    def complete(r, page):
        cn[r] = jnp.where(at_edge, seen(patch, 0, r, page), cn[r])
        inverse = jnp.where(at_edge, seen(patch, 1, r, page), inv[r])
        force = jnp.where(at_edge, seen(patch, 2, r, page), z0[r])
        z = force * inverse
        inv[r] = inverse
        z0[r] = z
        return force * z

    def fold(x):
        return x[:half] + x[half:]

    first = R - ITERS
    ce[first - 1] = high_of(first - 1)
    for r in (*range(first, R + 1), *range(R + rows - 1, R + rows + ITERS)):
        prepare(r)
    for r in range(first, R):
        complete(r, -1)
        complete(r + ITERS + rows, 1)
    m0 = lax.fori_loop(R, R + rows, lambda r, acc: acc + fold(complete(r, 0)), blank, unroll=16)

    def next_in(x, edges_of):
        return lane_next(jnp.where(at_start, edges_of, x))

    def prev_in(x, edges_of):
        return lane_prev(jnp.where(at_end, edges_of, x))

    def spread(k, z, r, page):
        x = z[r]
        c = cn[r]
        u = jnp.where(top, 0.0, up[r])
        out = seen(beyond, k, r, page)
        return (
            ce[r - 1] * z[r - 1] + ce[r] * z[r + 1]
            + c * next_in(x, out) + prev_in(c * x, out)
            + u * above(x) + below(u * x)
        )

    def advance(k, z, target, reach):
        def inner(r, carry):
            odd, even = carry
            n = spread(k, z, r, 0)
            y = n * inv[r]
            target[r] = y
            return odd + fold(z[r] * n), even + fold(y * n)

        for r in range(reach):
            target[R - 1 - r] = spread(k, z, R - 1 - r, -1) * inv[R - 1 - r]
            target[R + rows + r] = spread(k, z, R + rows + r, 1) * inv[R + rows + r]
        return lax.fori_loop(R, R + rows, inner, (blank, blank), unroll=16)

    m1, m2 = advance(0, z0, z1, 2)
    m3, m4 = advance(1, z1, z2, 1)
    def faces(r, acc):
        x = z2[r]
        u = jnp.where(top, 0.0, up[r])
        t = ce[r] * z2[r + 1] + jnp.where(at_end, 0.0, cn[r]) * lane_next(x) + u * above(x)
        return acc + fold(x * t)

    m5 = lax.fori_loop(R, R + rows, faces, blank, unroll=16)
    beyond_low = ce[R - 1] * z2[R - 1] * z2[R]
    beyond_high = ce[R + rows - 1] * z2[R + rows - 1] * z2[R + rows]
    m5 = 2.0 * m5 + fold(beyond_low - beyond_high + face_ends)

    row_id = lax.broadcasted_iota(jnp.int32, (8, cols), 0)
    lane_id = lax.broadcasted_iota(jnp.int32, (8, cols), 1)
    diagonal_at = row_id == lane_id
    table = blank
    for k, x in enumerate((m0, m1, m2, m3, m4, m5)):
        table = jnp.where(row_id == k, jnp.sum(x, axis=0, keepdims=True), table)
    table = jnp.where(diagonal_at, jnp.sum(table, axis=1, keepdims=True), 0.0)
    own = len(peers)
    gather[own : own + 1, :] = jnp.sum(table, axis=0, keepdims=True)
    for n, (a, b) in enumerate(reversed(peers)):
        pltpu.make_async_remote_copy(
            src_ref=gather.at[pl.ds(own, 1)], dst_ref=gather.at[pl.ds(n, 1)], send_sem=send_sum, recv_sem=recv_sum,
            device_id=peer(a, b), device_id_type=MESH).start()

    def push_of(k, z):
        def row(r, carry):
            q, c = z[r], cn[r]
            east = 0.5 * (ce[r] * (z[r + 1] - q) + ce[r - 1] * (q - z[r - 1]))
            out = seen(slopes, k, r, 0)
            slope = c * (next_in(q, out) - q)
            north = 0.5 * (slope + prev_in(slope, out))
            upward = up[r] * (jnp.where(top, 0.0, above(q)) - q)
            for n, push in enumerate((east, north, upward)):
                pushes[k, n, r - R] = push
            return carry

        lax.fori_loop(R, R + rows, row, 0, unroll=4)

    def plain_out(r, carry):
        at = pl.ds(r - R, layers, stride=rows)
        depth_out[at, :] = jnp.where(jnp.broadcast_to(wet[r, :, :cols], (layers, cols)) > 0.0, res[0, r, :, :cols], staged[0, at, :])
        tracer_out[at, :] = res[4, r, :, :cols]
        return carry

    push_of(0, z0)
    push_of(1, z1)
    push_of(2, z2)
    lax.fori_loop(R, R + rows, plain_out, 0, unroll=4)
    all_sums = pltpu.make_async_remote_copy(
        src_ref=gather.at[pl.ds(0, own)], dst_ref=gather.at[pl.ds(0, own)], send_sem=send_sum, recv_sem=recv_sum,
        device_id=peer(1, 0), device_id_type=MESH)
    all_sums.wait_recv()
    table = jnp.sum(gather[...], axis=0, keepdims=True)
    table = jnp.where(diagonal_at, table, 0.0)
    sums = jnp.broadcast_to(jnp.sum(table, axis=1, keepdims=True), (8, cols))
    m = [sums[k : k + 1, :] for k in range(6)]

    def dots(a, b, table):
        out = None
        for i in range(3):
            for j in range(3):
                if a[i] is not None and b[j] is not None:
                    t = a[i] * b[j] * table[i + j]
                    out = t if out is None else out + t
        return out

    shifted = [m[k] - m[k + 1] for k in range(5)]

    def plus(a, b, f):
        out = []
        for x, y in zip(a, b):
            out.append(x if y is None else (f * y if x is None else x + f * y))
        return out

    def image(d):
        moved = [None, d[0], d[1]]
        return [x if y is None else (None if x is None and y is None else (-y if x is None else x - y)) for x, y in zip(d, moved)]

    one = jnp.ones_like(m[0])
    direction = [one, None, None]
    residual = [one, None, None]
    pressure = [None, None, None]
    energy = m[0]
    for sweep in range(ITERS):
        bottom = dots(direction, direction, shifted)
        size = energy / bottom
        pressure = plus(pressure, direction, size)
        if sweep + 1 < ITERS:
            residual = plus(residual, image(direction), -size)
            fresh = dots(residual, residual, m)
            direction = plus(residual, direction, fresh / energy)
            energy = fresh

    def correct(r, carry):
        at = pl.ds(r - R, layers, stride=rows)
        for n in range(3):
            push = pressure[0] * pushes[0, n, r - R]
            push = push + pressure[1] * pushes[1, n, r - R] + pressure[2] * pushes[2, n, r - R]
            mom_out[n, at, :] = res[1 + n, r, :, :cols] - push
        return carry

    lax.fori_loop(R, R + rows, correct, 0, unroll=4)
    all_sums.wait_send()
    for cond, go, come in started:
        @pl.when(cond)
        def _(go=go):
            go.wait_send()


def body(nx, ny, depth, momentum, tracer, cell_wet, tile_wet):
    layers, rows, cols = depth.shape
    assert TILE % rows == 0 and TILE % cols == 0 and cols == 128 and rows * SEG == cols and layers == 16 and 4 * DEEP == rows
    f32 = jnp.float32
    tall = rows + 2 * DEEP
    wide = 2 * cols
    half = layers // 2
    dma = pltpu.SemaphoreType.DMA
    vmem = pl.BlockSpec(memory_space=pltpu.VMEM)
    flat = jax.ShapeDtypeStruct((layers * rows, cols), f32)
    field = pltpu.VMEM((FIELDS, rows + 2 * REACH, layers, cols), f32)
    layer = pltpu.VMEM((tall, layers, cols), f32)
    three = pltpu.VMEM((3, layers, wide), f32)
    flows = 2 * FIELDS
    strip = pltpu.VMEM((4, flows + 1, half, cols), f32)
    pairs = [dma((4, 2))] * 2 + [dma((2,))] * 2 + [dma((4, 2))] * 2 + [dma((2, 2))] * 4
    pairs += [dma] * 2
    new_depth, new_momentum, new_tracer = pl.pallas_call(
        functools.partial(kernel, nx, ny, rows, cols, layers),
        out_shape=(pltpu.VMEM((layers * rows, cols), f32), pltpu.VMEM((3, layers * rows, cols), f32), pltpu.VMEM((layers * rows, cols), f32)),
        in_specs=[pl.BlockSpec(memory_space=pltpu.HBM)] * 5,
        out_specs=(vmem, vmem, vmem),
        scratch_shapes=[
            pltpu.VMEM((5, layers * rows, cols), f32),
            pltpu.VMEM((rows, cols), jnp.int32),
            pltpu.SMEM(tile_wet.shape, jnp.int32),
            dma((5,)),
            pltpu.VMEM((3, 3, rows, layers, cols), f32),
            field, field, field,
            pltpu.VMEM((FIELDS, tall, layers, cols), f32),
            pltpu.VMEM((tall, 1, cols), f32),
            pltpu.VMEM((rows + 1, half, cols), f32),
            pltpu.VMEM((rows, half, cols), f32),
            pltpu.VMEM((2, half, cols), f32),
            strip,
            pltpu.VMEM((3, FIELDS + 1, half, cols), f32),
            pltpu.VMEM((2, 2, half, cols), f32),
            strip, strip,
            pltpu.VMEM((2, 2, 2, half, cols), f32),
            pltpu.VMEM((2, 2, half, cols), f32),
            pltpu.VMEM((flows, half, cols), f32),
            layer, layer, layer, layer, layer, layer, layer,
            pltpu.VMEM((2, half, wide), f32),
            three, three, three,
            pltpu.VMEM((nx * ny, cols), f32),
            *pairs,
        ],
        compiler_params=pltpu.CompilerParams(
            collective_id=0, has_side_effects=True, vmem_limit_bytes=56 * 1024 * 1024
        ),
    )(
        tile_wet,
        depth.reshape(layers * rows, cols),
        momentum.reshape(3, layers * rows, cols),
        tracer.reshape(layers * rows, cols),
        cell_wet,
    )
    new_depth, new_momentum, new_tracer = pl.pallas_call(
        hand_on,
        out_shape=(flat, jax.ShapeDtypeStruct((3, layers * rows, cols), f32), flat),
        in_specs=[pl.BlockSpec(memory_space=pl.ANY)] * 3,
        out_specs=(pl.BlockSpec(memory_space=pl.ANY),) * 3,
        scratch_shapes=[dma((3,))],
        compiler_params=pltpu.CompilerParams(vmem_limit_bytes=8 * 1024 * 1024),
    )(new_depth, new_momentum, new_tracer)
    return (
        new_depth.reshape(depth.shape),
        new_momentum.reshape(momentum.shape),
        new_tracer.reshape(tracer.shape),
    )


def hand_on(a, b, c, x, y, z, sem):
    moves = [pltpu.make_async_copy(s, d, sem.at[k]) for k, (s, d) in enumerate(((a, x), (b, y), (c, z)))]
    for m in moves:
        m.start()
    for m in moves:
        m.wait()


def solution(mesh):
    placed = (
        P(None, "gx", "gy"),
        P(None, None, "gx", "gy"),
        P(None, "gx", "gy"),
        P("gx", "gy"),
        P(),
    )
    return jax.shard_map(
        functools.partial(body, mesh.shape["gx"], mesh.shape["gy"]),
        mesh=mesh,
        in_specs=placed,
        out_specs=(P(None, "gx", "gy"), P(None, None, "gx", "gy"), P(None, "gx", "gy")),
        check_vma=False,
    )
```

```python
import functools

import jax
import jax.numpy as jnp
from jax import lax
from jax.experimental import pallas as pl
from jax.experimental.pallas import tpu as pltpu
from jax.sharding import PartitionSpec as P

ITERS = 3
TILE = 128
REACH = 2
DEEP = 1 + ITERS
SEG = 2 * DEEP
FIELDS = 5

gravity = 9.81
time_step = 0.025
root = gravity**0.5
MESH = pl.DeviceIdType.MESH


def minmod(a, b):
    return jnp.maximum(jnp.minimum(a, jnp.maximum(b, 0.0)), jnp.minimum(b, 0.0))


def hll(left, right, weight, normal):
    hl, hr = left[0], right[0]
    rl, rr = lax.rsqrt(hl), lax.rsqrt(hr)
    ul, ur = left[normal] * (rl * rl), right[normal] * (rr * rr)
    al, ar = hl * rl, hr * rr
    lower = jnp.minimum(jnp.minimum(ul - al, ur - ar), 0.0)
    upper = jnp.maximum(jnp.maximum(ul + al, ur + ar), 0.0)
    scale = weight / (upper - lower)
    low, high = lower * scale, upper * scale
    take_left = high * (ul - lower)
    take_right = low * (upper - ur)
    flux = [take_left * l + take_right * r for l, r in zip(left, right)]
    flux[normal] = flux[normal] + 0.5 * (high * hl * hl - low * hr * hr)
    return flux


def lane_next(x):
    return pltpu.roll(x, x.shape[-1] - 1, 1)


def lane_prev(x):
    return pltpu.roll(x, 1, 1)


def halves(u):
    return [0.5 * x for x in u]


def minus(a, b):
    return [x - y for x, y in zip(a, b)]


def sides(u, before, after):
    s = [minmod(b, a) for b, a in zip(before, after)]
    return minus(u, s), [x + y for x, y in zip(u, s)]


def across_flux(u, v, weight):
    d = [lane_next(x) - x for x in v]
    right, left = sides(u, [lane_prev(x) for x in d], d)
    return hll(left, [lane_next(x) for x in right], weight, 2)


def strip_flux(u, weight):
    v = halves(u)
    v1 = [lane_next(x) for x in v]
    v2 = [pltpu.roll(x, x.shape[-1] - 2, 1) for x in v]
    d0, d1, d2 = minus(v, [lane_prev(x) for x in v]), minus(v1, v), minus(v2, v1)
    _, left = sides(u, d0, d1)
    right, _ = sides([x + x for x in v1], d1, d2)
    return hll(left, right, weight, 2)


def kernel(
    nx, ny, rows, cols, layers,
    tile_hbm, depth_hbm, mom_hbm, tracer_hbm, wet_hbm,
    depth_out, mom_out, tracer_out,
    staged, wet_ref, tile_ref, load_sem, pushes,
    fa, fb, fc, res, wet, wet_rows, wet_cols, wet_edge, packed, squeezed, corner_out, from_l, from_r, from_c, wet_c, change,
    ce, cn, up, inv, z0, z1, z2, wet_strip, patch, beyond, slopes, gather,
    send_row, recv_row, send_wet, recv_wet, send_col, recv_col,
    send_wc, recv_wc, send_cor, recv_cor, send_sum, recv_sum,
):
    R = DEEP
    H = REACH
    width = 2 * cols
    half = layers // 2
    flows = 2 * FIELDS
    gx, gy = lax.axis_index("gx"), lax.axis_index("gy")

    loads = [
        pltpu.make_async_copy(wet_hbm, wet_ref, load_sem.at[0]),
        pltpu.make_async_copy(tile_hbm, tile_ref, load_sem.at[4]),
        pltpu.make_async_copy(depth_hbm, staged.at[0], load_sem.at[1]),
        pltpu.make_async_copy(mom_hbm, staged.at[pl.ds(1, 3)], load_sem.at[2]),
        pltpu.make_async_copy(tracer_hbm, staged.at[4], load_sem.at[3]),
    ]

    barrier = pltpu.get_barrier_semaphore()
    has = {-1: gx > 0, 1: gx < nx - 1}
    side = {-1: gy > 0, 1: gy < ny - 1}
    near = [(a, b) for a in (1, nx - 1, 0) for b in (0, 1, ny - 1) if (a, b) != (0, 0)]
    peers = list(dict.fromkeys(near)) + [
        (a, b) for a in range(nx) for b in range(ny) if (a, b) not in near and (a, b) != (0, 0)]

    def peer(a, b):
        return (lax.rem(gx + a, nx), lax.rem(gy + b, ny))

    for n, (a, b) in enumerate(peers):
        pl.semaphore_signal(barrier, inc=1, device_id=peer(a, b), device_id_type=MESH)
        if n + 1 == len(near):
            for load in loads:
                load.start()

    f32 = jnp.float32
    for dx in (-1, 1):
        @pl.when(jnp.logical_not(has[dx]))
        def _(dx=dx):
            at = slice(0, H) if dx < 0 else slice(H + rows, rows + 2 * H)
            for x in (fa, fb, fc):
                x[0, at] = jnp.ones((H, layers, cols), f32)
                x[1:, at] = jnp.zeros((FIELDS - 1, H, layers, cols), f32)
            at = slice(0, R) if dx < 0 else slice(R + rows, rows + 2 * R)
            res[0, at, :, :cols] = jnp.ones((R, layers, cols), f32)
            res[1:4, at, :, :cols] = jnp.zeros((3, R, layers, cols), f32)
            wet[at, :, :cols] = jnp.zeros((R, 1, cols), f32)
    for dy, landing in ((-1, from_l), (1, from_r)):
        @pl.when(jnp.logical_not(side[dy]))
        def _(landing=landing):
            landing[:3, :1] = jnp.ones((3, 1, half, cols), f32)
            landing[:3, 1:] = jnp.zeros((3, flows, half, cols), f32)
            landing[3, :2] = jnp.ones((2, half, cols), f32)
            landing[3, 2:] = jnp.zeros((flows - 1, half, cols), f32)
    for i, dx in enumerate((-1, 1)):
        for j, dy in enumerate((-1, 1)):
            @pl.when(jnp.logical_not(jnp.logical_and(has[dx], side[dy])))
            def _(i=i, j=j):
                depth_slots = lax.broadcasted_iota(jnp.int32, (half, cols), 1) < 2 * R * SEG
                from_c[i, j, 0] = jnp.where(depth_slots, 1.0, 0.0)
                from_c[i, j, 1] = jnp.zeros((half, cols), f32)
                wet_c[i, j] = jnp.zeros((half, cols), f32)

    def exchange(cond, src, dst, send, recv, back, device):
        args = dict(src_ref=src, dst_ref=dst, send_sem=send, device_id=device, device_id_type=MESH)
        return (cond, pltpu.make_async_remote_copy(recv_sem=recv, **args),
                pltpu.make_async_remote_copy(recv_sem=back, **args))

    started = []

    def begin(group):
        for cond, go, come in group:
            @pl.when(cond)
            def _(go=go):
                go.start()
        started.extend(group)

    def arrive(group):
        for cond, go, come in group:
            @pl.when(cond)
            def _(come=come):
                come.wait_recv()

    def row_copies(k, x, deep, part_of):
        group = []
        for i, dx in enumerate((-1, 1)):
            mine = deep if dx < 0 else rows
            theirs = deep + rows if dx < 0 else 0
            group.append(exchange(
                has[dx], part_of(x, mine), part_of(x, theirs),
                send_row.at[k, i], recv_row.at[k, i], recv_row.at[k, 1 - i], (gx + dx, gy)))
        return group

    def stage_rows(x, at):
        return x.at[:, pl.ds(at, H)]

    def result_rows(x, at):
        return x.at[pl.ds(0, 4), pl.ds(at, R), :, pl.ds(0, cols)]

    def column_copies(k, count):
        group = []
        source = packed.at[k, pl.ds(0, count)] if k == 3 else squeezed.at[k, pl.ds(0, count)]
        for j, (dy, landing) in enumerate(((-1, from_r), (1, from_l))):
            group.append(exchange(
                side[dy], source, landing.at[k, pl.ds(0, count)],
                send_col.at[k, j], recv_col.at[k, j], recv_col.at[k, 1 - j], (gx, gy + dy)))
        return group

    def corner_copies(src, landing, send, recv):
        group = []
        for i, dx in enumerate((-1, 1)):
            for j, dy in enumerate((-1, 1)):
                group.append(exchange(
                    jnp.logical_and(has[dx], side[dy]), src(i), landing.at[1 - i, 1 - j],
                    send.at[i, j], recv.at[i, j], recv.at[1 - i, 1 - j], (gx + dx, gy + dy)))
        return group

    lane = lax.broadcasted_iota(jnp.int32, (half, cols), 1)
    seg = lane // SEG
    pos = lane % SEG
    own_right = pos < DEEP
    edge = jnp.logical_or(lane < H, lane >= cols - H)
    cuts = [slice(q * half, (q + 1) * half) for q in range(2)]

    def into(x, r, total):
        return jnp.where(seg == r, pltpu.roll(x, SEG * r + DEEP, 1), total)

    def out_of(x, r):
        return pltpu.roll(x, cols - DEEP - SEG * r, 1)

    middle = jnp.logical_and(pos >= H, pos < DEEP + H)

    def squeeze(k, values):
        for f in range(FIELDS):
            squeezed[k, f] = jnp.where(middle, values[2 * f], pltpu.roll(values[2 * f + 1], DEEP, 1))

    def spread_out(x, q):
        return pltpu.roll(x, cols - DEEP, 1) if q else x

    for load in loads:
        load.wait()
    tile = tile_ref[(gx * rows) // TILE, (gy * cols) // TILE].astype(f32)
    for r in range(rows):
        wet[R + r, :, :cols] = wet_ref[r : r + 1, :].astype(f32) * tile

    def load_row(r, carry):
        at = pl.ds(r, layers, stride=rows)
        w = wet[R + r, :, :cols]
        carry = list(carry)
        for f in range(FIELDS):
            x = staged[f, at, :]
            if f == 0:
                x = x * w + (1.0 - w)
            elif f < 3:
                x = x * (1.0 / root)
            fa[f, H + r] = x
            for q in range(2):
                carry[2 * f + q] = into(x[cuts[q]], r, carry[2 * f + q])
        carry[flows] = into(jnp.broadcast_to(w, (half, cols)), r, carry[flows])
        return tuple(carry)

    blank = jnp.zeros((half, cols), f32)
    carry = (blank,) * (flows + 1)
    for lo, hi in ((0, H), (rows - H, rows)):
        carry = lax.fori_loop(lo, hi, load_row, carry, unroll=True)
    pl.semaphore_wait(barrier, len(peers))
    coming_rows = row_copies(0, fa, H, stage_rows)
    begin(coming_rows)
    wet_copies = []
    for i, dx in enumerate((-1, 1)):
        mine, theirs = (R, R + rows) if dx < 0 else (rows, 0)
        wet_copies.append(exchange(
            has[dx], wet.at[pl.ds(mine, R), :, pl.ds(0, cols)], wet.at[pl.ds(theirs, R), :, pl.ds(0, cols)],
            send_wet.at[i], recv_wet.at[i], recv_wet.at[1 - i], (gx + dx, gy)))
    begin(wet_copies)
    carry = lax.fori_loop(H, rows - H, load_row, carry, unroll=12)
    for n in range(flows + 1):
        packed[0, n] = carry[n]
    squeeze(0, carry)
    squeezed[0, FIELDS] = carry[flows]
    coming_cols = column_copies(0, FIELDS + 1)
    begin(coming_cols)
    wet_corners = corner_copies(lambda i: packed.at[0, flows], wet_c, send_wc, recv_wc)

    inner = jnp.logical_and(lane >= 1, lane < cols - H)

    def column_weight(r, carry):
        w = jnp.broadcast_to(wet[R + r, :, :cols], (half, cols))
        wet_cols[r] = jnp.where(inner, (-time_step * root) * w * lane_next(w), 0.0)
        return carry

    def row_weight(r, carry):
        w = wet[R + r - 1, :, :cols] * wet[R + r, :, :cols]
        wet_rows[r] = jnp.broadcast_to((-time_step * root) * w, (half, cols))
        return carry

    lax.fori_loop(0, rows, column_weight, 0, unroll=4)
    lax.fori_loop(1, rows, row_weight, 0, unroll=5)

    def state(src, i, cut):
        return [src[f, i + H, cut, :] for f in range(FIELDS)]

    def blend(keep, i, cut, f, value):
        if keep is None:
            return value
        kept = fa[f, i + H, cut, :]
        if keep == 0.75:
            return 0.75 * kept + 0.25 * value
        return (1.0 / 3.0) * kept + (2.0 / 3.0) * value

    def sweep(src, dst, deep, keep):
        for cut in cuts:
            def store(i, rates, cut=cut):
                u = state(src, i, cut)
                across = across_flux(u, halves(u), wet_cols[i])
                for f in range(FIELDS):
                    rate = across[f] - lane_prev(across[f])
                    if rates is not None:
                        rate = rate + rates[f]
                    dst[f, i + deep, cut, :cols] = blend(keep, i, cut, f, u[f] + rate)

            def step(i, carry, cut=cut, store=store):
                flux_low, left, v1, d = carry
                v2 = halves(state(src, i + 2, cut))
                ahead = minus(v2, v1)
                right, following = sides(state(src, i + 1, cut), d, ahead)
                flux_high = hll(left, right, wet_rows[i + 1], 1)
                store(i, minus(flux_high, flux_low))
                return flux_high, following, v2, ahead

            a, b, c, e = [state(src, i, cut) for i in range(4)]
            va, vb, vc, ve = [halves(x) for x in (a, b, c, e)]
            dab, dbc, dce = minus(vb, va), minus(vc, vb), minus(ve, vc)
            _, left = sides(b, dab, dbc)
            right, following = sides(c, dbc, dce)
            flux = hll(left, right, wet_rows[H], 1)
            store(0, None)
            store(1, flux)
            flux, _, _, _ = lax.fori_loop(H, rows - H, step, (flux, following, ve, dce), unroll=6)
            store(rows - 2, [-x for x in flux])
            store(rows - 1, None)

    def ends(src, dst, deep, factor):
        for cut in cuts:
            for first in (-2, rows - 3):
                u = [state(src, first + n, cut) for n in range(5)]
                v = [halves(x) for x in u]
                d = [minus(y, x) for x, y in zip(v[:4], v[1:])]
                sided = [sides(u[n], d[n - 1], d[n]) for n in (1, 2, 3)]
                one = hll(sided[0][1], sided[1][0], wet_rows[first + 2], 1)
                two = hll(sided[1][1], sided[2][0], wet_rows[first + 3], 1)
                if first < 0:
                    changes = ((0, minus(two, one)), (1, [-x for x in two]))
                else:
                    changes = ((rows - 2, one), (rows - 1, minus(two, one)))
                for i, rates in changes:
                    for f in range(FIELDS):
                        rate = rates[f] if factor == 1.0 else factor * rates[f]
                        dst[f, i + deep, cut, :cols] = dst[f, i + deep, cut, :cols] + rate

    def edges(k, factor):
        for q in range(2):
            own = [packed[k, 2 * f + q] for f in range(FIELDS)]
            left = [jnp.where(own_right, spread_out(from_l[k, f], q), own[f]) for f in range(FIELDS)]
            right = [jnp.where(own_right, own[f], spread_out(from_r[k, f], q)) for f in range(FIELDS)]
            flux_l, flux_r = strip_flux(left, wet_edge[0]), strip_flux(right, wet_edge[1])
            for f in range(FIELDS):
                a, b = flux_r[f] - lane_prev(flux_r[f]), flux_l[f] - lane_prev(flux_l[f])
                t = jnp.where(own_right, a, b)
                change[2 * f + q] = t if factor == 1.0 else factor * t

    def pack(dst, deep, count):
        def row(r, carry):
            return tuple(
                into(dst[n // 2, r + deep, cuts[n % 2], :cols], r, carry[n]) for n in range(count))
        return row

    def mend(dst, deep, last):
        def row(r, carry):
            for f in range(FIELDS):
                for q in range(2):
                    x = dst[f, r + deep, cuts[q], :cols]
                    x = x + jnp.where(edge, out_of(change[2 * f + q], r), 0.0)
                    dst[f, r + deep, cuts[q], :cols] = x * root if last and f in (1, 2) else x
            return carry
        return row

    plan = ((fa, fb, H, None, 1.0), (fb, fc, H, 0.75, 0.25), (fc, res, R, 1.0 / 3.0, 2.0 / 3.0))
    for k, (src, dst, deep, keep, factor) in enumerate(plan):
        last = k == 2
        count = flows - 2 if last else flows
        sweep(src, dst, deep, keep)
        pack_row, mend_row = pack(dst, deep, count), mend(dst, deep, last)
        carry = lax.fori_loop(H, rows - H, pack_row, (blank,) * count, unroll=4)
        if k == 0:
            arrive(wet_copies)
            for r in (0, rows):
                row_weight(r, 0)
        arrive(coming_rows)
        arrive(coming_cols)
        ends(src, dst, deep, factor)
        if k == 0:
            own = packed[0, flows]
            for n, (w, first) in enumerate((
                    (jnp.where(own_right, from_l[0, FIELDS], own), DEEP - 1),
                    (jnp.where(own_right, own, from_r[0, FIELDS]), DEEP - 2))):
                used = jnp.logical_or(pos == first, pos == first + 1)
                wet_edge[n] = jnp.where(used, (-time_step * root) * w * lane_next(w), 0.0)
        edges(k, factor)
        for lo, hi in ((0, H), (rows - H, rows)):
            carry = lax.fori_loop(lo, hi, pack_row, carry, unroll=True)
        ahead = [carry[n] + change[n] for n in range(count)]
        for n in range(count):
            packed[k + 1, n] = ahead[n] * root if last and n // 2 in (1, 2) else ahead[n]
        if not last:
            squeeze(k + 1, ahead)
        for lo, hi in ((0, deep), (rows - deep, rows)):
            lax.fori_loop(lo, hi, mend_row, 0, unroll=True)
        coming_cols = column_copies(k + 1, count if last else FIELDS)
        begin(coming_cols)
        coming_rows = row_copies(k + 1, dst, deep, result_rows if last else stage_rows)
        begin(coming_rows)
        if k == 0:
            begin(wet_corners)
        lax.fori_loop(deep, rows - deep, mend_row, 0, unroll=4)
    block = R * SEG
    quarter = lane // block

    def moved(x, start, end):
        shift = (end - start) * block % cols
        return pltpu.roll(x, shift, 1) if shift else x

    for i, start in enumerate((0, 3)):
        for g in range(2):
            total = blank
            for t in range(4):
                total = jnp.where(quarter == t, moved(packed[3, 4 * g + t], start, t), total)
            corner_out[i, g] = total

    def corner_of(i, j, n):
        end = 0 if i else 3
        return jnp.where(quarter == end, moved(from_c[i, j, n // 4], n % 4, end), 1.0)

    coming_corners = corner_copies(lambda i: corner_out.at[i], from_c, send_cor, recv_cor)
    begin(coming_corners)

    layer_id = lax.broadcasted_iota(jnp.int32, (layers, cols), 0)
    top = layer_id == layers - 1
    lane_all = lax.broadcasted_iota(jnp.int32, (layers, cols), 1)
    at_start, at_end = lane_all == 0, lane_all == cols - 1
    at_edge = jnp.logical_or(at_start, at_end)

    def above(x):
        return pltpu.roll(x, layers - 1, 0)

    def below(x):
        return pltpu.roll(x, 1, 0)

    def upward_of(h, w, top):
        return jnp.where(w > 0.0, 2.0 / jnp.where(top, h, h + above(h)), 0.0)

    def high_of(r):
        return 0.5 * (res[0, r] + res[0, r + 1]) * (wet[r] * wet[r + 1])

    def prepare(r):
        h, w = res[0, r], jnp.broadcast_to(wet[r], (layers, cols))
        high = high_of(r)
        across = 0.5 * (h + lane_next(h)) * (w * lane_next(w))
        upward = upward_of(h, w, top)
        inner = jnp.where(top, 0.0, upward)
        diagonal = 0.5 * h + ce[r - 1] + high + lane_prev(across) + across + below(inner) + upward
        v = res[3, r]
        y = res[2, r]
        div = (
            0.5 * (res[1, r + 1] - res[1, r - 1])
            + 0.5 * (lane_next(y) - lane_prev(y))
            + (v - jnp.where(layer_id == 0, 0.0, below(v)))
        )
        ce[r] = high
        cn[r] = across
        up[r] = upward
        inv[r] = jnp.where(diagonal == 0.0, 0.0, 1.0 / diagonal)
        z0[r] = -div * w

    def prepare_loop(r, carry):
        prepare(r)
        return carry

    ce[R] = high_of(R)
    lax.fori_loop(R + 1, R + rows - 1, prepare_loop, 0, unroll=7)

    def wide_of(main, halo):
        return jnp.concatenate([main, halo], axis=1)

    def halo_pack(x):
        total = blank
        for n in range(R):
            total = into(x(R + rows + n), n, total)
            total = into(x(n), rows - R + n, total)
        return total

    lower_rows = seg < rows // 2

    def strips_of(l, own, r, halo, corner):
        far_l = jnp.where(lower_rows, corner(1, 0), corner(0, 0))
        far_r = jnp.where(lower_rows, corner(1, 1), corner(0, 1))
        return (
            wide_of(jnp.where(own_right, l, own), jnp.where(own_right, far_l, halo)),
            wide_of(jnp.where(own_right, own, r), jnp.where(own_right, halo, far_r)))

    arrive(wet_corners)
    wet_halo = halo_pack(lambda r: jnp.broadcast_to(wet[r], (half, cols)))
    for n, w in enumerate(strips_of(
            from_l[0, FIELDS], packed[0, flows], from_r[0, FIELDS], wet_halo, lambda i, j: wet_c[i, j])):
        wet_strip[n] = w

    arrive(coming_cols)
    arrive(coming_corners)
    arrive(coming_rows)

    fields = []
    for f in range(4):
        parts = []
        for q in range(2):
            n = 2 * f + q
            parts.append(strips_of(
                from_l[3, n], packed[3, n], from_r[3, n],
                halo_pack(lambda r: res[f, r, cuts[q], :]), lambda i, j: corner_of(i, j, n)))
        fields.append([jnp.concatenate([parts[0][n], parts[1][n]], axis=0) for n in range(2)])

    wide_layer = lax.broadcasted_iota(jnp.int32, (layers, width), 0)
    wide_top = wide_layer == layers - 1
    wide_pos = lax.broadcasted_iota(jnp.int32, (layers, width), 1) % SEG < DEEP

    def row_next(x):
        return pltpu.roll(x, width - SEG, 1)

    def row_prev(x):
        return pltpu.roll(x, SEG, 1)

    systems = []
    for n in range(2):
        h, x, y, v = [fields[f][n] for f in range(4)]
        w = jnp.concatenate([wet_strip[n], wet_strip[n]], axis=0)
        high = 0.5 * (h + row_next(h)) * (w * row_next(w))
        low = row_prev(high)
        across = 0.5 * (h + lane_next(h)) * (w * lane_next(w))
        back = lane_prev(across)
        upward = upward_of(h, w, wide_top)
        inner = jnp.where(wide_top, 0.0, upward)
        diagonal = 0.5 * h + low + high + back + across + below(inner) + upward
        inverse = jnp.where(diagonal == 0.0, 0.0, 1.0 / diagonal)
        div = (
            0.5 * (row_next(x) - row_prev(x))
            + 0.5 * (lane_next(y) - lane_prev(y))
            + (v - jnp.where(wide_layer == 0, 0.0, below(v)))
        )
        force = -div * w
        z = force * inverse
        levels = [z]
        for _ in range(2):
            z = inverse * (
                low * row_prev(z) + high * row_next(z) + across * lane_next(z) + back * lane_prev(z)
                + inner * above(z) + below(inner * z))
            levels.append(z)
        systems.append((across, inverse, force, levels))
    left, right = systems
    for n in range(3):
        patch[n] = jnp.where(wide_pos, right[n], left[n])
    for k in range(3):
        zl, zr = left[3][k], right[3][k]
        beyond[k] = jnp.where(wide_pos, left[0] * zl, zr)
        slopes[k] = jnp.where(wide_pos, left[0] * (lane_next(zl) - zl), zr)

    face_ends = jnp.zeros((layers, cols), f32)
    for across, _, _, levels in systems:
        z, c = levels[2][:, :cols], across[:, :cols]
        face_ends = face_ends + c * z * lane_next(z)
    face_ends = jnp.where(lane_all % SEG == DEEP - 1, face_ends, 0.0)

    def seen(strip, k, r, page):
        shift = {0: R, 1: R + rows, -1: R - rows}[page]
        lanes = slice(0, cols) if page == 0 else slice(cols, width)
        return out_of(strip[k, :, lanes], r - shift)

    def complete(r, page):
        cn[r] = jnp.where(at_edge, seen(patch, 0, r, page), cn[r])
        inverse = jnp.where(at_edge, seen(patch, 1, r, page), inv[r])
        force = jnp.where(at_edge, seen(patch, 2, r, page), z0[r])
        z = force * inverse
        inv[r] = inverse
        z0[r] = z
        return force * z

    def fold(x):
        return x[:half] + x[half:]

    first = R - ITERS
    ce[first - 1] = high_of(first - 1)
    for r in (*range(first, R + 1), *range(R + rows - 1, R + rows + ITERS)):
        prepare(r)
    for r in range(first, R):
        complete(r, -1)
        complete(r + ITERS + rows, 1)
    m0 = lax.fori_loop(R, R + rows, lambda r, acc: acc + fold(complete(r, 0)), blank, unroll=16)

    def next_in(x, edges_of):
        return lane_next(jnp.where(at_start, edges_of, x))

    def prev_in(x, edges_of):
        return lane_prev(jnp.where(at_end, edges_of, x))

    def spread(k, z, r, page):
        x = z[r]
        c = cn[r]
        u = jnp.where(top, 0.0, up[r])
        out = seen(beyond, k, r, page)
        return (
            ce[r - 1] * z[r - 1] + ce[r] * z[r + 1]
            + c * next_in(x, out) + prev_in(c * x, out)
            + u * above(x) + below(u * x)
        )

    def advance(k, z, target, reach):
        def inner(r, carry):
            odd, even = carry
            n = spread(k, z, r, 0)
            y = n * inv[r]
            target[r] = y
            return odd + fold(z[r] * n), even + fold(y * n)

        for r in range(reach):
            target[R - 1 - r] = spread(k, z, R - 1 - r, -1) * inv[R - 1 - r]
            target[R + rows + r] = spread(k, z, R + rows + r, 1) * inv[R + rows + r]
        return lax.fori_loop(R, R + rows, inner, (blank, blank), unroll=16)

    m1, m2 = advance(0, z0, z1, 2)
    m3, m4 = advance(1, z1, z2, 1)
    def faces(r, acc):
        x = z2[r]
        u = jnp.where(top, 0.0, up[r])
        t = ce[r] * z2[r + 1] + jnp.where(at_end, 0.0, cn[r]) * lane_next(x) + u * above(x)
        return acc + fold(x * t)

    m5 = lax.fori_loop(R, R + rows, faces, blank, unroll=16)
    beyond_low = ce[R - 1] * z2[R - 1] * z2[R]
    beyond_high = ce[R + rows - 1] * z2[R + rows - 1] * z2[R + rows]
    m5 = 2.0 * m5 + fold(beyond_low - beyond_high + face_ends)

    row_id = lax.broadcasted_iota(jnp.int32, (8, cols), 0)
    lane_id = lax.broadcasted_iota(jnp.int32, (8, cols), 1)
    diagonal_at = row_id == lane_id
    table = blank
    for k, x in enumerate((m0, m1, m2, m3, m4, m5)):
        table = jnp.where(row_id == k, jnp.sum(x, axis=0, keepdims=True), table)
    table = jnp.where(diagonal_at, jnp.sum(table, axis=1, keepdims=True), 0.0)
    own = len(peers)
    gather[own : own + 1, :] = jnp.sum(table, axis=0, keepdims=True)
    for n, (a, b) in enumerate(reversed(peers)):
        pltpu.make_async_remote_copy(
            src_ref=gather.at[pl.ds(own, 1)], dst_ref=gather.at[pl.ds(n, 1)], send_sem=send_sum, recv_sem=recv_sum,
            device_id=peer(a, b), device_id_type=MESH).start()

    def push_of(k, z):
        def row(r, carry):
            q, c = z[r], cn[r]
            east = 0.5 * (ce[r] * (z[r + 1] - q) + ce[r - 1] * (q - z[r - 1]))
            out = seen(slopes, k, r, 0)
            slope = c * (next_in(q, out) - q)
            north = 0.5 * (slope + prev_in(slope, out))
            upward = up[r] * (jnp.where(top, 0.0, above(q)) - q)
            for n, push in enumerate((east, north, upward)):
                pushes[k, n, r - R] = push
            return carry

        lax.fori_loop(R, R + rows, row, 0, unroll=4)

    def plain_out(r, carry):
        at = pl.ds(r - R, layers, stride=rows)
        depth_out[at, :] = jnp.where(jnp.broadcast_to(wet[r, :, :cols], (layers, cols)) > 0.0, res[0, r, :, :cols], staged[0, at, :])
        tracer_out[at, :] = res[4, r, :, :cols]
        return carry

    push_of(0, z0)
    push_of(1, z1)
    push_of(2, z2)
    lax.fori_loop(R, R + rows, plain_out, 0, unroll=4)
    all_sums = pltpu.make_async_remote_copy(
        src_ref=gather.at[pl.ds(0, own)], dst_ref=gather.at[pl.ds(0, own)], send_sem=send_sum, recv_sem=recv_sum,
        device_id=peer(1, 0), device_id_type=MESH)
    all_sums.wait_recv()
    table = jnp.sum(gather[...], axis=0, keepdims=True)
    table = jnp.where(diagonal_at, table, 0.0)
    sums = jnp.broadcast_to(jnp.sum(table, axis=1, keepdims=True), (8, cols))
    m = [sums[k : k + 1, :] for k in range(6)]

    def dots(a, b, table):
        out = None
        for i in range(3):
            for j in range(3):
                if a[i] is not None and b[j] is not None:
                    t = a[i] * b[j] * table[i + j]
                    out = t if out is None else out + t
        return out

    shifted = [m[k] - m[k + 1] for k in range(5)]

    def plus(a, b, f):
        out = []
        for x, y in zip(a, b):
            out.append(x if y is None else (f * y if x is None else x + f * y))
        return out

    def image(d):
        moved = [None, d[0], d[1]]
        return [x if y is None else (None if x is None and y is None else (-y if x is None else x - y)) for x, y in zip(d, moved)]

    one = jnp.ones_like(m[0])
    direction = [one, None, None]
    residual = [one, None, None]
    pressure = [None, None, None]
    energy = m[0]
    for sweep in range(ITERS):
        bottom = dots(direction, direction, shifted)
        size = energy / bottom
        pressure = plus(pressure, direction, size)
        if sweep + 1 < ITERS:
            residual = plus(residual, image(direction), -size)
            fresh = dots(residual, residual, m)
            direction = plus(residual, direction, fresh / energy)
            energy = fresh

    def correct(r, carry):
        at = pl.ds(r - R, layers, stride=rows)
        for n in range(3):
            push = pressure[0] * pushes[0, n, r - R]
            push = push + pressure[1] * pushes[1, n, r - R] + pressure[2] * pushes[2, n, r - R]
            mom_out[n, at, :] = res[1 + n, r, :, :cols] - push
        return carry

    lax.fori_loop(R, R + rows, correct, 0, unroll=4)
    all_sums.wait_send()
    for cond, go, come in started:
        @pl.when(cond)
        def _(go=go):
            go.wait_send()


def body(nx, ny, depth, momentum, tracer, cell_wet, tile_wet):
    layers, rows, cols = depth.shape
    assert TILE % rows == 0 and TILE % cols == 0 and cols == 128 and rows * SEG == cols and layers == 16 and 4 * DEEP == rows
    f32 = jnp.float32
    tall = rows + 2 * DEEP
    wide = 2 * cols
    half = layers // 2
    dma = pltpu.SemaphoreType.DMA
    vmem = pl.BlockSpec(memory_space=pltpu.VMEM)
    flat = jax.ShapeDtypeStruct((layers * rows, cols), f32)
    field = pltpu.VMEM((FIELDS, rows + 2 * REACH, layers, cols), f32)
    layer = pltpu.VMEM((tall, layers, cols), f32)
    three = pltpu.VMEM((3, layers, wide), f32)
    flows = 2 * FIELDS
    strip = pltpu.VMEM((4, flows + 1, half, cols), f32)
    pairs = [dma((4, 2))] * 2 + [dma((2,))] * 2 + [dma((4, 2))] * 2 + [dma((2, 2))] * 4
    pairs += [dma] * 2
    new_depth, new_momentum, new_tracer = pl.pallas_call(
        functools.partial(kernel, nx, ny, rows, cols, layers),
        out_shape=(pltpu.VMEM((layers * rows, cols), f32), pltpu.VMEM((3, layers * rows, cols), f32), pltpu.VMEM((layers * rows, cols), f32)),
        in_specs=[pl.BlockSpec(memory_space=pltpu.HBM)] * 5,
        out_specs=(vmem, vmem, vmem),
        scratch_shapes=[
            pltpu.VMEM((5, layers * rows, cols), f32),
            pltpu.VMEM((rows, cols), jnp.int32),
            pltpu.SMEM(tile_wet.shape, jnp.int32),
            dma((5,)),
            pltpu.VMEM((3, 3, rows, layers, cols), f32),
            field, field, field,
            pltpu.VMEM((FIELDS, tall, layers, cols), f32),
            pltpu.VMEM((tall, 1, cols), f32),
            pltpu.VMEM((rows + 1, half, cols), f32),
            pltpu.VMEM((rows, half, cols), f32),
            pltpu.VMEM((2, half, cols), f32),
            strip,
            pltpu.VMEM((3, FIELDS + 1, half, cols), f32),
            pltpu.VMEM((2, 2, half, cols), f32),
            strip, strip,
            pltpu.VMEM((2, 2, 2, half, cols), f32),
            pltpu.VMEM((2, 2, half, cols), f32),
            pltpu.VMEM((flows, half, cols), f32),
            layer, layer, layer, layer, layer, layer, layer,
            pltpu.VMEM((2, half, wide), f32),
            three, three, three,
            pltpu.VMEM((nx * ny, cols), f32),
            *pairs,
        ],
        compiler_params=pltpu.CompilerParams(
            collective_id=0, has_side_effects=True, vmem_limit_bytes=56 * 1024 * 1024
        ),
    )(
        tile_wet,
        depth.reshape(layers * rows, cols),
        momentum.reshape(3, layers * rows, cols),
        tracer.reshape(layers * rows, cols),
        cell_wet,
    )
    new_depth, new_momentum, new_tracer = pl.pallas_call(
        hand_on,
        out_shape=(flat, jax.ShapeDtypeStruct((3, layers * rows, cols), f32), flat),
        in_specs=[pl.BlockSpec(memory_space=pl.ANY)] * 3,
        out_specs=(pl.BlockSpec(memory_space=pl.ANY),) * 3,
        scratch_shapes=[dma((3,))],
        compiler_params=pltpu.CompilerParams(vmem_limit_bytes=8 * 1024 * 1024),
    )(new_depth, new_momentum, new_tracer)
    return (
        new_depth.reshape(depth.shape),
        new_momentum.reshape(momentum.shape),
        new_tracer.reshape(tracer.shape),
    )


def hand_on(a, b, c, x, y, z, sem):
    moves = [pltpu.make_async_copy(s, d, sem.at[k]) for k, (s, d) in enumerate(((a, x), (b, y), (c, z)))]
    for m in moves:
        m.start()
    for m in moves:
        m.wait()


def solution(mesh):
    placed = (
        P(None, "gx", "gy"),
        P(None, None, "gx", "gy"),
        P(None, "gx", "gy"),
        P("gx", "gy"),
        P(),
    )
    return jax.shard_map(
        functools.partial(body, mesh.shape["gx"], mesh.shape["gy"]),
        mesh=mesh,
        in_specs=placed,
        out_specs=(P(None, "gx", "gy"), P(None, None, "gx", "gy"), P(None, "gx", "gy")),
        check_vma=False,
    )
```
